128 devices in a mesh: row: 16 (over z, y), col: 8 (over x, core).
Axes of the slice: x: 4, y: 4, z: 4, core: 2. Of those that a mesh axis runs over, the one named last changes fastest.
Arguments:
- covariance: float32 [4, 16, 256, 8, 8, 256], P(None, 'row', None, None, 'col'), as said below
- check_weights: float32 [4, 16, 256], P(None, 'row'), may hold values from 0.05 to 0.5
Outputs:
- trailing: float32 [4, 16, 256, 8, 8, 256], P(None, 'row', None, None, 'col')
- panels: float32 [4, 16, 256, 512], P(None, 'row')
- checksum: float32 [8, 8, 256], P(None, 'col')
The draws below stay inside these ranges and needn't reach their ends.
Inputs may be any that keep to these rules, and one draw needn't show every extreme that they name: covariance is symmetric with smallest eigenvalue at least 0.5: an exponential kernel of jittered grid sites plus a nugget plus a small symmetric rough part.
All inputs are finite; a program needn't handle non-finite values.
Results may differ from the reference program's by a relative error of at most 0.0003.
Values sent between devices are 32-bit elements; how exact they have to be, the bound alone decides.
No kernel may reach another device: no remote copies, remote signals or barrier semaphores. Data moves between devices by JAX's collectives and lax.ppermute only.
A program may use at most 128 MiB of HBM per device.

```python
import math
import jax
import jax.numpy as jnp
from jax import lax

NB = 256
TR_DEV = 4
TC_DEV = 8
ORDER = 16384
N_ROW = 16
N_COL = 8


def draw_covariance(key, part):
    count = ORDER
    across = NB // 4
    first, second, third = jax.random.split(key, 3)
    index = jnp.arange(count)
    xsite = (index % across).astype(jnp.float32) + jax.random.uniform(first, (count,), dtype=jnp.float32)
    ysite = (index // across).astype(jnp.float32) + jax.random.uniform(second, (count,), dtype=jnp.float32)
    reach = 6.0
    rough = jax.random.normal(third, (count, count), dtype=jnp.float32)
    rough = (rough + rough.T) * (0.7071068 / math.sqrt(count))
    xdiff = xsite[:, None] - xsite[None, :]
    ydiff = ysite[:, None] - ysite[None, :]
    distance = jnp.sqrt(xdiff * xdiff + ydiff * ydiff)
    kernel = jnp.exp(-distance / reach)
    full = kernel + rough + 3.0 * jnp.eye(count, dtype=jnp.float32)
    return full.reshape(TR_DEV, N_ROW, NB, TC_DEV, N_COL, NB)


def block_scale(own_key, extent, cuts, least, top_value):
    factor_of = 1.0
    for axis_at, blocks in cuts:
        heights = jax.random.uniform(jax.random.fold_in(jax.random.fold_in(own_key, 6), axis_at), (blocks,), jnp.float32, least / len(cuts), top_value / len(cuts))
        factor_of = factor_of * jnp.repeat(jnp.exp(heights), extent[axis_at] // blocks).reshape((-1,) + (1,) * (len(extent) - 1 - axis_at))
    return factor_of


def setup_inputs(seed: int = 0) -> dict:
    streams_of = jax.random.split(jax.random.key(seed), 3)
    return {
        "covariance": draw_covariance(jax.random.fold_in(streams_of[2], 71), 0),
        "check_weights": jnp.clip(jnp.exp(math.log(0.5) - 2.3025851 * jax.random.uniform(streams_of[1], (TR_DEV, N_ROW, NB), jnp.float32) ** block_scale(streams_of[1], (TR_DEV, N_ROW, NB), ((1, 16),), -0.2, 0.2)), 0.05, 0.5),
    }


HIGHEST = lax.Precision.HIGHEST

def reference(covariance, check_weights):
    order = TR_DEV * N_ROW * NB
    matrix = covariance.reshape(order, order)
    weights = check_weights.reshape(order)
    tiles = jnp.arange(order, dtype=jnp.int32) // NB
    panel_list = []
    for step in range(2):
        start = step * NB
        factor = jnp.linalg.cholesky(matrix[start:start + NB, start:start + NB])
        column = matrix[:, start:start + NB]
        solved = jax.scipy.linalg.solve_triangular(factor, column.T, lower=True).T
        solved = jnp.where((tiles >= step)[:, None], solved, 0.0)
        matrix = matrix - jnp.dot(solved, solved.T, precision=HIGHEST)
        panel_list.append(solved)
    keep = tiles >= 2
    trailing = jnp.where(keep[:, None] & keep[None, :], matrix, 0.0)
    checksum = jnp.dot(weights, trailing, precision=HIGHEST)
    panels = jnp.concatenate(panel_list, axis=1)
    return (trailing.reshape(TR_DEV, N_ROW, NB, TC_DEV, N_COL, NB), panels.reshape(TR_DEV, N_ROW, NB, 2 * NB), checksum.reshape(TC_DEV, N_COL, NB))
```

```python
import functools

import jax
import jax.numpy as jnp
from jax import lax
from jax.experimental import pallas as pl
from jax.experimental.pallas import tpu as pltpu
from jax.sharding import PartitionSpec as P

HIGHEST = lax.Precision.HIGHEST
F32 = jnp.float32
BF16 = jnp.bfloat16
NB = 256
NT = (((1,), (1,)), ((), ()))
NN = (((1,), (0,)), ((), ()))


def dot6(a, b, dims):
    return lax.dot_general(a, b, dims, precision=HIGHEST, preferred_element_type=F32)


def halves(value):
    high = value.astype(BF16)
    return high, (value - high.astype(F32)).astype(BF16)


def dot3(a, b, dims):
    total = lax.dot_general(a[0], b[0], dims, preferred_element_type=F32)
    total += lax.dot_general(a[0], b[1], dims, preferred_element_type=F32)
    return total + lax.dot_general(a[1], b[0], dims, preferred_element_type=F32)


def splat_row(ref, row, lanes):
    return jnp.broadcast_to(ref[row : row + 1, lanes], (8, 128))


def splat_lane(value, lane):
    return jnp.broadcast_to(value[:, lane : lane + 1], (8, 128))


def invert_factor(m, put):
    left, right = slice(0, 128), slice(128, 256)
    for block in range(16):
        base = 8 * block
        rows = [[splat_row(m, base + a, side) for a in range(8)] for side in (left, right)]
        b = {(a, k): splat_lane(rows[0][a], base + k) for a in range(8) for k in range(a + 1)}
        n = {}
        inverse, root = [], []
        for i in range(8):
            inverse.append(1.0 / b[i, i])
            root.append(lax.rsqrt(b[i, i]))
            for k in range(i + 1, 8):
                ratio = b[k, i] * inverse[i]
                for j in range(i + 1, k + 1):
                    b[k, j] = b[k, j] - ratio * b[j, i]
                for j in range(i):
                    n[k, j] = n[k, j] - ratio * n[i, j]
                n[k, i] = -ratio
        solved = []
        for side in range(2):
            upper = []
            for i in range(8):
                value = rows[side][i]
                for j in range(i):
                    value = value + n[i, j] * rows[side][j]
                upper.append(value)
            if side == 1:
                for i in range(8):
                    put(base + i, root[i] * upper[i])
            scaled = [inverse[i] * upper[i] for i in range(8)]
            out = []
            for i in range(8):
                value = scaled[i]
                for k in range(i + 1, 8):
                    value = value + n[k, i] * scaled[k]
                out.append(value)
            solved.append(out)
        for other in range(block + 1, 16):
            span = slice(8 * other, 8 * other + 8)
            a_part, n_part = m[span, left], m[span, right]
            columns = [splat_lane(a_part, base + i) for i in range(8)]
            for i in range(8):
                a_part = a_part - columns[i] * solved[0][i]
                n_part = n_part - columns[i] * solved[1][i]
            m[span, left] = a_part
            m[span, right] = n_part


def factor_tile(source, out, m, part):
    eye = (lax.broadcasted_iota(jnp.int32, (128, 128), 0) == lax.broadcasted_iota(jnp.int32, (128, 128), 1)).astype(F32)
    m[:, 0:128] = source[0:128, 0:128]

    def body(i, carry):
        m[:, 128:256] = eye

        def put(row, value):
            part[i, row : row + 1, :] = value[0:1, :]

        invert_factor(m, put)

        @pl.when(i == 0)
        def _():
            low = dot6(source[128:256, 0:128], part[0], NT)
            m[:, 0:128] = source[128:256, 128:256] - dot6(low, low, NT)
            part[2] = low

        return carry

    lax.fori_loop(0, 2, body, 0)
    out[0:128, 0:128] = part[0]
    out[0:128, 128:256] = jnp.zeros((128, 128), F32)
    out[128:256, 128:256] = part[1]
    out[128:256, 0:128] = -dot6(part[1], dot6(part[2], part[0], NN), NN)


def first_kernel(c00, w00, m, part):
    factor_tile(c00, w00, m, part)


def second_kernel(w00, c10, c11, l10, w11, schur, m, part):
    low = dot6(c10[...], w00[...], NT)
    l10[...] = low
    schur[...] = c11[...] - dot6(low, low, NT)
    factor_tile(schur, w11, m, part)


TILE = jax.ShapeDtypeStruct((NB, NB), F32)
WORK = [pltpu.VMEM((128, 256), F32), pltpu.VMEM((3, 128, 128), F32)]
VMEM = pl.BlockSpec(memory_space=pltpu.VMEM)
SMEM = pl.BlockSpec(memory_space=pltpu.SMEM)


def first_factor(c00):
    return pl.pallas_call(
        first_kernel, out_shape=TILE, in_specs=[VMEM], out_specs=VMEM, scratch_shapes=WORK, name="first_factor",
        cost_estimate=pl.CostEstimate(flops=20_000_000_000, bytes_accessed=1_000_000, transcendentals=0),
    )(c00)


def second_factor(w00, c10, c11):
    return pl.pallas_call(
        second_kernel, out_shape=(TILE, TILE), in_specs=[VMEM] * 3, out_specs=(VMEM, VMEM),
        scratch_shapes=[pltpu.VMEM((NB, NB), F32)] + WORK, name="second_factor",
        cost_estimate=pl.CostEstimate(flops=20_000_000_000, bytes_accessed=1_000_000, transcendentals=0),
    )(w00, c10, c11)


def corner_kernel(a, corner, pieces):
    for q in range(16):
        value = a[:, q, :]
        pieces[q // 2, :, 128 * (q % 2) : 128 * (q % 2) + 128] = value
        if q < 2:
            corner[:, 128 * q : 128 * q + 128] = value


def corner_call(flat):
    return pl.pallas_call(
        corner_kernel, grid=(2,),
        out_shape=(TILE, jax.ShapeDtypeStruct((8, NB, NB), F32)),
        in_specs=[pl.BlockSpec((128, 16, 128), lambda i: (i, 0, 0))],
        out_specs=(pl.BlockSpec((128, NB), lambda i: (i, 0)), pl.BlockSpec((8, 128, NB), lambda i: (0, i, 0))),
        name="corner_tiles",
    )(flat)


def column_kernel(weights, a, column, sums):
    step = pl.program_id(0)
    for q in range(2):
        column[:, 128 * q : 128 * q + 128] = a[:, q, :]

    @pl.when(step == 0)
    def _():
        sums[...] = jnp.zeros_like(sums)

    def body(i, total):
        for j in range(8):
            row = 8 * i + j
            total = total + weights[step * 128 + row] * a[row]
        return total

    sums[...] += lax.fori_loop(0, 16, body, jnp.zeros((16, 128), F32))


def column_call(weights, flat):
    return pl.pallas_call(
        column_kernel, grid=(8,),
        out_shape=(jax.ShapeDtypeStruct((1024, NB), F32), jax.ShapeDtypeStruct((16, 128), F32)),
        in_specs=[SMEM, pl.BlockSpec((128, 16, 128), lambda i: (i, 0, 0))],
        out_specs=(pl.BlockSpec((128, NB), lambda i: (i, 0)), pl.BlockSpec((16, 128), lambda i: (0, 0))),
        name="first_column",
    )(weights, flat)


def update_kernel(place, flat, row_panel, across, w00, l10, w11, sums, out, panels, checksum, high, low, factors):
    step = pl.program_id(0)
    row_index, col_index = place[0], place[1]

    def solve(first, second, dims):
        kept = [(factors[0, k], factors[1, k]) for k in range(3)]
        if dims == NN:
            top = dot3(kept[0], halves(first), NN)
            return top, dot3(kept[2], halves(second - dot3(kept[1], halves(top), NN)), NN)
        left = dot3(halves(first), kept[0], NT)
        return left, dot3(halves(second - dot3(halves(left), kept[1], NT)), kept[2], NT)

    @pl.when(step == 0)
    def _():
        for k, ref in enumerate((w00, l10, w11)):
            factors[0, k], factors[1, k] = halves(ref[...])
        y0 = dot6(jnp.broadcast_to(sums[2:3, 0:256], (8, 256)), w00[...], NT)
        y1 = dot6(jnp.broadcast_to(sums[2:3, 256:512], (8, 256)) - dot6(y0, l10[...], NT), w11[...], NT)
        y = halves(jnp.concatenate([y0, y1], axis=1))
        for u in range(8):
            top, bottom = solve(across[2 * u], across[2 * u + 1], NN)
            high[u, 0:256], low[u, 0:256] = halves(top)
            high[u, 256:512], low[u, 256:512] = halves(bottom)
            taken = dot3(y, (high[u], low[u]), NN)[0:1]
            whole = sums[3 + u : 4 + u, 0:256]
            kept = jnp.where((u == 0) & (col_index < 2), 0.0, whole - taken)
            checksum[u : u + 1, :] = kept

    left, right = solve(row_panel[:, 0:256], row_panel[:, 256:512], NT)
    right = jnp.where((step < 2) & (row_index == 0), 0.0, right)
    panels[:, 0:256] = left
    panels[:, 256:512] = right
    mine = halves(jnp.concatenate([left, right], axis=1))
    top_rows = (step < 2) & (row_index < 2)
    for u in range(8):
        product = dot3(mine, (high[u], low[u]), NN)
        gone = top_rows | (col_index < 2) if u == 0 else top_rows
        for h in range(2):
            q = 2 * u + h
            value = flat[:, q, :] - product[:, 128 * h : 128 * h + 128]
            out[:, q, :] = jnp.where(gone, 0.0, value)


def update_call(place, flat, row_panel, across, w00, l10, w11, sums):
    full = lambda *shape: pl.BlockSpec(shape, lambda i: (0,) * len(shape))
    return pl.pallas_call(
        update_kernel, grid=(8,),
        out_shape=(
            jax.ShapeDtypeStruct((1024, 16, 128), F32),
            jax.ShapeDtypeStruct((1024, 512), F32),
            jax.ShapeDtypeStruct((8, 256), F32),
        ),
        in_specs=[
            SMEM,
            pl.BlockSpec((128, 16, 128), lambda i: (i, 0, 0)),
            pl.BlockSpec((128, 512), lambda i: (i, 0)),
            full(16, NB, NB), full(NB, NB), full(NB, NB), full(NB, NB), full(16, 512),
        ],
        out_specs=(
            pl.BlockSpec((128, 16, 128), lambda i: (i, 0, 0)),
            pl.BlockSpec((128, 512), lambda i: (i, 0)),
            full(8, 256),
        ),
        scratch_shapes=[pltpu.VMEM((8, 512, 256), BF16), pltpu.VMEM((8, 512, 256), BF16), pltpu.VMEM((2, 3, NB, NB), BF16)],
        name="trailing_update",
    )(place, flat, row_panel, across, w00, l10, w11, sums)


def where_is(device):
    row, col = divmod(device, 8)
    return [row // 4, row % 4, col // 2, col % 2]


def device_at(z, y, x, core):
    return ((z % 4) * 4 + y % 4) * 8 + (x % 4) * 2 + core


def moved(device, dim, by):
    at = where_is(device)
    at[dim] += by
    return device_at(*at)


def spread(value, sources, dims):
    holders = list(sources)
    for dim in dims:
        first = [(h, moved(h, dim, 1)) for h in holders]
        value = value + lax.ppermute(value, ("row", "col"), first)
        second = [(h, moved(h, dim, -1)) for h in holders] + [(moved(h, dim, 1), moved(h, dim, 2)) for h in holders]
        value = value + lax.ppermute(value, ("row", "col"), second)
        holders = [moved(h, dim, k) for h in holders for k in range(4)]
    return value


def shards(covariance, check_weights):
    row = lax.axis_index("row")
    col = lax.axis_index("col")
    core = col % 2
    flat = covariance.reshape(1024, 16, 128)
    tiles = jnp.arange(4, dtype=jnp.int32) * 16 + row
    weights = jnp.where((tiles >= 2)[:, None], check_weights.reshape(4, NB), 0.0).reshape(1024)

    corner, pieces = corner_call(flat)
    c00 = jnp.where((row == 0) & (col == 0), corner, 0.0)
    c00 = spread(c00, [device_at(0, 0, 0, 0)], (2, 1, 0))
    swap_cores = [(c, c ^ 1) for c in range(8)]
    c00 = c00 + lax.ppermute(c00, "col", [(c, c + 1) for c in (0, 2, 4, 6)])
    below = jnp.where((row == 1) & (col < 2), corner, 0.0)
    below = spread(below, [device_at(0, 1, 0, 0), device_at(0, 1, 0, 1)], (0, 2, 1))
    other = lax.ppermute(below, "col", swap_cores)
    c10 = jnp.where(core == 0, below, other)
    c11 = jnp.where(core == 0, other, below)

    piece = jnp.where(row < 2, pieces[0], 0.0)
    for j in range(1, 8):
        piece = piece + lax.ppermute(pieces[j], "row", [(0, 2 * j), (1, 2 * j + 1)])
    across = lax.all_gather(piece, "row", axis=0)

    column, sums = column_call(weights, flat)
    mine = jnp.where(col < 2, column, 0.0)
    mine = mine + lax.ppermute(mine, "col", [(0, 2), (1, 3)]) + lax.ppermute(mine, "col", [(0, 6), (1, 7)])
    upper = mine[0:512] + lax.ppermute(mine[0:512], "col", [(2, 4), (3, 5)])
    lower = mine[512:1024] + lax.ppermute(mine[512:1024], "col", [(6, 4), (7, 5)])
    mine = jnp.concatenate([upper, lower], axis=0)
    theirs = lax.ppermute(mine, "col", swap_cores)
    row_panel = jnp.concatenate([jnp.where(core == 0, mine, theirs), jnp.where(core == 0, theirs, mine)], axis=1)

    panel_sums = jnp.dot(weights[None], row_panel, precision=HIGHEST)
    total = jnp.concatenate([sums, panel_sums.reshape(4, 128), jnp.zeros((4, 128), F32)], axis=0)
    for d in (1, 3, 4, 12):
        total = total + lax.ppermute(total, "row", [(r, r ^ d) for r in range(16)])
    wide = jnp.zeros((16, 512), F32).at[2, :].set(total[16:20].reshape(512)).at[3:11, 0:256].set(total[0:16].reshape(8, 256))

    w00 = first_factor(c00)
    l10, w11 = second_factor(w00, c10, c11)
    place = jnp.stack([row, col]).astype(jnp.int32)
    trailing, panels, checksum = update_call(place, flat, row_panel, across, w00, l10, w11, wide)
    return (
        trailing.reshape(4, 1, NB, 8, 1, NB),
        panels.reshape(4, 1, NB, 512),
        checksum.reshape(8, 1, NB),
    )


def solution(mesh):
    in_specs = (P(None, "row", None, None, "col", None), P(None, "row", None))
    out_specs = (
        P(None, "row", None, None, "col", None),
        P(None, "row", None, None),
        P(None, "col", None),
    )
    return jax.shard_map(shards, mesh=mesh, in_specs=in_specs, out_specs=out_specs, check_vma=False)
```

```python
import functools

import jax
import jax.numpy as jnp
from jax import lax
from jax.experimental import pallas as pl
from jax.experimental.pallas import tpu as pltpu
from jax.sharding import PartitionSpec as P

HIGHEST = lax.Precision.HIGHEST
F32 = jnp.float32
BF16 = jnp.bfloat16
NB = 256
NT = (((1,), (1,)), ((), ()))
NN = (((1,), (0,)), ((), ()))


def dot6(a, b, dims):
    return lax.dot_general(a, b, dims, precision=HIGHEST, preferred_element_type=F32)


def halves(value):
    high = value.astype(BF16)
    return high, (value - high.astype(F32)).astype(BF16)


def dot3(a, b, dims):
    total = lax.dot_general(a[0], b[0], dims, preferred_element_type=F32)
    total += lax.dot_general(a[0], b[1], dims, preferred_element_type=F32)
    return total + lax.dot_general(a[1], b[0], dims, preferred_element_type=F32)


def splat_row(ref, row, lanes):
    return jnp.broadcast_to(ref[row : row + 1, lanes], (8, 128))


def splat_lane(value, lane):
    return jnp.broadcast_to(value[:, lane : lane + 1], (8, 128))


def invert_factor(m, put):
    left, right = slice(0, 128), slice(128, 256)
    for block in range(16):
        base = 8 * block
        rows = [[splat_row(m, base + a, side) for a in range(8)] for side in (left, right)]
        b = {(a, k): splat_lane(rows[0][a], base + k) for a in range(8) for k in range(a + 1)}
        n = {}
        inverse, root = [], []
        for i in range(8):
            inverse.append(1.0 / b[i, i])
            root.append(lax.rsqrt(b[i, i]))
            for k in range(i + 1, 8):
                ratio = b[k, i] * inverse[i]
                for j in range(i + 1, k + 1):
                    b[k, j] = b[k, j] - ratio * b[j, i]
                for j in range(i):
                    n[k, j] = n[k, j] - ratio * n[i, j]
                n[k, i] = -ratio
        solved = []
        for side in range(2):
            upper = []
            for i in range(8):
                value = rows[side][i]
                for j in range(i):
                    value = value + n[i, j] * rows[side][j]
                upper.append(value)
            if side == 1:
                for i in range(8):
                    put(base + i, root[i] * upper[i])
            scaled = [inverse[i] * upper[i] for i in range(8)]
            out = []
            for i in range(8):
                value = scaled[i]
                for k in range(i + 1, 8):
                    value = value + n[k, i] * scaled[k]
                out.append(value)
            solved.append(out)
        for other in range(block + 1, 16):
            span = slice(8 * other, 8 * other + 8)
            a_part, n_part = m[span, left], m[span, right]
            columns = [splat_lane(a_part, base + i) for i in range(8)]
            for i in range(8):
                a_part = a_part - columns[i] * solved[0][i]
                n_part = n_part - columns[i] * solved[1][i]
            m[span, left] = a_part
            m[span, right] = n_part


def factor_tile(source, out, m, part):
    eye = (lax.broadcasted_iota(jnp.int32, (128, 128), 0) == lax.broadcasted_iota(jnp.int32, (128, 128), 1)).astype(F32)
    m[:, 0:128] = source[0:128, 0:128]

    def body(i, carry):
        m[:, 128:256] = eye

        def put(row, value):
            part[i, row : row + 1, :] = value[0:1, :]

        invert_factor(m, put)

        @pl.when(i == 0)
        def _():
            low = dot6(source[128:256, 0:128], part[0], NT)
            m[:, 0:128] = source[128:256, 128:256] - dot6(low, low, NT)
            part[2] = low

        return carry

    lax.fori_loop(0, 2, body, 0)
    out[0:128, 0:128] = part[0]
    out[0:128, 128:256] = jnp.zeros((128, 128), F32)
    out[128:256, 128:256] = part[1]
    out[128:256, 0:128] = -dot6(part[1], dot6(part[2], part[0], NN), NN)


def first_kernel(c00, w00, m, part):
    factor_tile(c00, w00, m, part)


def second_kernel(w00, c10, c11, l10, w11, schur, m, part):
    low = dot6(c10[...], w00[...], NT)
    l10[...] = low
    schur[...] = c11[...] - dot6(low, low, NT)
    factor_tile(schur, w11, m, part)


TILE = jax.ShapeDtypeStruct((NB, NB), F32)
WORK = [pltpu.VMEM((128, 256), F32), pltpu.VMEM((3, 128, 128), F32)]
VMEM = pl.BlockSpec(memory_space=pltpu.VMEM)
SMEM = pl.BlockSpec(memory_space=pltpu.SMEM)


def first_factor(c00):
    return pl.pallas_call(
        first_kernel, out_shape=TILE, in_specs=[VMEM], out_specs=VMEM, scratch_shapes=WORK, name="first_factor",
        cost_estimate=pl.CostEstimate(flops=20_000_000_000, bytes_accessed=1_000_000, transcendentals=0),
    )(c00)


def second_factor(w00, c10, c11):
    return pl.pallas_call(
        second_kernel, out_shape=(TILE, TILE), in_specs=[VMEM] * 3, out_specs=(VMEM, VMEM),
        scratch_shapes=[pltpu.VMEM((NB, NB), F32)] + WORK, name="second_factor",
        cost_estimate=pl.CostEstimate(flops=20_000_000_000, bytes_accessed=1_000_000, transcendentals=0),
    )(w00, c10, c11)


def corner_kernel(a, *pieces):
    for q in range(16):
        pieces[q // 2][:, 128 * (q % 2) : 128 * (q % 2) + 128] = a[:, q, :]


def corner_call(flat):
    return pl.pallas_call(
        corner_kernel, grid=(2,), out_shape=(TILE,) * 8,
        in_specs=[pl.BlockSpec((128, 16, 128), lambda i: (i, 0, 0))],
        out_specs=(pl.BlockSpec((128, NB), lambda i: (i, 0)),) * 8,
        name="corner_tiles",
    )(flat)


def column_kernel(weights, a, column, sums):
    step = pl.program_id(0)

    @pl.when(step < 8)
    def _():
        for q in range(2):
            column[:, 128 * q : 128 * q + 128] = a[:, q, :]

    @pl.when(step == 0)
    def _():
        sums[...] = jnp.zeros_like(sums)

    @pl.when(step < 8)
    def _():
        def body(i, total):
            for j in range(8):
                row = 8 * i + j
                total = total + weights[step * 128 + row] * a[row]
            return total

        sums[...] += lax.fori_loop(0, 16, body, jnp.zeros((16, 128), F32))

    @pl.when(step == 8)
    def _():
        for q in range(2):
            column[0:8, 128 * q : 128 * q + 128] = jnp.broadcast_to(sums[q : q + 1, :], (8, 128))


def column_call(weights, flat):
    return pl.pallas_call(
        column_kernel, grid=(9,),
        out_shape=(jax.ShapeDtypeStruct((1032, NB), F32), jax.ShapeDtypeStruct((16, 128), F32)),
        in_specs=[SMEM, pl.BlockSpec((128, 16, 128), lambda i: (jnp.minimum(i, 7), 0, 0))],
        out_specs=(pl.BlockSpec((128, NB), lambda i: (i, 0)), pl.BlockSpec((16, 128), lambda i: (0, 0))),
        name="first_column",
    )(weights, flat)


def panel_kernel(place, mine, theirs, sums, w00, l10, w11, panels, high, low, taken, factors):
    step = pl.program_id(0)
    even = place[1] % 2 == 0

    @pl.when(step == 0)
    def _():
        for k, ref in enumerate((w00, l10, w11)):
            factors[0, k], factors[1, k] = halves(ref[...])
        v0 = jnp.broadcast_to(jnp.concatenate([sums[16:17], sums[17:18]], axis=1), (8, NB))
        v1 = jnp.broadcast_to(jnp.concatenate([sums[18:19], sums[19:20]], axis=1), (8, NB))
        y0 = dot6(v0, w00[...], NT)
        y1 = dot6(v1 - dot6(y0, l10[...], NT), w11[...], NT)
        z1 = dot6(y1, w11[...], NN)
        taken[:, 256:512] = z1
        taken[:, 0:256] = dot6(y0 - dot6(z1, l10[...], NN), w00[...], NN)

    f00, f10, f11 = [(factors[0, k], factors[1, k]) for k in range(3)]
    own, other = mine[...], theirs[...]
    first = jnp.where(even, own, other)
    second = jnp.where(even, other, own)
    left = dot3(halves(first), f00, NT)
    right = dot3(halves(second - dot3(halves(left), f10, NT)), f11, NT)
    panels[:, 0:256] = left
    panels[:, 256:512] = jnp.where((step * 512 < 256) & (place[0] == 0) & (lax.broadcasted_iota(jnp.int32, (512, 1), 0) < 256), 0.0, right)
    last = dot3(halves(right), f11, NN)
    last_halves = halves(last)
    high[:, 256:512], low[:, 256:512] = last_halves
    high[:, 0:256], low[:, 0:256] = halves(dot3(halves(left - dot3(last_halves, f10, NN)), f00, NN))


def panel_call(place, mine, theirs, sums, w00, l10, w11):
    full = lambda *shape: pl.BlockSpec(shape, lambda i: (0,) * len(shape))
    part = lambda n: pl.BlockSpec((512, n), lambda i: (i, 0))
    return pl.pallas_call(
        panel_kernel, grid=(2,),
        out_shape=(
            jax.ShapeDtypeStruct((1024, 512), F32),
            jax.ShapeDtypeStruct((1024, 512), BF16),
            jax.ShapeDtypeStruct((1024, 512), BF16),
            jax.ShapeDtypeStruct((8, 512), F32),
        ),
        in_specs=[SMEM, part(NB), part(NB), full(24, 128), full(NB, NB), full(NB, NB), full(NB, NB)],
        out_specs=(part(512), part(512), part(512), full(8, 512)),
        scratch_shapes=[pltpu.VMEM((2, 3, NB, NB), BF16)],
        name="panel_solve",
        cost_estimate=pl.CostEstimate(flops=8_000_000_000, bytes_accessed=8_000_000, transcendentals=0),
    )(place, mine, theirs, sums, w00, l10, w11)


def update_kernel(place, flat, across, high, low, sums, taken, out, checksum, right_high, right_low):
    group, step = pl.program_id(0), pl.program_id(1)
    row_index, col_index = place[0], place[1]

    @pl.when(step == 0)
    def _():
        y = halves(taken[...])
        for u in range(4):
            for h in range(2):
                span = slice(NB * h, NB * h + NB)
                right_high[u, span], right_low[u, span] = halves(across[2 * u + h])
            part = dot3(y, (right_high[u], right_low[u]), NN)[0:1]
            for h in range(2):
                q = 2 * u + h
                kept = sums[pl.ds(8 * group + q, 1), :] - part[:, 128 * h : 128 * h + 128]
                if u == 0:
                    kept = jnp.where((group == 0) & (col_index < 2), 0.0, kept)
                checksum[pl.ds(8 * group + q, 1), :] = kept

    rows = flat.shape[0]
    top = (step * rows + lax.broadcasted_iota(jnp.int32, (rows, 1), 0) < NB) & (row_index < 2)
    for u in range(4):
        product = dot3((high[...], low[...]), (right_high[u], right_low[u]), NN)
        gone = top | ((group == 0) & (col_index < 2)) if u == 0 else top
        for h in range(2):
            q = 2 * u + h
            value = flat[:, q, :] - product[:, 128 * h : 128 * h + 128]
            out[:, q, :] = jnp.where(gone, 0.0, value)


def update_call(place, flat, across, high, low, sums, taken):
    rows = 256
    full = lambda *shape: pl.BlockSpec(shape, lambda g, i: (0,) * len(shape))
    return pl.pallas_call(
        update_kernel, grid=(2, 1024 // rows),
        out_shape=(jax.ShapeDtypeStruct((1024, 16, 128), F32), jax.ShapeDtypeStruct((16, 128), F32)),
        in_specs=[
            SMEM,
            pl.BlockSpec((rows, 8, 128), lambda g, i: (i, g, 0)),
            pl.BlockSpec((8, NB, NB), lambda g, i: (g, 0, 0)),
            pl.BlockSpec((rows, 512), lambda g, i: (i, 0)),
            pl.BlockSpec((rows, 512), lambda g, i: (i, 0)),
            full(24, 128),
            full(8, 512),
        ],
        out_specs=(pl.BlockSpec((rows, 8, 128), lambda g, i: (i, g, 0)), full(16, 128)),
        scratch_shapes=[pltpu.VMEM((4, 512, NB), BF16), pltpu.VMEM((4, 512, NB), BF16)],
        name="trailing_update",
    )(place, flat, across, high, low, sums, taken)


def where_is(device):
    row, col = divmod(device, 8)
    return [row // 4, row % 4, col // 2, col % 2]


def device_at(z, y, x, core):
    return ((z % 4) * 4 + y % 4) * 8 + (x % 4) * 2 + core


def moved(device, dim, by):
    at = where_is(device)
    at[dim] += by
    return device_at(*at)


def spread(value, sources, dims, start, here):
    holders = list(sources)
    stages = []
    for dim in dims:
        away = (here[dim] - start[dim]) % 4
        pairs = [(h, moved(h, dim, 1)) for h in holders]
        value = jnp.where(away == 1, lax.ppermute(value, ("row", "col"), pairs), value)
        stages.append(value)
        pairs = [(h, moved(h, dim, -1)) for h in holders] + [(moved(h, dim, 1), moved(h, dim, 2)) for h in holders]
        value = jnp.where(away >= 2, lax.ppermute(value, ("row", "col"), pairs), value)
        stages.append(value)
        holders = [moved(h, dim, k) for h in holders for k in range(4)]
    return stages


def after(value, token):
    return lax.optimization_barrier((value, token))[0]


def shards(covariance, check_weights):
    row = lax.axis_index("row")
    col = lax.axis_index("col")
    core = col % 2
    x = col // 2
    here = [row // 4, row % 4, x]
    flat = covariance.reshape(1024, 16, 128)
    tiles = jnp.arange(4, dtype=jnp.int32) * 16 + row
    weights = jnp.where((tiles >= 2)[:, None], check_weights.reshape(4, NB), 0.0).reshape(1024)
    place = jnp.stack([row, col]).astype(jnp.int32)
    swap_cores = [(c, c ^ 1) for c in range(8)]

    pieces = corner_call(flat)
    tree0 = spread(pieces[0], [device_at(0, 0, 0, 0)], (2, 1, 0), (0, 0, 0), here)
    c00 = jnp.where(core == 1, lax.ppermute(tree0[-1], "col", [(c, c + 1) for c in (0, 2, 4, 6)]), tree0[-1])
    tree1 = spread(pieces[0], [device_at(0, 1, 0, 0), device_at(0, 1, 0, 1)], (1, 0, 2), (0, 1, 0), here)
    below = tree1[-1]
    other = lax.ppermute(below, "col", swap_cores)
    c10 = jnp.where(core == 0, below, other)
    c11 = jnp.where(core == 0, other, below)

    piece = pieces[0]
    for j in range(1, 8):
        piece = jnp.where(row // 2 == j, lax.ppermute(pieces[j], "row", [(0, 2 * j), (1, 2 * j + 1)]), piece)
    across = lax.all_gather(piece, "row", axis=0)

    column, sums = column_call(weights, after(flat, tree0[0]))
    from_left = lax.ppermute(column, "col", [(0, 2), (1, 3)])
    from_right = lax.ppermute(column, "col", [(0, 6), (1, 7)])
    mine = jnp.where(x == 1, from_left, jnp.where(x == 3, from_right, column))
    upper = jnp.where(x == 2, lax.ppermute(mine[0:512], "col", [(2, 4), (3, 5)]), mine[0:512])
    lower = jnp.where(x == 2, lax.ppermute(mine[512:1032], "col", [(6, 4), (7, 5)]), mine[512:1032])
    mine = jnp.concatenate([upper, lower], axis=0)
    theirs = lax.ppermute(mine, "col", swap_cores)
    first_sums = jnp.where(core == 0, mine[1024:1025], theirs[1024:1025])
    second_sums = jnp.where(core == 0, theirs[1024:1025], mine[1024:1025])
    total = jnp.concatenate([sums, first_sums.reshape(2, 128), second_sums.reshape(2, 128), jnp.zeros((4, 128), F32)], axis=0)
    for d in (1, 3, 4, 12):
        total = total + lax.ppermute(total, "row", [(r, r ^ d) for r in range(16)])

    w00 = first_factor(c00)
    l10, w11 = second_factor(w00, c10, c11)
    panels, high, low, taken = panel_call(place, mine, theirs, total, w00, l10, w11)
    trailing, checksum = update_call(place, flat, across, high, low, total, taken)
    return (
        trailing.reshape(4, 1, NB, 8, 1, NB),
        panels.reshape(4, 1, NB, 512),
        checksum.reshape(8, 1, NB),
    )


def solution(mesh):
    in_specs = (P(None, "row", None, None, "col", None), P(None, "row", None))
    out_specs = (
        P(None, "row", None, None, "col", None),
        P(None, "row", None, None),
        P(None, "col", None),
    )
    return jax.shard_map(shards, mesh=mesh, in_specs=in_specs, out_specs=out_specs, check_vma=False)
```

```python
import functools

import jax
import jax.numpy as jnp
from jax import lax
from jax.experimental import pallas as pl
from jax.experimental.pallas import tpu as pltpu
from jax.sharding import PartitionSpec as P

HIGHEST = lax.Precision.HIGHEST
F32 = jnp.float32
BF16 = jnp.bfloat16
NB = 256
NT = (((1,), (1,)), ((), ()))
NN = (((1,), (0,)), ((), ()))


def dot6(a, b, dims):
    return lax.dot_general(a, b, dims, precision=HIGHEST, preferred_element_type=F32)


def halves(value):
    high = value.astype(BF16)
    return high, (value - high.astype(F32)).astype(BF16)


def dot3(a, b, dims):
    total = lax.dot_general(a[0], b[0], dims, preferred_element_type=F32)
    total += lax.dot_general(a[0], b[1], dims, preferred_element_type=F32)
    return total + lax.dot_general(a[1], b[0], dims, preferred_element_type=F32)


def splat_row(ref, row, lanes):
    return jnp.broadcast_to(ref[row : row + 1, lanes], (8, 128))


def splat_lane(value, lane):
    return jnp.broadcast_to(value[:, lane : lane + 1], (8, 128))


def invert_factor(m, put):
    left, right = slice(0, 128), slice(128, 256)
    for block in range(16):
        base = 8 * block
        rows = [[splat_row(m, base + a, side) for a in range(8)] for side in (left, right)]
        b = {(a, k): splat_lane(rows[0][a], base + k) for a in range(8) for k in range(a + 1)}
        n = {}
        inverse, root = [], []
        for i in range(8):
            inverse.append(1.0 / b[i, i])
            root.append(lax.rsqrt(b[i, i]))
            for k in range(i + 1, 8):
                ratio = b[k, i] * inverse[i]
                for j in range(i + 1, k + 1):
                    b[k, j] = b[k, j] - ratio * b[j, i]
                for j in range(i):
                    n[k, j] = n[k, j] - ratio * n[i, j]
                n[k, i] = -ratio
        solved = []
        for side in range(2):
            upper = []
            for i in range(8):
                value = rows[side][i]
                for j in range(i):
                    value = value + n[i, j] * rows[side][j]
                upper.append(value)
            if side == 1:
                for i in range(8):
                    put(base + i, root[i] * upper[i])
            scaled = [inverse[i] * upper[i] for i in range(8)]
            out = []
            for i in range(8):
                value = scaled[i]
                for k in range(i + 1, 8):
                    value = value + n[k, i] * scaled[k]
                out.append(value)
            solved.append(out)
        for other in range(block + 1, 16):
            span = slice(8 * other, 8 * other + 8)
            a_part, n_part = m[span, left], m[span, right]
            columns = [splat_lane(a_part, base + i) for i in range(8)]
            for i in range(8):
                a_part = a_part - columns[i] * solved[0][i]
                n_part = n_part - columns[i] * solved[1][i]
            m[span, left] = a_part
            m[span, right] = n_part


def factor_tile(source, out, m, part):
    eye = (lax.broadcasted_iota(jnp.int32, (128, 128), 0) == lax.broadcasted_iota(jnp.int32, (128, 128), 1)).astype(F32)
    m[:, 0:128] = source[0:128, 0:128]

    def body(i, carry):
        m[:, 128:256] = eye

        def put(row, value):
            part[i, row : row + 1, :] = value[0:1, :]

        invert_factor(m, put)

        @pl.when(i == 0)
        def _():
            low = dot6(source[128:256, 0:128], part[0], NT)
            m[:, 0:128] = source[128:256, 128:256] - dot6(low, low, NT)
            part[2] = low

        return carry

    lax.fori_loop(0, 2, body, 0)
    out[0:128, 0:128] = part[0]
    out[0:128, 128:256] = jnp.zeros((128, 128), F32)
    out[128:256, 128:256] = part[1]
    out[128:256, 0:128] = -dot6(part[1], dot6(part[2], part[0], NN), NN)


def first_kernel(c00, w00, m, part):
    factor_tile(c00, w00, m, part)


def second_kernel(w00, c10, c11, l10, w11, schur, m, part):
    low = dot6(c10[...], w00[...], NT)
    l10[...] = low
    schur[...] = c11[...] - dot6(low, low, NT)
    factor_tile(schur, w11, m, part)


TILE = jax.ShapeDtypeStruct((NB, NB), F32)
WORK = [pltpu.VMEM((128, 256), F32), pltpu.VMEM((3, 128, 128), F32)]
VMEM = pl.BlockSpec(memory_space=pltpu.VMEM)
SMEM = pl.BlockSpec(memory_space=pltpu.SMEM)


def first_factor(c00):
    return pl.pallas_call(
        first_kernel, out_shape=TILE, in_specs=[VMEM], out_specs=VMEM, scratch_shapes=WORK, name="first_factor",
        cost_estimate=pl.CostEstimate(flops=100_000_000, bytes_accessed=100_000, transcendentals=0),
    )(c00)


def second_factor(w00, c10, c11):
    return pl.pallas_call(
        second_kernel, out_shape=(TILE, TILE), in_specs=[VMEM] * 3, out_specs=(VMEM, VMEM),
        scratch_shapes=[pltpu.VMEM((NB, NB), F32)] + WORK, name="second_factor",
        cost_estimate=pl.CostEstimate(flops=100_000_000, bytes_accessed=100_000, transcendentals=0),
    )(w00, c10, c11)


def corner_kernel(a, *pieces):
    for q in range(16):
        value = a[:, q, :]
        for ref in pieces[q // 2 :: 8]:
            ref[:, 128 * (q % 2) : 128 * (q % 2) + 128] = value


def corner_call(flat):
    return pl.pallas_call(
        corner_kernel, grid=(2,), out_shape=(TILE,) * 9,
        in_specs=[pl.BlockSpec((128, 16, 128), lambda i: (i, 0, 0))],
        out_specs=(pl.BlockSpec((128, NB), lambda i: (i, 0)),) * 9,
        name="corner_tiles",
    )(flat)


def column_kernel(a, column, again):
    for q in range(2):
        value = a[:, q, :]
        column[:, 128 * q : 128 * q + 128] = value

        @pl.when(pl.program_id(0) == 0)
        def _():
            again[:, 128 * q : 128 * q + 128] = value[0:NB]


def column_call(flat):
    return pl.pallas_call(
        column_kernel, grid=(4,), out_shape=(jax.ShapeDtypeStruct((1024, NB), F32), TILE),
        in_specs=[pl.BlockSpec((256, 8, 128), lambda i: (i, 0, 0))],
        out_specs=(pl.BlockSpec((256, NB), lambda i: (i, 0)), pl.BlockSpec((NB, NB), lambda i: (0, 0))),
        name="first_column",
    )(flat)


def sums_kernel(weights, a, sums):
    step = pl.program_id(0)

    @pl.when(step == 0)
    def _():
        sums[...] = jnp.zeros_like(sums)

    def body(i, total):
        for j in range(8):
            row = 8 * i + j
            total = total + weights[step * 128 + row] * a[row]
        return total

    sums[...] += lax.fori_loop(0, 16, body, jnp.zeros((16, 128), F32))


def sums_call(weights, flat):
    return pl.pallas_call(
        sums_kernel, grid=(8,), out_shape=jax.ShapeDtypeStruct((16, 128), F32),
        in_specs=[SMEM, pl.BlockSpec((128, 16, 128), lambda i: (i, 0, 0))],
        out_specs=pl.BlockSpec((16, 128), lambda i: (0, 0)),
        name="column_sums",
        cost_estimate=pl.CostEstimate(flops=100_000_000, bytes_accessed=100_000, transcendentals=0),
    )(weights, flat)


def taken_kernel(sums, w00, l10, w11, taken):
    v0 = jnp.broadcast_to(jnp.concatenate([sums[16:17], sums[17:18]], axis=1), (8, NB))
    v1 = jnp.broadcast_to(jnp.concatenate([sums[18:19], sums[19:20]], axis=1), (8, NB))
    y0 = dot6(v0, w00[...], NT)
    y1 = dot6(v1 - dot6(y0, l10[...], NT), w11[...], NT)
    z1 = dot6(y1, w11[...], NN)
    taken[:, 256:512] = z1
    taken[:, 0:256] = dot6(y0 - dot6(z1, l10[...], NN), w00[...], NN)


def taken_call(sums, w00, l10, w11):
    return pl.pallas_call(
        taken_kernel, out_shape=jax.ShapeDtypeStruct((8, 512), F32), in_specs=[VMEM] * 4, out_specs=VMEM, name="taken_sums",
        cost_estimate=pl.CostEstimate(flops=100_000_000, bytes_accessed=100_000, transcendentals=0),
    )(sums, w00, l10, w11)


def panel_kernel(place, mine, theirs, w00, l10, w11, panels, high, low, factors):
    step = pl.program_id(0)
    even = place[1] % 2 == 0

    @pl.when(step == 0)
    def _():
        for k, ref in enumerate((w00, l10, w11)):
            factors[0, k], factors[1, k] = halves(ref[...])

    f00, f10, f11 = [(factors[0, k], factors[1, k]) for k in range(3)]
    own, other = mine[...], theirs[...]
    first = jnp.where(even, own, other)
    second = jnp.where(even, other, own)
    left = dot3(halves(first), f00, NT)
    right = dot3(halves(second - dot3(halves(left), f10, NT)), f11, NT)
    panels[:, 0:256] = left
    panels[:, 256:512] = jnp.where((step * 512 < 256) & (place[0] == 0) & (lax.broadcasted_iota(jnp.int32, (512, 1), 0) < 256), 0.0, right)
    last = dot3(halves(right), f11, NN)
    last_halves = halves(last)
    high[:, 256:512], low[:, 256:512] = last_halves
    high[:, 0:256], low[:, 0:256] = halves(dot3(halves(left - dot3(last_halves, f10, NN)), f00, NN))


def panel_call(place, mine, theirs, w00, l10, w11):
    full = lambda *shape: pl.BlockSpec(shape, lambda i: (0,) * len(shape))
    part = lambda n: pl.BlockSpec((512, n), lambda i: (i, 0))
    return pl.pallas_call(
        panel_kernel, grid=(2,),
        out_shape=(
            jax.ShapeDtypeStruct((1024, 512), F32),
            jax.ShapeDtypeStruct((1024, 512), BF16),
            jax.ShapeDtypeStruct((1024, 512), BF16),
        ),
        in_specs=[SMEM, part(NB), part(NB), full(NB, NB), full(NB, NB), full(NB, NB)],
        out_specs=(part(512), part(512), part(512)),
        scratch_shapes=[pltpu.VMEM((2, 3, NB, NB), BF16)],
        name="panel_solve",
        cost_estimate=pl.CostEstimate(flops=100_000_000, bytes_accessed=100_000, transcendentals=0),
    )(place, mine, theirs, w00, l10, w11)


def update_kernel(place, flat, across, high, low, sums, taken, out, checksum, right_high, right_low):
    group, step = pl.program_id(0), pl.program_id(1)
    row_index, col_index = place[0], place[1]

    @pl.when(step == 0)
    def _():
        y = halves(taken[...])
        for u in range(4):
            for h in range(2):
                span = slice(NB * h, NB * h + NB)
                right_high[u, span], right_low[u, span] = halves(across[2 * u + h])
            part = dot3(y, (right_high[u], right_low[u]), NN)[0:1]
            for h in range(2):
                q = 2 * u + h
                kept = sums[pl.ds(8 * group + q, 1), :] - part[:, 128 * h : 128 * h + 128]
                if u == 0:
                    kept = jnp.where((group == 0) & (col_index < 2), 0.0, kept)
                checksum[pl.ds(8 * group + q, 1), :] = kept

    rows = flat.shape[0]
    top = (step * rows + lax.broadcasted_iota(jnp.int32, (rows, 1), 0) < NB) & (row_index < 2)
    for u in range(4):
        product = dot3((high[...], low[...]), (right_high[u], right_low[u]), NN)
        gone = top | ((group == 0) & (col_index < 2)) if u == 0 else top
        for h in range(2):
            q = 2 * u + h
            value = flat[:, q, :] - product[:, 128 * h : 128 * h + 128]
            out[:, q, :] = jnp.where(gone, 0.0, value)


def update_call(place, flat, across, high, low, sums, taken):
    rows = 512
    full = lambda *shape: pl.BlockSpec(shape, lambda g, i: (0,) * len(shape))
    return pl.pallas_call(
        update_kernel, grid=(2, 1024 // rows),
        out_shape=(jax.ShapeDtypeStruct((1024, 16, 128), F32), jax.ShapeDtypeStruct((16, 128), F32)),
        in_specs=[
            SMEM,
            pl.BlockSpec((rows, 8, 128), lambda g, i: (i, g, 0)),
            pl.BlockSpec((8, NB, NB), lambda g, i: (g, 0, 0)),
            pl.BlockSpec((rows, 512), lambda g, i: (i, 0)),
            pl.BlockSpec((rows, 512), lambda g, i: (i, 0)),
            full(24, 128),
            full(8, 512),
        ],
        out_specs=(pl.BlockSpec((rows, 8, 128), lambda g, i: (i, g, 0)), full(16, 128)),
        scratch_shapes=[pltpu.VMEM((4, 512, NB), BF16), pltpu.VMEM((4, 512, NB), BF16)],
        name="trailing_update",
    )(place, flat, across, high, low, sums, taken)


def where_is(device):
    row, col = divmod(device, 8)
    return [row // 4, row % 4, col // 2, col % 2]


def device_at(z, y, x, core):
    return ((z % 4) * 4 + y % 4) * 8 + (x % 4) * 2 + core


def moved(device, dim, by):
    at = where_is(device)
    at[dim] += by
    return device_at(*at)


def spread(value, sources, dims, start, here):
    holders = list(sources)
    stages = []
    for dim in dims:
        away = (here[dim] - start[dim]) % 4
        pairs = [(h, moved(h, dim, 1)) for h in holders]
        value = jnp.where(away == 1, lax.ppermute(value, ("row", "col"), pairs), value)
        stages.append(value)
        pairs = [(h, moved(h, dim, -1)) for h in holders] + [(moved(h, dim, 1), moved(h, dim, 2)) for h in holders]
        value = jnp.where(away >= 2, lax.ppermute(value, ("row", "col"), pairs), value)
        stages.append(value)
        holders = [moved(h, dim, k) for h in holders for k in range(4)]
    return stages


def after(value, token):
    return lax.optimization_barrier((value, token))[0]


def shards(covariance, check_weights):
    row = lax.axis_index("row")
    col = lax.axis_index("col")
    core = col % 2
    x = col // 2
    here = [row // 4, row % 4, x]
    flat = covariance.reshape(1024, 16, 128)
    tiles = jnp.arange(4, dtype=jnp.int32) * 16 + row
    weights = jnp.where((tiles >= 2)[:, None], check_weights.reshape(4, NB), 0.0).reshape(1024)
    place = jnp.stack([row, col]).astype(jnp.int32)
    swap_cores = [(c, c ^ 1) for c in range(8)]

    pieces = corner_call(flat)
    column, corner = column_call(after(flat, pieces[7]))
    tree0 = spread(pieces[0], [device_at(0, 0, 0, 0)], (2, 1, 0), (0, 0, 0), here)
    c00 = jnp.where(core == 1, lax.ppermute(tree0[-1], "col", [(c, c + 1) for c in (0, 2, 4, 6)]), tree0[-1])
    tree1 = spread(pieces[8], [device_at(0, 1, 0, 0), device_at(0, 1, 0, 1)], (1, 0, 2), (0, 1, 0), here)
    below = tree1[-1]
    other = lax.ppermute(below, "col", swap_cores)
    c10 = jnp.where(core == 0, below, other)
    c11 = jnp.where(core == 0, other, below)

    piece = corner
    for j in range(1, 8):
        piece = jnp.where(row // 2 == j, lax.ppermute(pieces[j], "row", [(0, 2 * j), (1, 2 * j + 1)]), piece)
    sums = sums_call(weights, after(flat, (tree0[0], column)))
    across = lax.all_gather(after(piece, (tree0[2], tree1[0], sums)), "row", axis=0)

    w00 = first_factor(c00)
    l10, w11 = second_factor(w00, c10, c11)
    from_left = lax.ppermute(column, "col", [(0, 2), (1, 3)])
    from_right = lax.ppermute(column, "col", [(0, 6), (1, 7)])
    from_left, from_right = after((from_left, from_right), (tree0[4], tree1[3]))
    mine = jnp.where(x == 1, from_left, jnp.where(x == 3, from_right, column))
    upper = lax.ppermute(mine[0:512], "col", [(2, 4), (3, 5)])
    lower = lax.ppermute(mine[512:1024], "col", [(6, 4), (7, 5)])
    upper, lower = after((upper, lower), (w00, tree1[-1]))
    upper = jnp.where(x == 2, upper, mine[0:512])
    lower = jnp.where(x == 2, lower, mine[512:1024])
    mine = jnp.concatenate([upper, lower], axis=0)
    theirs = after(lax.ppermute(mine, "col", swap_cores), w11)
    own_sums = jnp.dot(weights[None], mine, precision=HIGHEST)
    other_sums = jnp.dot(weights[None], theirs, precision=HIGHEST)
    first_sums = jnp.where(core == 0, own_sums, other_sums)
    second_sums = jnp.where(core == 0, other_sums, own_sums)
    total = jnp.concatenate([sums, first_sums.reshape(2, 128), second_sums.reshape(2, 128), jnp.zeros((4, 128), F32)], axis=0)
    for d in (1, 3, 4, 12):
        total = total + lax.ppermute(total, "row", [(r, r ^ d) for r in range(16)])

    panels, high, low = panel_call(place, mine, theirs, w00, l10, w11)
    taken = taken_call(total, w00, l10, w11)
    trailing, checksum = update_call(place, flat, across, high, low, total, taken)
    return (
        trailing.reshape(4, 1, NB, 8, 1, NB),
        panels.reshape(4, 1, NB, 512),
        checksum.reshape(8, 1, NB),
    )


def solution(mesh):
    in_specs = (P(None, "row", None, None, "col", None), P(None, "row", None))
    out_specs = (
        P(None, "row", None, None, "col", None),
        P(None, "row", None, None),
        P(None, "col", None),
    )
    return jax.shard_map(shards, mesh=mesh, in_specs=in_specs, out_specs=out_specs, check_vma=False)
```

```python
import functools

import jax
import jax.numpy as jnp
from jax import lax
from jax.experimental import pallas as pl
from jax.experimental.pallas import tpu as pltpu
from jax.sharding import PartitionSpec as P

HIGHEST = lax.Precision.HIGHEST
F32 = jnp.float32
BF16 = jnp.bfloat16
NB = 256
NT = (((1,), (1,)), ((), ()))
NN = (((1,), (0,)), ((), ()))


def dot6(a, b, dims):
    return lax.dot_general(a, b, dims, precision=HIGHEST, preferred_element_type=F32)


def halves(value):
    high = value.astype(BF16)
    return high, (value - high.astype(F32)).astype(BF16)


def dot3(a, b, dims):
    total = lax.dot_general(a[0], b[0], dims, preferred_element_type=F32)
    total += lax.dot_general(a[0], b[1], dims, preferred_element_type=F32)
    return total + lax.dot_general(a[1], b[0], dims, preferred_element_type=F32)


def splat_row(ref, row, lanes):
    return jnp.broadcast_to(ref[row : row + 1, lanes], (8, 128))


def splat_lane(value, lane):
    return jnp.broadcast_to(value[:, lane : lane + 1], (8, 128))


def invert_factor(m, put):
    left, right = slice(0, 128), slice(128, 256)
    for block in range(16):
        base = 8 * block
        rows = [[splat_row(m, base + a, side) for a in range(8)] for side in (left, right)]
        b = {(a, k): splat_lane(rows[0][a], base + k) for a in range(8) for k in range(a + 1)}
        n = {}
        inverse, root = [], []
        for i in range(8):
            inverse.append(1.0 / b[i, i])
            root.append(lax.rsqrt(b[i, i]))
            for k in range(i + 1, 8):
                ratio = b[k, i] * inverse[i]
                for j in range(i + 1, k + 1):
                    b[k, j] = b[k, j] - ratio * b[j, i]
                for j in range(i):
                    n[k, j] = n[k, j] - ratio * n[i, j]
                n[k, i] = -ratio
        solved = []
        for side in range(2):
            upper = []
            for i in range(8):
                value = rows[side][i]
                for j in range(i):
                    value = value + n[i, j] * rows[side][j]
                upper.append(value)
            if side == 1:
                for i in range(8):
                    put(base + i, root[i] * upper[i])
            scaled = [inverse[i] * upper[i] for i in range(8)]
            out = []
            for i in range(8):
                value = scaled[i]
                for k in range(i + 1, 8):
                    value = value + n[k, i] * scaled[k]
                out.append(value)
            solved.append(out)
        for other in range(block + 1, 16):
            span = slice(8 * other, 8 * other + 8)
            a_part, n_part = m[span, left], m[span, right]
            columns = [splat_lane(a_part, base + i) for i in range(8)]
            for i in range(8):
                a_part = a_part - columns[i] * solved[0][i]
                n_part = n_part - columns[i] * solved[1][i]
            m[span, left] = a_part
            m[span, right] = n_part


def factor_tile(source, out, m, part):
    eye = (lax.broadcasted_iota(jnp.int32, (128, 128), 0) == lax.broadcasted_iota(jnp.int32, (128, 128), 1)).astype(F32)
    m[:, 0:128] = source[0:128, 0:128]

    def body(i, carry):
        m[:, 128:256] = eye

        def put(row, value):
            part[i, row : row + 1, :] = value[0:1, :]

        invert_factor(m, put)

        @pl.when(i == 0)
        def _():
            low = dot6(source[128:256, 0:128], part[0], NT)
            m[:, 0:128] = source[128:256, 128:256] - dot6(low, low, NT)
            part[2] = low

        return carry

    lax.fori_loop(0, 2, body, 0)
    out[0:128, 0:128] = part[0]
    out[0:128, 128:256] = jnp.zeros((128, 128), F32)
    out[128:256, 128:256] = part[1]
    out[128:256, 0:128] = -dot6(part[1], dot6(part[2], part[0], NN), NN)


def first_kernel(place, own, other, w00, tile, m, part):
    tile[...] = jnp.where(place[1] % 2 == 0, own[...], other[...])
    factor_tile(tile, w00, m, part)


def second_kernel(place, w00, own, other, l10, w11, schur, m, part):
    even = place[1] % 2 == 0
    low = dot6(jnp.where(even, own[0:NB], other[0:NB]), w00[...], NT)
    l10[...] = low
    schur[...] = jnp.where(even, other[0:NB], own[0:NB]) - dot6(low, low, NT)
    factor_tile(schur, w11, m, part)


TILE = jax.ShapeDtypeStruct((NB, NB), F32)
WORK = [pltpu.VMEM((128, 256), F32), pltpu.VMEM((3, 128, 128), F32)]
VMEM = pl.BlockSpec(memory_space=pltpu.VMEM)
SMEM = pl.BlockSpec(memory_space=pltpu.SMEM)


LIMIT = 24 * 1024 * 1024
SMALL = pl.CostEstimate(flops=100_000_000, bytes_accessed=100_000, transcendentals=0)
FACTOR = dict(compiler_params=pltpu.CompilerParams(vmem_limit_bytes=LIMIT), cost_estimate=SMALL)
TILE_WORK = [pltpu.VMEM((NB, NB), F32)] + WORK


def first_factor(place, own, other):
    return pl.pallas_call(
        first_kernel, out_shape=TILE, in_specs=[SMEM, VMEM, VMEM], out_specs=VMEM,
        scratch_shapes=TILE_WORK, name="first_factor", **FACTOR,
    )(place, own, other)


def second_factor(place, w00, own, other):
    return pl.pallas_call(
        second_kernel, out_shape=(TILE, TILE), in_specs=[SMEM, VMEM, VMEM, VMEM], out_specs=(VMEM, VMEM),
        scratch_shapes=TILE_WORK, name="second_factor", **FACTOR,
    )(place, w00, own, other)


def corner_kernel(a, *pieces):
    for q in range(16):
        value = a[:, q, :]
        for ref in pieces[q // 2 :: 8]:
            ref[:, 128 * (q % 2) : 128 * (q % 2) + 128] = value


def corner_call(flat):
    return pl.pallas_call(
        corner_kernel, grid=(2,), out_shape=(TILE,) * 9,
        in_specs=[pl.BlockSpec((128, 16, 128), lambda i: (i, 0, 0))],
        out_specs=(pl.BlockSpec((128, NB), lambda i: (i, 0)),) * 9,
        name="corner_tiles",
    )(flat)


def column_kernel(weights, a, column, again, sums):
    step = pl.program_id(0)
    for q in range(2):
        value = a[:, q, :]
        column[:, 128 * q : 128 * q + 128] = value

        @pl.when(step < 2)
        def _():
            again[:, 128 * q : 128 * q + 128] = value

    @pl.when(step == 0)
    def _():
        sums[...] = jnp.zeros_like(sums)

    def body(i, total):
        for j in range(8):
            row = 8 * i + j
            total = total + weights[step * 128 + row] * a[row]
        return total

    sums[...] += lax.fori_loop(0, 16, body, jnp.zeros((16, 128), F32))


def column_call(weights, flat):
    return pl.pallas_call(
        column_kernel, grid=(8,),
        out_shape=(jax.ShapeDtypeStruct((1024, NB), F32), TILE, jax.ShapeDtypeStruct((16, 128), F32)),
        in_specs=[SMEM, pl.BlockSpec((128, 16, 128), lambda i: (i, 0, 0))],
        out_specs=(
            pl.BlockSpec((128, NB), lambda i: (i, 0)),
            pl.BlockSpec((128, NB), lambda i: (jnp.minimum(i, 1), 0)),
            pl.BlockSpec((16, 128), lambda i: (0, 0)),
        ),
        name="first_column", **FACTOR,
    )(weights, flat)


def panel_kernel(place, mine, theirs, own_sums, other_sums, w00, l10, w11, panels, high, low, taken, factors):
    step = pl.program_id(0)
    even = place[1] % 2 == 0

    @pl.when(step == 0)
    def _():
        for k, ref in enumerate((w00, l10, w11)):
            factors[0, k], factors[1, k] = halves(ref[...])

    f00, f10, f11 = [(factors[0, k], factors[1, k]) for k in range(3)]
    own = jnp.concatenate([mine[...], own_sums[...]], axis=0)
    other = jnp.concatenate([theirs[...], other_sums[...]], axis=0)
    first = jnp.where(even, own, other)
    second = jnp.where(even, other, own)
    left = dot3(halves(first), f00, NT)
    right = dot3(halves(second - dot3(halves(left), f10, NT)), f11, NT)
    panels[:, 0:256] = left[0:512]
    top = (step == 0) & (place[0] == 0) & (lax.broadcasted_iota(jnp.int32, (512, 1), 0) < NB)
    panels[:, 256:512] = jnp.where(top, 0.0, right[0:512])
    last = dot3(halves(right), f11, NN)
    last_high, last_low = halves(last)
    rest = dot3(halves(left - dot3((last_high, last_low), f10, NN)), f00, NN)
    high[:, 256:512] = last_high[0:512]
    low[:, 256:512] = last_low[0:512]
    high[:, 0:256], low[:, 0:256] = halves(rest[0:512])
    taken[:, 0:256] = rest[512:520]
    taken[:, 256:512] = last[512:520]


def panel_call(place, mine, theirs, below, other, w00, l10, w11):
    full = lambda *shape: pl.BlockSpec(shape, lambda i: (0,) * len(shape))
    part = lambda n: pl.BlockSpec((512, n), lambda i: (i, 0))
    tail = pl.BlockSpec((8, NB), lambda i: (NB // 8, 0))
    return pl.pallas_call(
        panel_kernel, grid=(2,),
        out_shape=(
            jax.ShapeDtypeStruct((1024, 512), F32),
            jax.ShapeDtypeStruct((1024, 512), BF16),
            jax.ShapeDtypeStruct((1024, 512), BF16),
            jax.ShapeDtypeStruct((8, 512), F32),
        ),
        in_specs=[SMEM, part(NB), part(NB), tail, tail, full(NB, NB), full(NB, NB), full(NB, NB)],
        out_specs=(part(512), part(512), part(512), full(8, 512)),
        scratch_shapes=[pltpu.VMEM((2, 3, NB, NB), BF16)],
        name="panel_solve", **FACTOR,
    )(place, mine, theirs, below, other, w00, l10, w11)


def update_kernel(place, flat, across, high, low, sums, taken, out, checksum, right_high, right_low):
    group, step = pl.program_id(0), pl.program_id(1)
    row_index, col_index = place[0], place[1]

    @pl.when(step == 0)
    def _():
        y = halves(taken[...])
        for u in range(4):
            for h in range(2):
                span = slice(NB * h, NB * h + NB)
                right_high[u, span], right_low[u, span] = halves(across[2 * u + h])
            part = dot3(y, (right_high[u], right_low[u]), NN)[0:1]
            for h in range(2):
                q = 2 * u + h
                kept = sums[pl.ds(8 * group + q, 1), :] - part[:, 128 * h : 128 * h + 128]
                if u == 0:
                    kept = jnp.where((group == 0) & (col_index < 2), 0.0, kept)
                checksum[pl.ds(8 * group + q, 1), :] = kept

    rows = out.shape[0]
    base = pl.multiple_of(step * rows, rows)
    top = (step * rows + lax.broadcasted_iota(jnp.int32, (rows, 1), 0) < NB) & (row_index < 2)
    mine = high[pl.ds(base, rows), :], low[pl.ds(base, rows), :]
    for u in range(4):
        product = dot3(mine, (right_high[u], right_low[u]), NN)
        gone = top | ((group == 0) & (col_index < 2)) if u == 0 else top
        for h in range(2):
            q = 2 * u + h
            value = flat[:, q, :] - product[:, 128 * h : 128 * h + 128]
            out[:, q, :] = jnp.where(gone, 0.0, value)


def update_call(place, flat, across, high, low, sums, taken):
    rows = 256
    full = lambda *shape: pl.BlockSpec(shape, lambda g, i: (0,) * len(shape))
    return pl.pallas_call(
        update_kernel, grid=(2, 1024 // rows),
        out_shape=(jax.ShapeDtypeStruct((1024, 16, 128), F32), jax.ShapeDtypeStruct((16, 128), F32)),
        in_specs=[
            SMEM,
            pl.BlockSpec((rows, 8, 128), lambda g, i: (i, g, 0)),
            pl.BlockSpec((8, NB, NB), lambda g, i: (g, 0, 0)),
            full(1024, 512),
            full(1024, 512),
            full(16, 128),
            full(8, 512),
        ],
        out_specs=(pl.BlockSpec((rows, 8, 128), lambda g, i: (i, g, 0)), full(16, 128)),
        scratch_shapes=[pltpu.VMEM((4, 512, NB), BF16), pltpu.VMEM((4, 512, NB), BF16)],
        name="trailing_update", **FACTOR,
    )(place, flat, across, high, low, sums, taken)


def where_is(device):
    row, col = divmod(device, 8)
    return [row // 4, row % 4, col // 2, col % 2]


def device_at(z, y, x, core):
    return ((z % 4) * 4 + y % 4) * 8 + (x % 4) * 2 + core


def moved(device, dim, by):
    at = where_is(device)
    at[dim] += by
    return device_at(*at)


def spread(value, trees, here, gates=None, cargo=None):
    core = here[3]
    holders = [[device_at(z, y, 0, c)] for (z, y), c, _ in trees]
    stages = []
    for at in range(3):
        if at == 2 and cargo is not None:
            value = jnp.concatenate([value, cargo], axis=0)
        aways = []
        for (z, y), c, dims in trees:
            start = (z, y, 0)
            aways.append((c, (here[dims[at]] - start[dims[at]]) % 4))
        away = aways[0][1] if len(trees) == 1 else jnp.where(core == aways[0][0], aways[0][1], aways[1][1])
        for half in range(2):
            pairs = []
            for held, (_, _, dims) in zip(holders, trees):
                dim = dims[at]
                if half == 0:
                    pairs += [(h, moved(h, dim, 1)) for h in held]
                else:
                    pairs += [(h, moved(h, dim, -1)) for h in held] + [(moved(h, dim, 1), moved(h, dim, 2)) for h in held]
            sent = value if gates is None else after(value, gates[2 * at + half])
            arrived = lax.ppermute(sent, ("row", "col"), pairs)
            value = jnp.where((away == 1) if half == 0 else (away >= 2), arrived, sent)
            stages.append(value)
        holders = [[moved(h, dims[at], k) for h in held for k in range(4)] for held, (_, _, dims) in zip(holders, trees)]
    return stages


def after(value, token):
    return lax.optimization_barrier((value, token))[0]


def shards(covariance, check_weights):
    row = lax.axis_index("row")
    col = lax.axis_index("col")
    core = col % 2
    x = col // 2
    here = [row // 4, row % 4, x, core]
    flat = pltpu.with_memory_space_constraint(covariance.reshape(1024, 16, 128), pltpu.HBM)
    tiles = jnp.arange(4, dtype=jnp.int32) * 16 + row
    weights = jnp.where((tiles >= 2)[:, None], check_weights.reshape(4, NB), 0.0).reshape(1024)
    place = jnp.stack([row, col]).astype(jnp.int32)
    swap_cores = [(c, c ^ 1) for c in range(8)]

    pieces = corner_call(flat)
    tree0 = spread(pieces[0], [((0, 0), 0, (2, 1, 0))], here)
    c00_other = lax.ppermute(tree0[-1], "col", [(c, c + 1) for c in (0, 2, 4, 6)])
    column, corner, sums = column_call(weights, after(flat, tree0[1]))
    for d in (1, 3, 4, 12):
        sums = sums + lax.ppermute(sums, "row", [(r, r ^ d) for r in range(16)])
    panel_sums = jnp.broadcast_to(sums[0:2].reshape(1, NB), (8, NB))
    tree1 = spread(pieces[8], [((0, 1), 0, (0, 1, 2)), ((0, 1), 1, (1, 0, 2))], here, tree0, panel_sums)
    below = tree1[-1]
    below_other = lax.ppermute(below, "col", swap_cores)

    piece = corner
    for j in range(1, 8):
        piece = jnp.where(row // 2 == j, lax.ppermute(pieces[j], "row", [(0, 2 * j), (1, 2 * j + 1)]), piece)
    across = lax.all_gather(after(piece, tree0[1]), "row", axis=0)
    across = pltpu.with_memory_space_constraint(across, pltpu.HBM)

    w00 = first_factor(place, tree0[-1], c00_other)
    l10, w11 = second_factor(place, w00, below, below_other)
    from_left = lax.ppermute(column, "col", [(0, 2), (1, 3)])
    from_right = lax.ppermute(column, "col", [(0, 6), (1, 7)])
    from_left, from_right = after((from_left, from_right), (tree0[4], tree1[3]))
    mine = jnp.where(x == 1, from_left, jnp.where(x == 3, from_right, column))
    upper = lax.ppermute(mine[0:512], "col", [(2, 4), (3, 5)])
    lower = lax.ppermute(mine[512:1024], "col", [(6, 4), (7, 5)])
    upper, lower = after((upper, lower), (w00, tree1[-1]))
    upper = jnp.where(x == 2, upper, mine[0:512])
    lower = jnp.where(x == 2, lower, mine[512:1024])
    mine = jnp.concatenate([upper, lower], axis=0)
    theirs = after(lax.ppermute(mine, "col", swap_cores), w11)

    panels, high, low, taken = panel_call(place, mine, theirs, below, below_other, w00, l10, w11)
    trailing, checksum = update_call(place, flat, across, high, low, sums, taken)
    return (
        trailing.reshape(4, 1, NB, 8, 1, NB),
        panels.reshape(4, 1, NB, 512),
        checksum.reshape(8, 1, NB),
    )


def solution(mesh):
    in_specs = (P(None, "row", None, None, "col", None), P(None, "row", None))
    out_specs = (
        P(None, "row", None, None, "col", None),
        P(None, "row", None, None),
        P(None, "col", None),
    )
    return jax.shard_map(shards, mesh=mesh, in_specs=in_specs, out_specs=out_specs, check_vma=False)
```

```python
import functools

import jax
import jax.numpy as jnp
from jax import lax
from jax.experimental import pallas as pl
from jax.experimental.pallas import tpu as pltpu
from jax.sharding import PartitionSpec as P

HIGHEST = lax.Precision.HIGHEST
F32 = jnp.float32
BF16 = jnp.bfloat16
NB = 256
NT = (((1,), (1,)), ((), ()))
NN = (((1,), (0,)), ((), ()))


def dot6(a, b, dims):
    return lax.dot_general(a, b, dims, precision=HIGHEST, preferred_element_type=F32)


def halves(value):
    high = value.astype(BF16)
    return high, (value - high.astype(F32)).astype(BF16)


def dot3(a, b, dims):
    total = lax.dot_general(a[0], b[0], dims, preferred_element_type=F32)
    total += lax.dot_general(a[0], b[1], dims, preferred_element_type=F32)
    return total + lax.dot_general(a[1], b[0], dims, preferred_element_type=F32)


def splat_row(ref, row, lanes):
    return jnp.broadcast_to(ref[row : row + 1, lanes], (8, 128))


def splat_lane(value, lane):
    return jnp.broadcast_to(value[:, lane : lane + 1], (8, 128))


def invert_factor(m, put):
    left, right = slice(0, 128), slice(128, 256)
    for block in range(16):
        base = 8 * block
        rows = [[splat_row(m, base + a, side) for a in range(8)] for side in (left, right)]
        b = {(a, k): splat_lane(rows[0][a], base + k) for a in range(8) for k in range(a + 1)}
        n = {}
        inverse, root = [], []
        for i in range(8):
            inverse.append(1.0 / b[i, i])
            root.append(lax.rsqrt(b[i, i]))
            for k in range(i + 1, 8):
                ratio = b[k, i] * inverse[i]
                for j in range(i + 1, k + 1):
                    b[k, j] = b[k, j] - ratio * b[j, i]
                for j in range(i):
                    n[k, j] = n[k, j] - ratio * n[i, j]
                n[k, i] = -ratio
        solved = []
        for side in range(2):
            upper = []
            for i in range(8):
                value = rows[side][i]
                for j in range(i):
                    value = value + n[i, j] * rows[side][j]
                upper.append(value)
            if side == 1:
                for i in range(8):
                    put(base + i, root[i] * upper[i])
            scaled = [inverse[i] * upper[i] for i in range(8)]
            out = []
            for i in range(8):
                value = scaled[i]
                for k in range(i + 1, 8):
                    value = value + n[k, i] * scaled[k]
                out.append(value)
            solved.append(out)
        for other in range(block + 1, 16):
            span = slice(8 * other, 8 * other + 8)
            a_part, n_part = m[span, left], m[span, right]
            columns = [splat_lane(a_part, base + i) for i in range(8)]
            for i in range(8):
                a_part = a_part - columns[i] * solved[0][i]
                n_part = n_part - columns[i] * solved[1][i]
            m[span, left] = a_part
            m[span, right] = n_part


def factor_tile(source, out, m, part):
    eye = (lax.broadcasted_iota(jnp.int32, (128, 128), 0) == lax.broadcasted_iota(jnp.int32, (128, 128), 1)).astype(F32)
    m[:, 0:128] = source[0:128, 0:128]

    def body(i, carry):
        m[:, 128:256] = eye

        def put(row, value):
            part[i, row : row + 1, :] = value[0:1, :]

        invert_factor(m, put)

        @pl.when(i == 0)
        def _():
            low = dot6(source[128:256, 0:128], part[0], NT)
            m[:, 0:128] = source[128:256, 128:256] - dot6(low, low, NT)
            part[2] = low

        return carry

    lax.fori_loop(0, 2, body, 0)
    out[0:128, 0:128] = part[0]
    out[0:128, 128:256] = jnp.zeros((128, 128), F32)
    out[128:256, 128:256] = part[1]
    out[128:256, 0:128] = -dot6(part[1], dot6(part[2], part[0], NN), NN)


def first_kernel(place, own, other, w00, tile, m, part):
    tile[...] = jnp.where(place[1] % 2 == 0, own[0:NB], other[0:NB])
    factor_tile(tile, w00, m, part)


def second_kernel(place, w00, own, other, l10, w11, schur, m, part):
    even = place[1] % 2 == 0
    top, bottom = own[NB : NB + 128], other[NB : NB + 128]
    c10 = jnp.concatenate([jnp.where(even, top, bottom), jnp.where(even, bottom, top)], axis=0)
    low = dot6(c10, w00[...], NT)
    l10[...] = low
    schur[...] = jnp.where(even, other[0:NB], own[0:NB]) - dot6(low, low, NT)
    factor_tile(schur, w11, m, part)


TILE = jax.ShapeDtypeStruct((NB, NB), F32)
WORK = [pltpu.VMEM((128, 256), F32), pltpu.VMEM((3, 128, 128), F32)]
VMEM = pl.BlockSpec(memory_space=pltpu.VMEM)
SMEM = pl.BlockSpec(memory_space=pltpu.SMEM)


LIMIT = 24 * 1024 * 1024
SMALL = pl.CostEstimate(flops=100_000_000, bytes_accessed=100_000, transcendentals=0)
FACTOR = dict(compiler_params=pltpu.CompilerParams(vmem_limit_bytes=LIMIT), cost_estimate=SMALL)
TILE_WORK = [pltpu.VMEM((NB, NB), F32)] + WORK


def first_factor(place, own, other):
    return pl.pallas_call(
        first_kernel, out_shape=TILE, in_specs=[SMEM, VMEM, VMEM], out_specs=VMEM,
        scratch_shapes=TILE_WORK, name="first_factor", **FACTOR,
    )(place, own, other)


def second_factor(place, w00, own, other):
    return pl.pallas_call(
        second_kernel, out_shape=(TILE, TILE), in_specs=[SMEM, VMEM, VMEM, VMEM], out_specs=(VMEM, VMEM),
        scratch_shapes=TILE_WORK, name="second_factor", **FACTOR,
    )(place, w00, own, other)


def corner_kernel(a, *pieces):
    *pieces, flipped = pieces
    flipped[...] = a[:, 1, :].T
    for q in range(16):
        value = a[:, q, :]
        for ref in pieces[q // 2 :: 8]:
            ref[:, 128 * (q % 2) : 128 * (q % 2) + 128] = value


def corner_call(flat):
    return pl.pallas_call(
        corner_kernel, grid=(2,), out_shape=(TILE,) * 9 + (jax.ShapeDtypeStruct((128, NB), F32),),
        in_specs=[pl.BlockSpec((128, 16, 128), lambda i: (i, 0, 0))],
        out_specs=(pl.BlockSpec((128, NB), lambda i: (i, 0)),) * 9 + (pl.BlockSpec((128, 128), lambda i: (0, i)),),
        name="corner_tiles",
    )(flat)


def column_kernel(weights, a, column, sums):
    step = pl.program_id(0)
    for q in range(2):
        column[:, 128 * q : 128 * q + 128] = a[:, q, :]

    @pl.when(step == 0)
    def _():
        sums[...] = jnp.zeros_like(sums)

    def body(i, total):
        for j in range(8):
            row = 8 * i + j
            total = total + weights[step * 128 + row] * a[row]
        return total

    sums[...] += lax.fori_loop(0, 16, body, jnp.zeros((16, 128), F32))


def column_call(weights, flat):
    return pl.pallas_call(
        column_kernel, grid=(8,),
        out_shape=(jax.ShapeDtypeStruct((1024, NB), F32), jax.ShapeDtypeStruct((16, 128), F32)),
        in_specs=[SMEM, pl.BlockSpec((128, 16, 128), lambda i: (i, 0, 0))],
        out_specs=(
            pl.BlockSpec((128, NB), lambda i: (i, 0)),
            pl.BlockSpec((16, 128), lambda i: (0, 0)),
        ),
        name="first_column", **FACTOR,
    )(weights, flat)


def panel_kernel(place, mine, theirs, own_sums, other_sums, w00, l10, w11, panels, high, low, taken, factors):
    step = pl.program_id(0)
    even = place[1] % 2 == 0

    @pl.when(step == 0)
    def _():
        for k, ref in enumerate((w00, l10, w11)):
            factors[0, k], factors[1, k] = halves(ref[...])

    f00, f10, f11 = [(factors[0, k], factors[1, k]) for k in range(3)]
    own = jnp.concatenate([mine[...], own_sums[...]], axis=0)
    other = jnp.concatenate([theirs[...], other_sums[...]], axis=0)
    first = jnp.where(even, own, other)
    second = jnp.where(even, other, own)
    left = dot3(halves(first), f00, NT)
    right = dot3(halves(second - dot3(halves(left), f10, NT)), f11, NT)
    panels[:, 0:256] = left[0:512]
    top = (step == 0) & (place[0] == 0) & (lax.broadcasted_iota(jnp.int32, (512, 1), 0) < NB)
    panels[:, 256:512] = jnp.where(top, 0.0, right[0:512])
    last = dot3(halves(right), f11, NN)
    last_high, last_low = halves(last)
    rest = dot3(halves(left - dot3((last_high, last_low), f10, NN)), f00, NN)
    high[:, 256:512] = last_high[0:512]
    low[:, 256:512] = last_low[0:512]
    high[:, 0:256], low[:, 0:256] = halves(rest[0:512])
    taken[:, 0:256] = rest[512:528]
    taken[:, 256:512] = last[512:528]


def panel_call(place, mine, theirs, w00, l10, w11):
    full = lambda *shape: pl.BlockSpec(shape, lambda i: (0,) * len(shape))
    part = lambda n: pl.BlockSpec((512, n), lambda i: (i, 0))
    tail = pl.BlockSpec((16, NB), lambda i: (1024 // 16, 0))
    return pl.pallas_call(
        panel_kernel, grid=(2,),
        out_shape=(
            jax.ShapeDtypeStruct((1024, 512), F32),
            jax.ShapeDtypeStruct((1024, 512), BF16),
            jax.ShapeDtypeStruct((1024, 512), BF16),
            jax.ShapeDtypeStruct((16, 512), F32),
        ),
        in_specs=[SMEM, part(NB), part(NB), tail, tail, full(NB, NB), full(NB, NB), full(NB, NB)],
        out_specs=(part(512), part(512), part(512), full(16, 512)),
        scratch_shapes=[pltpu.VMEM((2, 3, NB, NB), BF16)],
        name="panel_solve", **FACTOR,
    )(place, mine, theirs, mine, theirs, w00, l10, w11)


def update_kernel(place, flat, across, high, low, sums, taken, out, checksum, right_high, right_low):
    group, step = pl.program_id(0), pl.program_id(1)
    row_index, col_index = place[0], place[1]

    @pl.when(step == 0)
    def _():
        for u in range(4):
            for h in range(2):
                span = slice(NB * h, NB * h + NB)
                right_high[u, span], right_low[u, span] = halves(across[2 * u + h])

    rows = out.shape[0]
    base = pl.multiple_of(step * rows, rows)
    top = (step * rows + lax.broadcasted_iota(jnp.int32, (rows, 1), 0) < NB) & (row_index < 2)
    y_high, y_low = halves(taken[...])
    mine = (
        jnp.concatenate([high[pl.ds(base, rows), :], y_high], axis=0),
        jnp.concatenate([low[pl.ds(base, rows), :], y_low], axis=0),
    )
    for u in range(4):
        product = dot3(mine, (right_high[u], right_low[u]), NN)
        gone = top | ((group == 0) & (col_index < 2)) if u == 0 else top
        for h in range(2):
            q = 2 * u + h
            value = flat[:, q, :] - product[0:rows, 128 * h : 128 * h + 128]
            out[:, q, :] = jnp.where(gone, 0.0, value)

            @pl.when(step == 0)
            def _():
                kept = sums[pl.ds(8 * group + q, 1), :] - product[rows : rows + 1, 128 * h : 128 * h + 128]
                if u == 0:
                    kept = jnp.where((group == 0) & (col_index < 2), 0.0, kept)
                checksum[pl.ds(8 * group + q, 1), :] = kept


def update_call(place, flat, across, high, low, sums, taken):
    rows = 256
    full = lambda *shape: pl.BlockSpec(shape, lambda g, i: (0,) * len(shape))
    return pl.pallas_call(
        update_kernel, grid=(2, 1024 // rows),
        out_shape=(jax.ShapeDtypeStruct((1024, 16, 128), F32), jax.ShapeDtypeStruct((16, 128), F32)),
        in_specs=[
            SMEM,
            pl.BlockSpec((rows, 8, 128), lambda g, i: (i, g, 0)),
            pl.BlockSpec((8, NB, NB), lambda g, i: (g, 0, 0)),
            full(1024, 512),
            full(1024, 512),
            full(16, 128),
            full(16, 512),
        ],
        out_specs=(pl.BlockSpec((rows, 8, 128), lambda g, i: (i, g, 0)), full(16, 128)),
        scratch_shapes=[pltpu.VMEM((4, 512, NB), BF16), pltpu.VMEM((4, 512, NB), BF16)],
        name="trailing_update", **FACTOR,
    )(place, flat, across, high, low, sums, taken)


def where_is(device):
    row, col = divmod(device, 8)
    return [row // 4, row % 4, col // 2, col % 2]


def device_at(z, y, x, core):
    return ((z % 4) * 4 + y % 4) * 8 + (x % 4) * 2 + core


def moved(device, dim, by):
    at = where_is(device)
    at[dim] += by
    return device_at(*at)


def spread(value, trees, here):
    holders = [[device_at(z, y, 0, c)] for (z, y), c, _ in trees]
    stages = []
    for at in range(3):
        aways = [(here[dims[at]] - (z, y, 0)[dims[at]]) % 4 for (z, y), _, dims in trees]
        away = jnp.where(here[3] == trees[0][1], aways[0], aways[1])
        for half in range(2):
            pairs = []
            for held, (_, _, dims) in zip(holders, trees):
                dim = dims[at]
                if half == 0:
                    pairs += [(h, moved(h, dim, 1)) for h in held]
                else:
                    pairs += [(h, moved(h, dim, -1)) for h in held] + [(moved(h, dim, 1), moved(h, dim, 2)) for h in held]
            arrived = lax.ppermute(value, ("row", "col"), pairs)
            value = jnp.where((away == 1) if half == 0 else (away >= 2), arrived, value)
            stages.append(value)
        holders = [[moved(h, dims[at], k) for h in held for k in range(4)] for held, (_, _, dims) in zip(holders, trees)]
    return stages


def after(value, token):
    return lax.optimization_barrier((value, token))[0]


def shards(covariance, check_weights):
    row = lax.axis_index("row")
    col = lax.axis_index("col")
    core = col % 2
    x = col // 2
    here = [row // 4, row % 4, x, core]
    flat = pltpu.with_memory_space_constraint(covariance.reshape(1024, 16, 128), pltpu.HBM)
    tiles = jnp.arange(4, dtype=jnp.int32) * 16 + row
    weights = jnp.where((tiles >= 2)[:, None], check_weights.reshape(4, NB), 0.0).reshape(1024)
    place = jnp.stack([row, col]).astype(jnp.int32)
    swap_cores = [(c, c ^ 1) for c in range(8)]

    pieces = corner_call(flat)
    fetched = lax.ppermute(pieces[0], ("row", "col"), [(8, 0), (9, 1)])
    corner = jnp.where(
        core == 0,
        jnp.concatenate([pieces[0], fetched[0:128]], axis=0),
        jnp.concatenate([fetched, pieces[9]], axis=0),
    )
    tree = spread(corner, [((0, 0), 0, (2, 1, 0)), ((0, 0), 1, (1, 0, 2))], here)
    own = tree[-1]
    other = lax.ppermute(own, "col", swap_cores)

    piece = pieces[8]
    for j in range(1, 8):
        piece = jnp.where(row // 2 == j, lax.ppermute(pieces[j], "row", [(0, 2 * j), (1, 2 * j + 1)]), piece)
    across = lax.all_gather(after(piece, tree[0]), "row", axis=0)
    across = pltpu.with_memory_space_constraint(across, pltpu.HBM)

    column, sums = column_call(weights, after(flat, corner))
    for d, stage in ((1, 1), (3, 2), (4, 3), (12, 4)):
        sums = sums + lax.ppermute(after(sums, tree[stage]), "row", [(r, r ^ d) for r in range(16)])
    near_sums = jnp.broadcast_to(sums[0:2].reshape(1, NB), (16, NB))
    panel_sums = near_sums
    for k in (1, 2, 3):
        arrived = lax.ppermute(near_sums, "col", [(0, 2 * k), (1, 2 * k + 1)])
        panel_sums = jnp.where(x == k, arrived, panel_sums)

    w00 = first_factor(place, own, other)
    l10, w11 = second_factor(place, w00, own, other)
    from_left = lax.ppermute(column, "col", [(0, 2), (1, 3)])
    from_right = lax.ppermute(column, "col", [(0, 6), (1, 7)])
    from_left, from_right = after((from_left, from_right), tree[5])
    mine = jnp.where(x == 1, from_left, jnp.where(x == 3, from_right, column))
    upper = lax.ppermute(mine[0:512], "col", [(2, 4), (3, 5)])
    lower = lax.ppermute(mine[512:1024], "col", [(6, 4), (7, 5)])
    upper, lower = after((upper, lower), w00)
    upper = jnp.where(x == 2, upper, mine[0:512])
    lower = jnp.where(x == 2, lower, mine[512:1024])
    mine = jnp.concatenate([upper, lower, panel_sums], axis=0)
    theirs = after(lax.ppermute(mine, "col", swap_cores), w11)

    panels, high, low, taken = panel_call(place, mine, theirs, w00, l10, w11)
    trailing, checksum = update_call(place, flat, across, high, low, sums, taken)
    return (
        trailing.reshape(4, 1, NB, 8, 1, NB),
        panels.reshape(4, 1, NB, 512),
        checksum.reshape(8, 1, NB),
    )


def solution(mesh):
    in_specs = (P(None, "row", None, None, "col", None), P(None, "row", None))
    out_specs = (
        P(None, "row", None, None, "col", None),
        P(None, "row", None, None),
        P(None, "col", None),
    )
    return jax.shard_map(shards, mesh=mesh, in_specs=in_specs, out_specs=out_specs, check_vma=False)
```

```python
import functools

import jax
import jax.numpy as jnp
from jax import lax
from jax.experimental import pallas as pl
from jax.experimental.pallas import tpu as pltpu
from jax.sharding import PartitionSpec as P

HIGHEST = lax.Precision.HIGHEST
F32 = jnp.float32
BF16 = jnp.bfloat16
NB = 256
NT = (((1,), (1,)), ((), ()))
NN = (((1,), (0,)), ((), ()))


def dot6(a, b, dims):
    return lax.dot_general(a, b, dims, precision=HIGHEST, preferred_element_type=F32)


def halves(value):
    high = value.astype(BF16)
    return high, (value - high.astype(F32)).astype(BF16)


def dot3(a, b, dims):
    total = lax.dot_general(a[0], b[0], dims, preferred_element_type=F32)
    total += lax.dot_general(a[0], b[1], dims, preferred_element_type=F32)
    return total + lax.dot_general(a[1], b[0], dims, preferred_element_type=F32)


def splat_row(ref, row, lanes):
    return jnp.broadcast_to(ref[row : row + 1, lanes], (8, 128))


def splat_lane(value, lane):
    return jnp.broadcast_to(value[:, lane : lane + 1], (8, 128))


def invert_factor(m, put):
    left, right = slice(0, 128), slice(128, 256)
    for block in range(16):
        base = 8 * block
        rows = [[splat_row(m, base + a, side) for a in range(8)] for side in (left, right)]
        b = {(a, k): splat_lane(rows[0][a], base + k) for a in range(8) for k in range(a + 1)}
        n = {}
        inverse, root = [], []
        for i in range(8):
            inverse.append(1.0 / b[i, i])
            root.append(lax.rsqrt(b[i, i]))
            for k in range(i + 1, 8):
                ratio = b[k, i] * inverse[i]
                for j in range(i + 1, k + 1):
                    b[k, j] = b[k, j] - ratio * b[j, i]
                for j in range(i):
                    n[k, j] = n[k, j] - ratio * n[i, j]
                n[k, i] = -ratio
        solved = []
        for side in range(2):
            upper = []
            for i in range(8):
                value = rows[side][i]
                for j in range(i):
                    value = value + n[i, j] * rows[side][j]
                upper.append(value)
            if side == 1:
                for i in range(8):
                    put(base + i, root[i] * upper[i])
            scaled = [inverse[i] * upper[i] for i in range(8)]
            out = []
            for i in range(8):
                value = scaled[i]
                for k in range(i + 1, 8):
                    value = value + n[k, i] * scaled[k]
                out.append(value)
            solved.append(out)
        for other in range(block + 1, 16):
            span = slice(8 * other, 8 * other + 8)
            a_part, n_part = m[span, left], m[span, right]
            columns = [splat_lane(a_part, base + i) for i in range(8)]
            for i in range(8):
                a_part = a_part - columns[i] * solved[0][i]
                n_part = n_part - columns[i] * solved[1][i]
            m[span, left] = a_part
            m[span, right] = n_part


def factor_tile(source, out, m, part):
    eye = (lax.broadcasted_iota(jnp.int32, (128, 128), 0) == lax.broadcasted_iota(jnp.int32, (128, 128), 1)).astype(F32)
    m[:, 0:128] = source[0:128, 0:128]

    def body(i, carry):
        m[:, 128:256] = eye

        def put(row, value):
            part[i, row : row + 1, :] = value[0:1, :]

        invert_factor(m, put)

        @pl.when(i == 0)
        def _():
            low = dot6(source[128:256, 0:128], part[0], NT)
            m[:, 0:128] = source[128:256, 128:256] - dot6(low, low, NT)
            part[2] = low

        return carry

    lax.fori_loop(0, 2, body, 0)
    out[0:128, 0:128] = part[0]
    out[0:128, 128:256] = jnp.zeros((128, 128), F32)
    out[128:256, 128:256] = part[1]
    out[128:256, 0:128] = -dot6(part[1], dot6(part[2], part[0], NN), NN)


def first_kernel(place, own, other, w00, tile, m, part):
    tile[...] = jnp.where(place[1] % 2 == 0, own[0:NB], other[0:NB])
    factor_tile(tile, w00, m, part)


def second_kernel(place, w00, own, other, l10, w11, schur, m, part):
    even = place[1] % 2 == 0
    top, bottom = own[NB : NB + 128], other[NB : NB + 128]
    c10 = jnp.concatenate([jnp.where(even, top, bottom), jnp.where(even, bottom, top)], axis=0)
    low = dot6(c10, w00[...], NT)
    l10[...] = low
    schur[...] = jnp.where(even, other[0:NB], own[0:NB]) - dot6(low, low, NT)
    factor_tile(schur, w11, m, part)


TILE = jax.ShapeDtypeStruct((NB, NB), F32)
WORK = [pltpu.VMEM((128, 256), F32), pltpu.VMEM((3, 128, 128), F32)]
VMEM = pl.BlockSpec(memory_space=pltpu.VMEM)
SMEM = pl.BlockSpec(memory_space=pltpu.SMEM)


LIMIT = 24 * 1024 * 1024
SMALL = pl.CostEstimate(flops=100_000_000, bytes_accessed=100_000, transcendentals=0)
FACTOR = dict(compiler_params=pltpu.CompilerParams(vmem_limit_bytes=LIMIT), cost_estimate=SMALL)
TILE_WORK = [pltpu.VMEM((NB, NB), F32)] + WORK


def first_factor(place, own, other):
    return pl.pallas_call(
        first_kernel, out_shape=TILE, in_specs=[SMEM, VMEM, VMEM], out_specs=VMEM,
        scratch_shapes=TILE_WORK, name="first_factor", **FACTOR,
    )(place, own, other)


def second_factor(place, w00, own, other):
    return pl.pallas_call(
        second_kernel, out_shape=(TILE, TILE), in_specs=[SMEM, VMEM, VMEM, VMEM], out_specs=(VMEM, VMEM),
        scratch_shapes=TILE_WORK, name="second_factor", **FACTOR,
    )(place, w00, own, other)


def corner_kernel(a, *pieces):
    *pieces, flipped = pieces
    flipped[...] = a[:, 1, :].T
    for q in range(16):
        value = a[:, q, :]
        for ref in pieces[q // 2 :: 8]:
            ref[:, 128 * (q % 2) : 128 * (q % 2) + 128] = value


def corner_call(flat):
    return pl.pallas_call(
        corner_kernel, grid=(2,), out_shape=(TILE,) * 9 + (jax.ShapeDtypeStruct((128, NB), F32),),
        in_specs=[pl.BlockSpec((128, 16, 128), lambda i: (i, 0, 0))],
        out_specs=(pl.BlockSpec((128, NB), lambda i: (i, 0)),) * 9 + (pl.BlockSpec((128, 128), lambda i: (0, i)),),
        name="corner_tiles",
    )(flat)


def column_kernel(weights, a, column, sums):
    step = pl.program_id(0)
    for q in range(2):
        column[:, 128 * q : 128 * q + 128] = a[:, q, :]

    @pl.when(step == 0)
    def _():
        sums[...] = jnp.zeros_like(sums)

    def body(i, total):
        for j in range(8):
            row = 8 * i + j
            total = total + weights[step * 128 + row] * a[row]
        return total

    sums[...] += lax.fori_loop(0, 16, body, jnp.zeros((16, 128), F32))


def column_call(weights, flat):
    return pl.pallas_call(
        column_kernel, grid=(8,),
        out_shape=(jax.ShapeDtypeStruct((1024, NB), F32), jax.ShapeDtypeStruct((16, 128), F32)),
        in_specs=[SMEM, pl.BlockSpec((128, 16, 128), lambda i: (i, 0, 0))],
        out_specs=(
            pl.BlockSpec((128, NB), lambda i: (i, 0)),
            pl.BlockSpec((16, 128), lambda i: (0, 0)),
        ),
        name="first_column", **FACTOR,
    )(weights, flat)


def panel_kernel(place, mine, theirs, own_sums, other_sums, w00, l10, w11, panels, high, low, taken, factors):
    step = pl.program_id(0)
    even = place[1] % 2 == 0

    @pl.when(step == 0)
    def _():
        for k, ref in enumerate((w00, l10, w11)):
            factors[0, k], factors[1, k] = halves(ref[...])

    f00, f10, f11 = [(factors[0, k], factors[1, k]) for k in range(3)]
    own = jnp.concatenate([mine[...], own_sums[...]], axis=0)
    other = jnp.concatenate([theirs[...], other_sums[...]], axis=0)
    first = jnp.where(even, own, other)
    second = jnp.where(even, other, own)
    left = dot3(halves(first), f00, NT)
    right = dot3(halves(second - dot3(halves(left), f10, NT)), f11, NT)
    panels[:, 0:256] = left[0:512]
    top = (step == 0) & (place[0] == 0) & (lax.broadcasted_iota(jnp.int32, (512, 1), 0) < NB)
    panels[:, 256:512] = jnp.where(top, 0.0, right[0:512])
    last = dot3(halves(right), f11, NN)
    last_high, last_low = halves(last)
    rest = dot3(halves(left - dot3((last_high, last_low), f10, NN)), f00, NN)
    high[:, 256:512] = last_high[0:512]
    low[:, 256:512] = last_low[0:512]
    high[:, 0:256], low[:, 0:256] = halves(rest[0:512])
    taken[:, 0:256] = rest[512:528]
    taken[:, 256:512] = last[512:528]


def panel_call(place, mine, theirs, w00, l10, w11):
    full = lambda *shape: pl.BlockSpec(shape, lambda i: (0,) * len(shape))
    part = lambda n: pl.BlockSpec((512, n), lambda i: (i, 0))
    tail = pl.BlockSpec((16, NB), lambda i: (1024 // 16, 0))
    return pl.pallas_call(
        panel_kernel, grid=(2,),
        out_shape=(
            jax.ShapeDtypeStruct((1024, 512), F32),
            jax.ShapeDtypeStruct((1024, 512), BF16),
            jax.ShapeDtypeStruct((1024, 512), BF16),
            jax.ShapeDtypeStruct((16, 512), F32),
        ),
        in_specs=[SMEM, part(NB), part(NB), tail, tail, full(NB, NB), full(NB, NB), full(NB, NB)],
        out_specs=(part(512), part(512), part(512), full(16, 512)),
        scratch_shapes=[pltpu.VMEM((2, 3, NB, NB), BF16)],
        name="panel_solve", **FACTOR,
    )(place, mine, theirs, mine, theirs, w00, l10, w11)


def update_kernel(place, flat, across, high, low, sums, taken, out, checksum, right_high, right_low):
    group, step = pl.program_id(0), pl.program_id(1)
    row_index, col_index = place[0], place[1]

    @pl.when(step == 0)
    def _():
        for u in range(4):
            for h in range(2):
                span = slice(NB * h, NB * h + NB)
                right_high[u, span], right_low[u, span] = halves(across[2 * u + h])

    rows = out.shape[0]
    base = pl.multiple_of(step * rows, rows)
    top = (step * rows + lax.broadcasted_iota(jnp.int32, (rows, 1), 0) < NB) & (row_index < 2)
    y_high, y_low = halves(taken[...])
    mine = (
        jnp.concatenate([high[pl.ds(base, rows), :], y_high], axis=0),
        jnp.concatenate([low[pl.ds(base, rows), :], y_low], axis=0),
    )
    for u in range(4):
        product = dot3(mine, (right_high[u], right_low[u]), NN)
        gone = top | ((group == 0) & (col_index < 2)) if u == 0 else top
        for h in range(2):
            q = 2 * u + h
            value = flat[:, q, :] - product[0:rows, 128 * h : 128 * h + 128]
            out[:, q, :] = jnp.where(gone, 0.0, value)
            kept = sums[q : q + 1, :] - product[rows : rows + 1, 128 * h : 128 * h + 128]
            if u == 0:
                kept = jnp.where((group == 0) & (col_index < 2), 0.0, kept)
            checksum[q : q + 1, :] = kept


def update_call(place, flat, across, high, low, sums, taken):
    rows = 256
    full = lambda *shape: pl.BlockSpec(shape, lambda g, i: (0,) * len(shape))
    return pl.pallas_call(
        update_kernel, grid=(2, 1024 // rows),
        out_shape=(jax.ShapeDtypeStruct((1024, 16, 128), F32), jax.ShapeDtypeStruct((16, 128), F32)),
        in_specs=[
            SMEM,
            pl.BlockSpec((rows, 8, 128), lambda g, i: (i, g, 0)),
            pl.BlockSpec((8, NB, NB), lambda g, i: (g, 0, 0)),
            full(1024, 512),
            full(1024, 512),
            pl.BlockSpec((8, 128), lambda g, i: (g, 0)),
            full(16, 512),
        ],
        out_specs=(pl.BlockSpec((rows, 8, 128), lambda g, i: (i, g, 0)), pl.BlockSpec((8, 128), lambda g, i: (g, 0))),
        scratch_shapes=[pltpu.VMEM((4, 512, NB), BF16), pltpu.VMEM((4, 512, NB), BF16)],
        name="trailing_update", **FACTOR,
    )(place, flat, across, high, low, sums, taken)


def where_is(device):
    row, col = divmod(device, 8)
    return [row // 4, row % 4, col // 2, col % 2]


def device_at(z, y, x, core):
    return ((z % 4) * 4 + y % 4) * 8 + (x % 4) * 2 + core


def moved(device, dim, by):
    at = where_is(device)
    at[dim] += by
    return device_at(*at)


def spread(value, trees, here, beside):
    holders = [[device_at(z, y, 0, c)] for (z, y), c, _ in trees]
    stages = []
    for at in range(3):
        aways = [(here[dims[at]] - (z, y, 0)[dims[at]]) % 4 for (z, y), _, dims in trees]
        away = jnp.where(here[3] == trees[0][1], aways[0], aways[1])
        for half in range(2):
            pairs = []
            for held, (_, _, dims) in zip(holders, trees):
                dim = dims[at]
                if half == 0:
                    pairs += [(h, moved(h, dim, 1)) for h in held]
                else:
                    pairs += [(h, moved(h, dim, -1)) for h in held] + [(moved(h, dim, 1), moved(h, dim, 2)) for h in held]
            if stages:
                value = beside(len(stages), value)
            arrived = lax.ppermute(value, ("row", "col"), pairs)
            value = jnp.where((away == 1) if half == 0 else (away >= 2), arrived, value)
            stages.append(value)
        holders = [[moved(h, dims[at], k) for h in held for k in range(4)] for held, (_, _, dims) in zip(holders, trees)]
    return stages


def after(value, token):
    return lax.optimization_barrier((value, token))[0]


def shards(covariance, check_weights):
    row = lax.axis_index("row")
    col = lax.axis_index("col")
    core = col % 2
    x = col // 2
    here = [row // 4, row % 4, x, core]
    flat = pltpu.with_memory_space_constraint(covariance.reshape(1024, 16, 128), pltpu.HBM)
    tiles = jnp.arange(4, dtype=jnp.int32) * 16 + row
    weights = jnp.where((tiles >= 2)[:, None], check_weights.reshape(4, NB), 0.0).reshape(1024)
    place = jnp.stack([row, col]).astype(jnp.int32)
    swap_cores = [(c, c ^ 1) for c in range(8)]

    pieces = corner_call(flat)
    fetched = lax.ppermute(pieces[0], ("row", "col"), [(8, 0), (9, 1)])
    corner = jnp.where(
        core == 0,
        jnp.concatenate([pieces[0], fetched[0:128]], axis=0),
        jnp.concatenate([fetched, pieces[9]], axis=0),
    )
    column, sums = column_call(weights, after(flat, corner))
    partial = [sums]

    def beside(stage, value):
        before = partial[-1]
        if stage >= 2:
            d = (1, 3, 4, 12)[stage - 2]
            partial.append(before + lax.ppermute(after(before, value), "row", [(r, r ^ d) for r in range(16)]))
        return after(value, before)

    tree = spread(corner, [((0, 0), 0, (2, 1, 0)), ((0, 0), 1, (1, 0, 2))], here, beside)
    sums = partial[-1]
    own = tree[-1]
    other = lax.ppermute(own, "col", swap_cores)

    piece = pieces[8]
    for j in range(1, 8):
        piece = jnp.where(row // 2 == j, lax.ppermute(pieces[j] if j < 4 else after(pieces[j], fetched), "row", [(0, 2 * j), (1, 2 * j + 1)]), piece)
    across = lax.all_gather(after(piece, (tree[0], column)), "row", axis=0)
    across = pltpu.with_memory_space_constraint(across, pltpu.HBM)

    near_sums = jnp.broadcast_to(sums[0:2].reshape(1, NB), (16, NB))
    far_sums = [lax.ppermute(near_sums, "col", [(0, 2 * k), (1, 2 * k + 1)]) for k in (1, 2, 3)]
    w00 = first_factor(place, own, other)
    far_sums = after(far_sums, w00)
    panel_sums = near_sums
    for k in (1, 2, 3):
        panel_sums = jnp.where(x == k, far_sums[k - 1], panel_sums)

    l10, w11 = second_factor(place, w00, own, other)
    from_left = lax.ppermute(column, "col", [(0, 2), (1, 3)])
    from_right = lax.ppermute(column, "col", [(0, 6), (1, 7)])
    from_left, from_right = after((from_left, from_right), tree[5])
    mine = jnp.where(x == 1, from_left, jnp.where(x == 3, from_right, column))
    upper = lax.ppermute(mine[0:512], "col", [(2, 4), (3, 5)])
    lower = lax.ppermute(mine[512:1024], "col", [(6, 4), (7, 5)])
    upper, lower = after((upper, lower), w00)
    upper = jnp.where(x == 2, upper, mine[0:512])
    lower = jnp.where(x == 2, lower, mine[512:1024])
    mine = jnp.concatenate([upper, lower, panel_sums], axis=0)
    theirs = after(lax.ppermute(mine, "col", swap_cores), w11)

    panels, high, low, taken = panel_call(place, mine, theirs, w00, l10, w11)
    trailing, checksum = update_call(place, flat, across, high, low, sums, taken)
    return (
        trailing.reshape(4, 1, NB, 8, 1, NB),
        panels.reshape(4, 1, NB, 512),
        checksum.reshape(8, 1, NB),
    )


def solution(mesh):
    in_specs = (P(None, "row", None, None, "col", None), P(None, "row", None))
    out_specs = (
        P(None, "row", None, None, "col", None),
        P(None, "row", None, None),
        P(None, "col", None),
    )
    return jax.shard_map(shards, mesh=mesh, in_specs=in_specs, out_specs=out_specs, check_vma=False)
```

```python
import functools

import jax
import jax.numpy as jnp
from jax import lax
from jax.experimental import pallas as pl
from jax.experimental.pallas import tpu as pltpu
from jax.sharding import PartitionSpec as P

HIGHEST = lax.Precision.HIGHEST
F32 = jnp.float32
BF16 = jnp.bfloat16
NB = 256
NT = (((1,), (1,)), ((), ()))
NN = (((1,), (0,)), ((), ()))


def dot6(a, b, dims):
    return lax.dot_general(a, b, dims, precision=HIGHEST, preferred_element_type=F32)


def halves(value):
    high = value.astype(BF16)
    return high, (value - high.astype(F32)).astype(BF16)


def dot3(a, b, dims):
    total = lax.dot_general(a[0], b[0], dims, preferred_element_type=F32)
    total += lax.dot_general(a[0], b[1], dims, preferred_element_type=F32)
    return total + lax.dot_general(a[1], b[0], dims, preferred_element_type=F32)


def splat_row(ref, row, lanes):
    return jnp.broadcast_to(ref[row : row + 1, lanes], (8, 128))


def splat_lane(value, lane):
    return jnp.broadcast_to(value[:, lane : lane + 1], (8, 128))


def invert_factor(m, put):
    left, right = slice(0, 128), slice(128, 256)
    for block in range(16):
        base = 8 * block
        rows = [[splat_row(m, base + a, side) for a in range(8)] for side in (left, right)]
        b = {(a, k): splat_lane(rows[0][a], base + k) for a in range(8) for k in range(a + 1)}
        n = {}
        inverse, root = [], []
        for i in range(8):
            inverse.append(1.0 / b[i, i])
            root.append(lax.rsqrt(b[i, i]))
            for k in range(i + 1, 8):
                ratio = b[k, i] * inverse[i]
                for j in range(i + 1, k + 1):
                    b[k, j] = b[k, j] - ratio * b[j, i]
                for j in range(i):
                    n[k, j] = n[k, j] - ratio * n[i, j]
                n[k, i] = -ratio
        solved = []
        for side in range(2):
            upper = []
            for i in range(8):
                value = rows[side][i]
                for j in range(i):
                    value = value + n[i, j] * rows[side][j]
                upper.append(value)
            if side == 1:
                for i in range(8):
                    put(base + i, root[i] * upper[i])
            scaled = [inverse[i] * upper[i] for i in range(8)]
            out = []
            for i in range(8):
                value = scaled[i]
                for k in range(i + 1, 8):
                    value = value + n[k, i] * scaled[k]
                out.append(value)
            solved.append(out)
        for other in range(block + 1, 16):
            span = slice(8 * other, 8 * other + 8)
            a_part, n_part = m[span, left], m[span, right]
            columns = [splat_lane(a_part, base + i) for i in range(8)]
            for i in range(8):
                a_part = a_part - columns[i] * solved[0][i]
                n_part = n_part - columns[i] * solved[1][i]
            m[span, left] = a_part
            m[span, right] = n_part


def factor_tile(source, out, m, part):
    eye = (lax.broadcasted_iota(jnp.int32, (128, 128), 0) == lax.broadcasted_iota(jnp.int32, (128, 128), 1)).astype(F32)
    m[:, 0:128] = source[0:128, 0:128]

    def body(i, carry):
        m[:, 128:256] = eye

        def put(row, value):
            part[i, row : row + 1, :] = value[0:1, :]

        invert_factor(m, put)

        @pl.when(i == 0)
        def _():
            low = dot6(source[128:256, 0:128], part[0], NT)
            m[:, 0:128] = source[128:256, 128:256] - dot6(low, low, NT)
            part[2] = low

        return carry

    lax.fori_loop(0, 2, body, 0)
    out[0:128, 0:128] = part[0]
    out[0:128, 128:256] = jnp.zeros((128, 128), F32)
    out[128:256, 128:256] = part[1]
    out[128:256, 0:128] = -dot6(part[1], dot6(part[2], part[0], NN), NN)


def first_kernel(place, own, other, w00, tile, m, part):
    tile[...] = jnp.where(place[1] % 2 == 0, own[0:NB], other[0:NB])
    factor_tile(tile, w00, m, part)


def second_kernel(place, w00, own, other, l10, w11, schur, m, part):
    even = place[1] % 2 == 0
    top, bottom = own[NB : NB + 128], other[NB : NB + 128]
    c10 = jnp.concatenate([jnp.where(even, top, bottom), jnp.where(even, bottom, top)], axis=0)
    low = dot6(c10, w00[...], NT)
    l10[...] = low
    schur[...] = jnp.where(even, other[0:NB], own[0:NB]) - dot6(low, low, NT)
    factor_tile(schur, w11, m, part)


TILE = jax.ShapeDtypeStruct((NB, NB), F32)
WORK = [pltpu.VMEM((128, 256), F32), pltpu.VMEM((3, 128, 128), F32)]
VMEM = pl.BlockSpec(memory_space=pltpu.VMEM)
SMEM = pl.BlockSpec(memory_space=pltpu.SMEM)


LIMIT = 24 * 1024 * 1024
SMALL = pl.CostEstimate(flops=100_000_000, bytes_accessed=100_000, transcendentals=0)
FACTOR = dict(compiler_params=pltpu.CompilerParams(vmem_limit_bytes=LIMIT), cost_estimate=SMALL)
TILE_WORK = [pltpu.VMEM((NB, NB), F32)] + WORK


def first_factor(place, own, other):
    return pl.pallas_call(
        first_kernel, out_shape=TILE, in_specs=[SMEM, VMEM, VMEM], out_specs=VMEM,
        scratch_shapes=TILE_WORK, name="first_factor", **FACTOR,
    )(place, own, other)


def second_factor(place, w00, own, other):
    return pl.pallas_call(
        second_kernel, out_shape=(TILE, TILE), in_specs=[SMEM, VMEM, VMEM, VMEM], out_specs=(VMEM, VMEM),
        scratch_shapes=TILE_WORK, name="second_factor", **FACTOR,
    )(place, w00, own, other)


def corner_kernel(a, *pieces):
    *pieces, flipped = pieces
    flipped[...] = a[:, 1, :].T
    for q in range(16):
        value = a[:, q, :]
        for ref in pieces[q // 2 :: 8]:
            ref[:, 128 * (q % 2) : 128 * (q % 2) + 128] = value


def corner_call(flat):
    return pl.pallas_call(
        corner_kernel, grid=(2,), out_shape=(TILE,) * 9 + (jax.ShapeDtypeStruct((128, NB), F32),),
        in_specs=[pl.BlockSpec((128, 16, 128), lambda i: (i, 0, 0))],
        out_specs=(pl.BlockSpec((128, NB), lambda i: (i, 0)),) * 9 + (pl.BlockSpec((128, 128), lambda i: (0, i)),),
        name="corner_tiles",
    )(flat)


def column_kernel(weights, a, column, sums):
    step = pl.program_id(0)
    for q in range(2):
        column[:, 128 * q : 128 * q + 128] = a[:, q, :]

    @pl.when(step == 0)
    def _():
        sums[...] = jnp.zeros_like(sums)

    def body(i, total):
        for j in range(8):
            row = 8 * i + j
            total = total + weights[step * 128 + row] * a[row]
        return total

    sums[...] += lax.fori_loop(0, 16, body, jnp.zeros((16, 128), F32))


def column_call(weights, flat):
    return pl.pallas_call(
        column_kernel, grid=(8,),
        out_shape=(jax.ShapeDtypeStruct((1024, NB), F32), jax.ShapeDtypeStruct((16, 128), F32)),
        in_specs=[SMEM, pl.BlockSpec((128, 16, 128), lambda i: (i, 0, 0))],
        out_specs=(
            pl.BlockSpec((128, NB), lambda i: (i, 0)),
            pl.BlockSpec((16, 128), lambda i: (0, 0)),
        ),
        name="first_column", **FACTOR,
    )(weights, flat)


ROWS = 256


def final_kernel(
    place, flat, across, mine, theirs, w00, l10, w11, sums, out, panels, checksum,
    block, right, solved, high, low, right_high, right_low, ready, factors, block_sem, right_sem, panel_sem, out_sem,
):
    row_index, col_index = place[0], place[1]
    even = col_index % 2 == 0
    blocks = [
        pltpu.make_async_copy(flat.at[pl.ds(ROWS * i, ROWS)], block.at[pl.ds(ROWS * i, ROWS)], block_sem.at[i]) for i in range(4)
    ]
    rights = [pltpu.make_async_copy(across.at[pl.ds(8 * i, 8)], right.at[pl.ds(8 * i, 8)], right_sem.at[i]) for i in range(2)]
    for copy in (rights[0], *blocks, rights[1]):
        copy.start()

    for k, ref in enumerate((w00, l10, w11)):
        factors[0, k], factors[1, k] = halves(ref[...])
    f00, f10, f11 = [(factors[0, k], factors[1, k]) for k in range(3)]
    solves = []
    for half in range(2):
        rows = slice(512 * half, 512 * half + 512 + 16 * half)
        first = jnp.where(even, mine[rows], theirs[rows])
        second = jnp.where(even, theirs[rows], mine[rows])
        left = dot3(halves(first), f00, NT)
        bottom = dot3(halves(second - dot3(halves(left), f10, NT)), f11, NT)
        solved[512 * half : 512 * half + 512, 0:256] = left[0:512]
        if half == 0:
            top = (row_index == 0) & (lax.broadcasted_iota(jnp.int32, (512, 1), 0) < NB)
            solved[0:512, 256:512] = jnp.where(top, 0.0, bottom)
        else:
            solved[512:1024, 256:512] = bottom[0:512]
        copy = pltpu.make_async_copy(
            solved.at[pl.ds(512 * half, 512)], panels.at[pl.ds(512 * half, 512)], panel_sem.at[half]
        )
        copy.start()
        solves.append(copy)
        last = halves(dot3(halves(bottom), f11, NN))
        high[rows, 256:512], low[rows, 256:512] = last
        high[rows, 0:256], low[rows, 0:256] = halves(dot3(halves(left - dot3(last, f10, NN)), f00, NN))

    def put(slot, group, step):
        return pltpu.make_async_copy(
            ready.at[slot], out.at[pl.ds(pl.multiple_of(step * ROWS, ROWS), ROWS), group], out_sem.at[slot]
        )

    for group in range(2):
        rights[group].wait()
        for u in range(4):
            for h in range(2):
                span = slice(NB * h, NB * h + NB)
                right_high[u, span], right_low[u, span] = halves(right[8 * group + 2 * u + h])

        def body(step, carry, group=group):
            slot = step % 2
            base = pl.multiple_of(step * ROWS, ROWS)
            if group == 0:
                for i in range(4):

                    @pl.when(step == i)
                    def _(i=i):
                        blocks[i].wait()

            @pl.when(step + 4 * group >= 2)
            def _():
                put(slot, group, step).wait()

            g_high = jnp.concatenate([high[pl.ds(base, ROWS), :], high[1024:1040, :]], axis=0)
            g_low = jnp.concatenate([low[pl.ds(base, ROWS), :], low[1024:1040, :]], axis=0)
            top = (step * ROWS + lax.broadcasted_iota(jnp.int32, (ROWS, 1), 0) < NB) & (row_index < 2)
            for u in range(4):
                product = dot3((g_high, g_low), (right_high[u], right_low[u]), NN)
                gone = top | (col_index < 2) if (group, u) == (0, 0) else top
                for h in range(2):
                    q = 2 * u + h
                    lanes = slice(128 * h, 128 * h + 128)
                    value = block[pl.ds(base, ROWS), group, q, :] - product[0:ROWS, lanes]
                    ready[slot, :, q, :] = jnp.where(gone, 0.0, value)
                    at = 8 * group + q
                    kept = sums[at : at + 1, :] - product[ROWS : ROWS + 1, lanes]
                    if (group, u) == (0, 0):
                        kept = jnp.where(col_index < 2, 0.0, kept)
                    checksum[at : at + 1, :] = kept
            put(slot, group, step).start()
            return carry

        lax.fori_loop(0, 4, body, 0)
    for slot in range(2):
        put(slot, 1, 2 + slot).wait()
    for copy in solves:
        copy.wait()


def final_call(place, flat, across, mine, theirs, w00, l10, w11, sums):
    hbm = pl.BlockSpec(memory_space=pl.ANY)
    return pl.pallas_call(
        final_kernel,
        out_shape=(
            jax.ShapeDtypeStruct((1024, 2, 8, 128), F32),
            jax.ShapeDtypeStruct((1024, 512), F32),
            jax.ShapeDtypeStruct((16, 128), F32),
        ),
        in_specs=[SMEM, hbm, hbm] + [VMEM] * 6,
        out_specs=(hbm, hbm, VMEM),
        scratch_shapes=[
            pltpu.VMEM((1024, 2, 8, 128), F32),
            pltpu.VMEM((16, NB, NB), F32),
            pltpu.VMEM((1024, 512), F32),
            pltpu.VMEM((1040, 512), BF16),
            pltpu.VMEM((1040, 512), BF16),
            pltpu.VMEM((4, 512, NB), BF16),
            pltpu.VMEM((4, 512, NB), BF16),
            pltpu.VMEM((2, ROWS, 8, 128), F32),
            pltpu.VMEM((2, 3, NB, NB), BF16),
            pltpu.SemaphoreType.DMA((4,)),
            pltpu.SemaphoreType.DMA((2,)),
            pltpu.SemaphoreType.DMA((2,)),
            pltpu.SemaphoreType.DMA((2,)),
        ],
        name="panels_and_trailing",
        compiler_params=pltpu.CompilerParams(vmem_limit_bytes=40 * 1024 * 1024),
        cost_estimate=SMALL,
    )(place, flat, across, mine, theirs, w00, l10, w11, sums)


def where_is(device):
    row, col = divmod(device, 8)
    return [row // 4, row % 4, col // 2, col % 2]


def device_at(z, y, x, core):
    return ((z % 4) * 4 + y % 4) * 8 + (x % 4) * 2 + core


def moved(device, dim, by):
    at = where_is(device)
    at[dim] += by
    return device_at(*at)


def spread(value, trees, here, beside):
    holders = [[device_at(z, y, 0, c)] for (z, y), c, _ in trees]
    stages = []
    for at in range(3):
        aways = [(here[dims[at]] - (z, y, 0)[dims[at]]) % 4 for (z, y), _, dims in trees]
        away = jnp.where(here[3] == trees[0][1], aways[0], aways[1])
        for half in range(2):
            pairs = []
            for held, (_, _, dims) in zip(holders, trees):
                dim = dims[at]
                if half == 0:
                    pairs += [(h, moved(h, dim, 1)) for h in held]
                else:
                    pairs += [(h, moved(h, dim, -1)) for h in held] + [(moved(h, dim, 1), moved(h, dim, 2)) for h in held]
            if stages:
                value = beside(len(stages), value)
            arrived = lax.ppermute(value, ("row", "col"), pairs)
            value = jnp.where((away == 1) if half == 0 else (away >= 2), arrived, value)
            stages.append(value)
        holders = [[moved(h, dims[at], k) for h in held for k in range(4)] for held, (_, _, dims) in zip(holders, trees)]
    return stages


def after(value, token):
    return lax.optimization_barrier((value, token))[0]


def shards(covariance, check_weights):
    row = lax.axis_index("row")
    col = lax.axis_index("col")
    core = col % 2
    x = col // 2
    here = [row // 4, row % 4, x, core]
    flat = pltpu.with_memory_space_constraint(covariance.reshape(1024, 16, 128), pltpu.HBM)
    tiles = jnp.arange(4, dtype=jnp.int32) * 16 + row
    weights = jnp.where((tiles >= 2)[:, None], check_weights.reshape(4, NB), 0.0).reshape(1024)
    place = jnp.stack([row, col]).astype(jnp.int32)
    swap_cores = [(c, c ^ 1) for c in range(8)]

    pieces = corner_call(flat)
    fetched = lax.ppermute(pieces[0], ("row", "col"), [(8, 0), (9, 1)])
    corner = jnp.where(
        core == 0,
        jnp.concatenate([pieces[0], fetched[0:128]], axis=0),
        jnp.concatenate([fetched, pieces[9]], axis=0),
    )
    column, sums = column_call(weights, after(flat, corner))
    partial = [sums]

    def beside(stage, value):
        before = partial[-1]
        if stage <= 4:
            d = (1, 3, 4, 12)[stage - 1]
            partial.append(before + lax.ppermute(after(before, value), "row", [(r, r ^ d) for r in range(16)]))
        return after(value, before)

    tree = spread(corner, [((0, 0), 0, (2, 1, 0)), ((0, 0), 1, (0, 2, 1))], here, beside)
    sums = partial[-1]
    own = tree[-1]
    other = lax.ppermute(own, "col", swap_cores)

    piece = pieces[8]
    for j in range(1, 8):
        piece = jnp.where(row // 2 == j, lax.ppermute(pieces[j] if j < 4 else after(pieces[j], fetched), "row", [(0, 2 * j), (1, 2 * j + 1)]), piece)
    across = lax.all_gather(after(piece, (tree[0], column)), "row", axis=0)
    across = pltpu.with_memory_space_constraint(across, pltpu.HBM)

    near_sums = jnp.broadcast_to(sums[0:2].reshape(1, NB), (16, NB))
    far_sums = [lax.ppermute(near_sums, "col", [(0, 2 * k), (1, 2 * k + 1)]) for k in (1, 2, 3)]
    w00 = first_factor(place, own, other)
    far_sums = after(far_sums, w00)
    panel_sums = near_sums
    for k in (1, 2, 3):
        panel_sums = jnp.where(x == k, far_sums[k - 1], panel_sums)

    l10, w11 = second_factor(place, w00, own, other)
    from_left = lax.ppermute(column, "col", [(0, 2), (1, 3)])
    from_right = lax.ppermute(column, "col", [(0, 6), (1, 7)])
    from_left, from_right = after((from_left, from_right), tree[5])
    mine = jnp.where(x == 1, from_left, jnp.where(x == 3, from_right, column))
    upper = lax.ppermute(mine[0:512], "col", [(2, 4), (3, 5)])
    lower = lax.ppermute(mine[512:1024], "col", [(6, 4), (7, 5)])
    upper, lower = after((upper, lower), w00)
    upper = jnp.where(x == 2, upper, mine[0:512])
    lower = jnp.where(x == 2, lower, mine[512:1024])
    mine = jnp.concatenate([upper, lower, panel_sums], axis=0)
    theirs = after(lax.ppermute(mine, "col", swap_cores), w11)

    grouped = pltpu.with_memory_space_constraint(covariance.reshape(1024, 2, 8, 128), pltpu.HBM)
    trailing, panels, checksum = final_call(place, grouped, across, mine, theirs, w00, l10, w11, sums)
    return (
        trailing.reshape(4, 1, NB, 8, 1, NB),
        panels.reshape(4, 1, NB, 512),
        checksum.reshape(8, 1, NB),
    )


def solution(mesh):
    in_specs = (P(None, "row", None, None, "col", None), P(None, "row", None))
    out_specs = (
        P(None, "row", None, None, "col", None),
        P(None, "row", None, None),
        P(None, "col", None),
    )
    return jax.shard_map(shards, mesh=mesh, in_specs=in_specs, out_specs=out_specs, check_vma=False)
```

```python
import functools

import jax
import jax.numpy as jnp
from jax import lax
from jax.experimental import pallas as pl
from jax.experimental.pallas import tpu as pltpu
from jax.sharding import PartitionSpec as P

HIGHEST = lax.Precision.HIGHEST
F32 = jnp.float32
BF16 = jnp.bfloat16
NB = 256
NT = (((1,), (1,)), ((), ()))
NN = (((1,), (0,)), ((), ()))


def dot6(a, b, dims):
    return lax.dot_general(a, b, dims, precision=HIGHEST, preferred_element_type=F32)


def halves(value):
    high = value.astype(BF16)
    return high, (value - high.astype(F32)).astype(BF16)


def dot3(a, b, dims):
    total = lax.dot_general(a[0], b[0], dims, preferred_element_type=F32)
    total += lax.dot_general(a[0], b[1], dims, preferred_element_type=F32)
    return total + lax.dot_general(a[1], b[0], dims, preferred_element_type=F32)


def splat_row(ref, row, lanes):
    return jnp.broadcast_to(ref[row : row + 1, lanes], (8, 128))


def splat_lane(value, lane):
    return jnp.broadcast_to(value[:, lane : lane + 1], (8, 128))


def invert_factor(m, put):
    left, right = slice(0, 128), slice(128, 256)
    for block in range(16):
        base = 8 * block
        rows = [[splat_row(m, base + a, side) for a in range(8)] for side in (left, right)]
        b = {(a, k): splat_lane(rows[0][a], base + k) for a in range(8) for k in range(a + 1)}
        n = {}
        inverse, root = [], []
        for i in range(8):
            inverse.append(1.0 / b[i, i])
            root.append(lax.rsqrt(b[i, i]))
            for k in range(i + 1, 8):
                ratio = b[k, i] * inverse[i]
                for j in range(i + 1, k + 1):
                    b[k, j] = b[k, j] - ratio * b[j, i]
                for j in range(i):
                    n[k, j] = n[k, j] - ratio * n[i, j]
                n[k, i] = -ratio
        solved = []
        for side in range(2):
            upper = []
            for i in range(8):
                value = rows[side][i]
                for j in range(i):
                    value = value + n[i, j] * rows[side][j]
                upper.append(value)
            if side == 1:
                for i in range(8):
                    put(base + i, root[i] * upper[i])
            scaled = [inverse[i] * upper[i] for i in range(8)]
            out = []
            for i in range(8):
                value = scaled[i]
                for k in range(i + 1, 8):
                    value = value + n[k, i] * scaled[k]
                out.append(value)
            solved.append(out)
        for other in range(block + 1, 16):
            span = slice(8 * other, 8 * other + 8)
            a_part, n_part = m[span, left], m[span, right]
            columns = [splat_lane(a_part, base + i) for i in range(8)]
            for i in range(8):
                a_part = a_part - columns[i] * solved[0][i]
                n_part = n_part - columns[i] * solved[1][i]
            m[span, left] = a_part
            m[span, right] = n_part


def factor_tile(source, out, m, part):
    eye = (lax.broadcasted_iota(jnp.int32, (128, 128), 0) == lax.broadcasted_iota(jnp.int32, (128, 128), 1)).astype(F32)
    m[:, 0:128] = source[0:128, 0:128]

    def body(i, carry):
        m[:, 128:256] = eye

        def put(row, value):
            part[i, row : row + 1, :] = value[0:1, :]

        invert_factor(m, put)

        @pl.when(i == 0)
        def _():
            low = dot6(source[128:256, 0:128], part[0], NT)
            m[:, 0:128] = source[128:256, 128:256] - dot6(low, low, NT)
            part[2] = low

        return carry

    lax.fori_loop(0, 2, body, 0)
    out[0:128, 0:128] = part[0]
    out[0:128, 128:256] = jnp.zeros((128, 128), F32)
    out[128:256, 128:256] = part[1]
    out[128:256, 0:128] = -dot6(part[1], dot6(part[2], part[0], NN), NN)


def first_kernel(place, own, other, w00, tile, m, part):
    tile[...] = jnp.where(place[1] % 2 == 0, own[0:NB], other[0:NB])
    factor_tile(tile, w00, m, part)


def second_kernel(place, w00, own, other, l10, w11, schur, m, part):
    even = place[1] % 2 == 0
    top, bottom = own[NB : NB + 128], other[NB : NB + 128]
    c10 = jnp.concatenate([jnp.where(even, top, bottom), jnp.where(even, bottom, top)], axis=0)
    low = dot6(c10, w00[...], NT)
    l10[...] = low
    schur[...] = jnp.where(even, other[0:NB], own[0:NB]) - dot6(low, low, NT)
    factor_tile(schur, w11, m, part)


TILE = jax.ShapeDtypeStruct((NB, NB), F32)
WORK = [pltpu.VMEM((128, 256), F32), pltpu.VMEM((3, 128, 128), F32)]
VMEM = pl.BlockSpec(memory_space=pltpu.VMEM)
SMEM = pl.BlockSpec(memory_space=pltpu.SMEM)


LIMIT = 24 * 1024 * 1024
SMALL = pl.CostEstimate(flops=100_000_000, bytes_accessed=100_000, transcendentals=0)
FACTOR = dict(compiler_params=pltpu.CompilerParams(vmem_limit_bytes=LIMIT), cost_estimate=SMALL)
TILE_WORK = [pltpu.VMEM((NB, NB), F32)] + WORK


def first_factor(place, own, other):
    return pl.pallas_call(
        first_kernel, out_shape=TILE, in_specs=[SMEM, VMEM, VMEM], out_specs=VMEM,
        scratch_shapes=TILE_WORK, name="first_factor", **FACTOR,
    )(place, own, other)


def second_factor(place, w00, own, other):
    return pl.pallas_call(
        second_kernel, out_shape=(TILE, TILE), in_specs=[SMEM, VMEM, VMEM, VMEM], out_specs=(VMEM, VMEM),
        scratch_shapes=TILE_WORK, name="second_factor", **FACTOR,
    )(place, w00, own, other)


def corner_kernel(a, *pieces):
    *pieces, flipped = pieces
    flipped[...] = a[:, 1, :].T
    for q in range(16):
        value = a[:, q, :]
        for ref in pieces[q // 2 :: 8]:
            ref[:, 128 * (q % 2) : 128 * (q % 2) + 128] = value


def corner_call(flat):
    return pl.pallas_call(
        corner_kernel, grid=(2,), out_shape=(TILE,) * 9 + (jax.ShapeDtypeStruct((128, NB), F32),),
        in_specs=[pl.BlockSpec((128, 16, 128), lambda i: (i, 0, 0))],
        out_specs=(pl.BlockSpec((128, NB), lambda i: (i, 0)),) * 9 + (pl.BlockSpec((128, 128), lambda i: (0, i)),),
        name="corner_tiles",
    )(flat)


def column_kernel(weights, a, column, sums):
    step = pl.program_id(0)
    for q in range(2):
        column[:, 128 * q : 128 * q + 128] = a[:, q, :]

    @pl.when(step == 0)
    def _():
        sums[...] = jnp.zeros_like(sums)

    def body(i, total):
        for j in range(8):
            row = 8 * i + j
            total = total + weights[step * 128 + row] * a[row]
        return total

    sums[...] += lax.fori_loop(0, 16, body, jnp.zeros((16, 128), F32))


def column_call(weights, flat):
    return pl.pallas_call(
        column_kernel, grid=(8,),
        out_shape=(jax.ShapeDtypeStruct((1024, NB), F32), jax.ShapeDtypeStruct((16, 128), F32)),
        in_specs=[SMEM, pl.BlockSpec((128, 16, 128), lambda i: (i, 0, 0))],
        out_specs=(
            pl.BlockSpec((128, NB), lambda i: (i, 0)),
            pl.BlockSpec((16, 128), lambda i: (0, 0)),
        ),
        name="first_column", **FACTOR,
    )(weights, flat)


ROWS = 256


def final_kernel(
    place, flat, across, mine, theirs, w00, l10, w11, sums, out, panels, checksum,
    block, right, solved, high, low, right_high, right_low, ready, factors, block_sem, right_sem, panel_sem, out_sem,
):
    row_index, col_index = place[0], place[1]
    even = col_index % 2 == 0
    blocks = [
        pltpu.make_async_copy(flat.at[pl.ds(ROWS * i, ROWS)], block.at[pl.ds(ROWS * i, ROWS)], block_sem.at[i]) for i in range(4)
    ]
    rights = [pltpu.make_async_copy(across.at[pl.ds(8 * i, 8)], right.at[pl.ds(8 * i, 8)], right_sem.at[i]) for i in range(2)]
    for copy in (rights[0], *blocks, rights[1]):
        copy.start()

    for k, ref in enumerate((w00, l10, w11)):
        factors[0, k], factors[1, k] = halves(ref[...])
    f00, f10, f11 = [(factors[0, k], factors[1, k]) for k in range(3)]
    solves = []
    for half in range(2):
        rows = slice(512 * half, 512 * half + 512 + 16 * half)
        first = jnp.where(even, mine[rows], theirs[rows])
        second = jnp.where(even, theirs[rows], mine[rows])
        left = dot3(halves(first), f00, NT)
        bottom = dot3(halves(second - dot3(halves(left), f10, NT)), f11, NT)
        solved[512 * half : 512 * half + 512, 0:256] = left[0:512]
        if half == 0:
            top = (row_index == 0) & (lax.broadcasted_iota(jnp.int32, (512, 1), 0) < NB)
            solved[0:512, 256:512] = jnp.where(top, 0.0, bottom)
        else:
            solved[512:1024, 256:512] = bottom[0:512]
        copy = pltpu.make_async_copy(
            solved.at[pl.ds(512 * half, 512)], panels.at[pl.ds(512 * half, 512)], panel_sem.at[half]
        )
        copy.start()
        solves.append(copy)
        last = halves(dot3(halves(bottom), f11, NN))
        high[rows, 256:512], low[rows, 256:512] = last
        high[rows, 0:256], low[rows, 0:256] = halves(dot3(halves(left - dot3(last, f10, NN)), f00, NN))

    def put(slot, group, step):
        return pltpu.make_async_copy(
            ready.at[slot], out.at[pl.ds(pl.multiple_of(step * ROWS, ROWS), ROWS), group], out_sem.at[slot]
        )

    for group in range(2):
        rights[group].wait()
        for u in range(4):
            for h in range(2):
                span = slice(NB * h, NB * h + NB)
                right_high[u, span], right_low[u, span] = halves(right[8 * group + 2 * u + h])

        def body(step, carry, group=group):
            slot = step % 2
            base = pl.multiple_of(step * ROWS, ROWS)
            if group == 0:
                for i in range(4):

                    @pl.when(step == i)
                    def _(i=i):
                        blocks[i].wait()

            @pl.when(step + 4 * group >= 2)
            def _():
                put(slot, group, step).wait()

            g_high = jnp.concatenate([high[pl.ds(base, ROWS), :], high[1024:1040, :]], axis=0)
            g_low = jnp.concatenate([low[pl.ds(base, ROWS), :], low[1024:1040, :]], axis=0)
            top = (step * ROWS + lax.broadcasted_iota(jnp.int32, (ROWS, 1), 0) < NB) & (row_index < 2)
            for u in range(4):
                product = dot3((g_high, g_low), (right_high[u], right_low[u]), NN)
                gone = top | (col_index < 2) if (group, u) == (0, 0) else top
                for h in range(2):
                    q = 2 * u + h
                    lanes = slice(128 * h, 128 * h + 128)
                    value = block[pl.ds(base, ROWS), group, q, :] - product[0:ROWS, lanes]
                    ready[slot, :, q, :] = jnp.where(gone, 0.0, value)
                    at = 8 * group + q
                    kept = sums[at : at + 1, :] - product[ROWS : ROWS + 1, lanes]
                    if (group, u) == (0, 0):
                        kept = jnp.where(col_index < 2, 0.0, kept)
                    checksum[at : at + 1, :] = kept
            put(slot, group, step).start()
            return carry

        lax.fori_loop(0, 4, body, 0)
    for slot in range(2):
        put(slot, 1, 2 + slot).wait()
    for copy in solves:
        copy.wait()


def final_call(place, flat, across, mine, theirs, w00, l10, w11, sums):
    hbm = pl.BlockSpec(memory_space=pl.ANY)
    return pl.pallas_call(
        final_kernel,
        out_shape=(
            jax.ShapeDtypeStruct((1024, 2, 8, 128), F32),
            jax.ShapeDtypeStruct((1024, 512), F32),
            jax.ShapeDtypeStruct((16, 128), F32),
        ),
        in_specs=[SMEM, hbm, hbm] + [VMEM] * 6,
        out_specs=(hbm, hbm, VMEM),
        scratch_shapes=[
            pltpu.VMEM((1024, 2, 8, 128), F32),
            pltpu.VMEM((16, NB, NB), F32),
            pltpu.VMEM((1024, 512), F32),
            pltpu.VMEM((1040, 512), BF16),
            pltpu.VMEM((1040, 512), BF16),
            pltpu.VMEM((4, 512, NB), BF16),
            pltpu.VMEM((4, 512, NB), BF16),
            pltpu.VMEM((2, ROWS, 8, 128), F32),
            pltpu.VMEM((2, 3, NB, NB), BF16),
            pltpu.SemaphoreType.DMA((4,)),
            pltpu.SemaphoreType.DMA((2,)),
            pltpu.SemaphoreType.DMA((2,)),
            pltpu.SemaphoreType.DMA((2,)),
        ],
        name="panels_and_trailing",
        compiler_params=pltpu.CompilerParams(vmem_limit_bytes=40 * 1024 * 1024),
        cost_estimate=SMALL,
    )(place, flat, across, mine, theirs, w00, l10, w11, sums)


def where_is(device):
    row, col = divmod(device, 8)
    return [row // 4, row % 4, col // 2, col % 2]


def device_at(z, y, x, core):
    return ((z % 4) * 4 + y % 4) * 8 + (x % 4) * 2 + core


def moved(device, dim, by):
    at = where_is(device)
    at[dim] += by
    return device_at(*at)


def spread(value, trees, here, beside):
    holders = [[device_at(z, y, 0, c)] for (z, y), c, _ in trees]
    stages = []
    for at in range(3):
        aways = [(here[dims[at]] - (z, y, 0)[dims[at]]) % 4 for (z, y), _, dims in trees]
        away = jnp.where(here[3] == trees[0][1], aways[0], aways[1])
        for half in range(2):
            pairs = []
            for held, (_, _, dims) in zip(holders, trees):
                dim = dims[at]
                if half == 0:
                    pairs += [(h, moved(h, dim, 1)) for h in held]
                else:
                    pairs += [(h, moved(h, dim, -1)) for h in held] + [(moved(h, dim, 1), moved(h, dim, 2)) for h in held]
            if stages:
                value = beside(len(stages), value)
            arrived = lax.ppermute(value, ("row", "col"), pairs)
            value = jnp.where((away == 1) if half == 0 else (away >= 2), arrived, value)
            stages.append(value)
        holders = [[moved(h, dims[at], k) for h in held for k in range(4)] for held, (_, _, dims) in zip(holders, trees)]
    return stages


def after(value, token):
    return lax.optimization_barrier((value, token))[0]


def shards(covariance, check_weights):
    row = lax.axis_index("row")
    col = lax.axis_index("col")
    core = col % 2
    x = col // 2
    here = [row // 4, row % 4, x, core]
    flat = pltpu.with_memory_space_constraint(covariance.reshape(1024, 16, 128), pltpu.HBM)
    tiles = jnp.arange(4, dtype=jnp.int32) * 16 + row
    weights = jnp.where((tiles >= 2)[:, None], check_weights.reshape(4, NB), 0.0).reshape(1024)
    place = jnp.stack([row, col]).astype(jnp.int32)
    swap_cores = [(c, c ^ 1) for c in range(8)]

    pieces = corner_call(flat)
    fetched = lax.ppermute(pieces[0], ("row", "col"), [(8, 0), (9, 1)])
    corner = jnp.where(
        core == 0,
        jnp.concatenate([pieces[0], fetched[0:128]], axis=0),
        jnp.concatenate([fetched, pieces[9]], axis=0),
    )
    column, sums = column_call(weights, after(flat, corner))
    partial = [sums]
    from_left = lax.ppermute(column, "col", [(0, 2), (1, 3)])
    from_right = lax.ppermute(column, "col", [(0, 6), (1, 7)])

    def beside(stage, value):
        before = partial[-1]
        if stage <= 4:
            d = (1, 3, 4, 12)[stage - 1]
            partial.append(before + lax.ppermute(after(before, value), "row", [(r, r ^ d) for r in range(16)]))
        return after(value, (before, from_left, from_right) if stage == 4 else before)

    tree = spread(corner, [((0, 0), 0, (2, 1, 0)), ((0, 0), 1, (1, 0, 2))], here, beside)
    sums = partial[-1]
    near_sums = jnp.broadcast_to(sums[0:2].reshape(1, NB), (16, NB))
    far_sums = [lax.ppermute(near_sums, "col", [(0, 2 * k), (1, 2 * k + 1)]) for k in (1, 2, 3)]
    own, far_sums = lax.optimization_barrier((tree[-1], far_sums))
    other = lax.ppermute(own, "col", swap_cores)

    piece = pieces[8]
    for j in range(1, 8):
        piece = jnp.where(row // 2 == j, lax.ppermute(pieces[j] if j < 4 else after(pieces[j], fetched), "row", [(0, 2 * j), (1, 2 * j + 1)]), piece)
    across = lax.all_gather(after(piece, (tree[0], column)), "row", axis=0)
    across = pltpu.with_memory_space_constraint(across, pltpu.HBM)

    w00 = first_factor(place, own, other)
    panel_sums = near_sums
    for k in (1, 2, 3):
        panel_sums = jnp.where(x == k, far_sums[k - 1], panel_sums)

    l10, w11 = second_factor(place, w00, own, other)
    mine = jnp.where(x == 1, from_left, jnp.where(x == 3, from_right, column))
    mine = after(mine, own)
    upper = lax.ppermute(mine[0:512], "col", [(2, 4), (3, 5)])
    lower = lax.ppermute(mine[512:1024], "col", [(6, 4), (7, 5)])
    upper, lower = after((upper, lower), w00)
    upper = jnp.where(x == 2, upper, mine[0:512])
    lower = jnp.where(x == 2, lower, mine[512:1024])
    mine = jnp.concatenate([upper, lower, panel_sums], axis=0)
    theirs = after(lax.ppermute(mine, "col", swap_cores), w11)

    grouped = pltpu.with_memory_space_constraint(covariance.reshape(1024, 2, 8, 128), pltpu.HBM)
    trailing, panels, checksum = final_call(place, grouped, across, mine, theirs, w00, l10, w11, sums)
    return (
        trailing.reshape(4, 1, NB, 8, 1, NB),
        panels.reshape(4, 1, NB, 512),
        checksum.reshape(8, 1, NB),
    )


def solution(mesh):
    in_specs = (P(None, "row", None, None, "col", None), P(None, "row", None))
    out_specs = (
        P(None, "row", None, None, "col", None),
        P(None, "row", None, None),
        P(None, "col", None),
    )
    return jax.shard_map(shards, mesh=mesh, in_specs=in_specs, out_specs=out_specs, check_vma=False)
```

```python
import functools

import jax
import jax.numpy as jnp
from jax import lax
from jax.experimental import pallas as pl
from jax.experimental.pallas import tpu as pltpu
from jax.sharding import PartitionSpec as P

HIGHEST = lax.Precision.HIGHEST
F32 = jnp.float32
BF16 = jnp.bfloat16
NB = 256
NT = (((1,), (1,)), ((), ()))
NN = (((1,), (0,)), ((), ()))


def dot6(a, b, dims):
    return lax.dot_general(a, b, dims, precision=HIGHEST, preferred_element_type=F32)


def halves(value):
    high = value.astype(BF16)
    return high, (value - high.astype(F32)).astype(BF16)


def dot3(a, b, dims):
    total = lax.dot_general(a[0], b[0], dims, preferred_element_type=F32)
    total += lax.dot_general(a[0], b[1], dims, preferred_element_type=F32)
    return total + lax.dot_general(a[1], b[0], dims, preferred_element_type=F32)


def splat_row(ref, row, lanes):
    return jnp.broadcast_to(ref[row : row + 1, lanes], (8, 128))


def splat_lane(value, lane):
    return jnp.broadcast_to(value[:, lane : lane + 1], (8, 128))


def invert_factor(m, put):
    left, right = slice(0, 128), slice(128, 256)
    for block in range(16):
        base = 8 * block
        rows = [[splat_row(m, base + a, side) for a in range(8)] for side in (left, right)]
        b = {(a, k): splat_lane(rows[0][a], base + k) for a in range(8) for k in range(a + 1)}
        n = {}
        inverse, root = [], []
        for i in range(8):
            inverse.append(1.0 / b[i, i])
            root.append(lax.rsqrt(b[i, i]))
            for k in range(i + 1, 8):
                ratio = b[k, i] * inverse[i]
                for j in range(i + 1, k + 1):
                    b[k, j] = b[k, j] - ratio * b[j, i]
                for j in range(i):
                    n[k, j] = n[k, j] - ratio * n[i, j]
                n[k, i] = -ratio
        solved = []
        for side in range(2):
            upper = []
            for i in range(8):
                value = rows[side][i]
                for j in range(i):
                    value = value + n[i, j] * rows[side][j]
                upper.append(value)
            if side == 1:
                for i in range(8):
                    put(base + i, root[i] * upper[i])
            scaled = [inverse[i] * upper[i] for i in range(8)]
            out = []
            for i in range(8):
                value = scaled[i]
                for k in range(i + 1, 8):
                    value = value + n[k, i] * scaled[k]
                out.append(value)
            solved.append(out)
        for other in range(block + 1, 16):
            span = slice(8 * other, 8 * other + 8)
            a_part, n_part = m[span, left], m[span, right]
            columns = [splat_lane(a_part, base + i) for i in range(8)]
            for i in range(8):
                a_part = a_part - columns[i] * solved[0][i]
                n_part = n_part - columns[i] * solved[1][i]
            m[span, left] = a_part
            m[span, right] = n_part


def factor_tile(source, out, m, part):
    eye = (lax.broadcasted_iota(jnp.int32, (128, 128), 0) == lax.broadcasted_iota(jnp.int32, (128, 128), 1)).astype(F32)
    m[:, 0:128] = source[0:128, 0:128]

    def body(i, carry):
        m[:, 128:256] = eye

        def put(row, value):
            part[i, row : row + 1, :] = value[0:1, :]

        invert_factor(m, put)

        @pl.when(i == 0)
        def _():
            low = dot6(source[128:256, 0:128], part[0], NT)
            m[:, 0:128] = source[128:256, 128:256] - dot6(low, low, NT)
            part[2] = low

        return carry

    lax.fori_loop(0, 2, body, 0)
    out[0:128, 0:128] = part[0]
    out[0:128, 128:256] = jnp.zeros((128, 128), F32)
    out[128:256, 128:256] = part[1]
    out[128:256, 0:128] = -dot6(part[1], dot6(part[2], part[0], NN), NN)


def first_kernel(place, own, other, w00, tile, m, part):
    tile[...] = jnp.where(place[1] % 2 == 0, own[0:NB], other[0:NB])
    factor_tile(tile, w00, m, part)


def second_kernel(place, w00, own, other, l10, w11, schur, m, part):
    even = place[1] % 2 == 0
    top, bottom = own[NB : NB + 128], other[NB : NB + 128]
    c10 = jnp.concatenate([jnp.where(even, top, bottom), jnp.where(even, bottom, top)], axis=0)
    low = dot6(c10, w00[...], NT)
    l10[...] = low
    schur[...] = jnp.where(even, other[0:NB], own[0:NB]) - dot6(low, low, NT)
    factor_tile(schur, w11, m, part)


TILE = jax.ShapeDtypeStruct((NB, NB), F32)
WORK = [pltpu.VMEM((128, 256), F32), pltpu.VMEM((3, 128, 128), F32)]
VMEM = pl.BlockSpec(memory_space=pltpu.VMEM)
SMEM = pl.BlockSpec(memory_space=pltpu.SMEM)


LIMIT = 24 * 1024 * 1024
SMALL = pl.CostEstimate(flops=100_000_000, bytes_accessed=100_000, transcendentals=0)
FACTOR = dict(compiler_params=pltpu.CompilerParams(vmem_limit_bytes=LIMIT), cost_estimate=SMALL)
TILE_WORK = [pltpu.VMEM((NB, NB), F32)] + WORK


def first_factor(place, own, other):
    return pl.pallas_call(
        first_kernel, out_shape=TILE, in_specs=[SMEM, VMEM, VMEM], out_specs=VMEM,
        scratch_shapes=TILE_WORK, name="first_factor", **FACTOR,
    )(place, own, other)


def second_factor(place, w00, own, other):
    return pl.pallas_call(
        second_kernel, out_shape=(TILE, TILE), in_specs=[SMEM, VMEM, VMEM, VMEM], out_specs=(VMEM, VMEM),
        scratch_shapes=TILE_WORK, name="second_factor", **FACTOR,
    )(place, w00, own, other)


def corner_kernel(near, far, column, *pieces):
    *pieces, flipped = pieces
    for q in range(2):
        column[:, 128 * q : 128 * q + 128] = near[:, q, :]

    @pl.when(pl.program_id(0) == 0)
    def _():
        flipped[...] = near[:, 1, :].T
        for q in range(16):
            value = (near, far)[q // 8][:, q % 8, :]
            for ref in pieces[q // 2 :: 8]:
                ref[:, 128 * (q % 2) : 128 * (q % 2) + 128] = value


def corner_call(flat):
    whole = pl.BlockSpec((NB, NB), lambda i: (0, 0))
    return pl.pallas_call(
        corner_kernel, grid=(4,),
        out_shape=(jax.ShapeDtypeStruct((1024, NB), F32),) + (TILE,) * 9 + (jax.ShapeDtypeStruct((128, NB), F32),),
        in_specs=[pl.BlockSpec((NB, 8, 128), lambda i: (i, 0, 0)), pl.BlockSpec((NB, 8, 128), lambda i: (0, 1, 0))],
        out_specs=(pl.BlockSpec((NB, NB), lambda i: (i, 0)),) + (whole,) * 9 + (pl.BlockSpec((128, NB), lambda i: (0, 0)),),
        name="corner_tiles", **FACTOR,
    )(flat, flat)


def sums_kernel(weights, a, sums):
    step = pl.program_id(0)

    @pl.when(step == 0)
    def _():
        sums[...] = jnp.zeros_like(sums)

    def body(i, total):
        for j in range(8):
            row = 8 * i + j
            total = total + weights[step * 128 + row] * a[row]
        return total

    sums[...] += lax.fori_loop(0, 16, body, jnp.zeros((16, 128), F32))


def sums_call(weights, flat):
    return pl.pallas_call(
        sums_kernel, grid=(8,), out_shape=jax.ShapeDtypeStruct((16, 128), F32),
        in_specs=[SMEM, pl.BlockSpec((128, 16, 128), lambda i: (i, 0, 0))],
        out_specs=pl.BlockSpec((16, 128), lambda i: (0, 0)),
        name="column_sums", **FACTOR,
    )(weights, flat)


ROWS = 256


def final_kernel(
    place, flat, across, mine, theirs, w00, l10, w11, sums, out, panels, checksum,
    block, right, solved, high, low, right_high, right_low, ready, factors, block_sem, right_sem, panel_sem, out_sem,
):
    row_index, col_index = place[0], place[1]
    even = col_index % 2 == 0
    blocks = [
        pltpu.make_async_copy(flat.at[pl.ds(ROWS * i, ROWS)], block.at[pl.ds(ROWS * i, ROWS)], block_sem.at[i]) for i in range(4)
    ]
    rights = [pltpu.make_async_copy(across.at[pl.ds(8 * i, 8)], right.at[pl.ds(8 * i, 8)], right_sem.at[i]) for i in range(2)]
    for copy in (rights[0], *blocks, rights[1]):
        copy.start()

    for k, ref in enumerate((w00, l10, w11)):
        factors[0, k], factors[1, k] = halves(ref[...])
    f00, f10, f11 = [(factors[0, k], factors[1, k]) for k in range(3)]
    solves = []
    for half in range(2):
        rows = slice(512 * half, 512 * half + 512 + 16 * half)
        first = jnp.where(even, mine[rows], theirs[rows])
        second = jnp.where(even, theirs[rows], mine[rows])
        left = dot3(halves(first), f00, NT)
        bottom = dot3(halves(second - dot3(halves(left), f10, NT)), f11, NT)
        solved[512 * half : 512 * half + 512, 0:256] = left[0:512]
        if half == 0:
            top = (row_index == 0) & (lax.broadcasted_iota(jnp.int32, (512, 1), 0) < NB)
            solved[0:512, 256:512] = jnp.where(top, 0.0, bottom)
        else:
            solved[512:1024, 256:512] = bottom[0:512]
        copy = pltpu.make_async_copy(
            solved.at[pl.ds(512 * half, 512)], panels.at[pl.ds(512 * half, 512)], panel_sem.at[half]
        )
        copy.start()
        solves.append(copy)
        last = halves(dot3(halves(bottom), f11, NN))
        high[rows, 256:512], low[rows, 256:512] = last
        high[rows, 0:256], low[rows, 0:256] = halves(dot3(halves(left - dot3(last, f10, NN)), f00, NN))

    def put(slot, group, step):
        return pltpu.make_async_copy(
            ready.at[slot], out.at[pl.ds(pl.multiple_of(step * ROWS, ROWS), ROWS), group], out_sem.at[slot]
        )

    for group in range(2):
        rights[group].wait()
        for u in range(4):
            for h in range(2):
                span = slice(NB * h, NB * h + NB)
                right_high[u, span], right_low[u, span] = halves(right[8 * group + 2 * u + h])

        def body(step, carry, group=group):
            slot = step % 2
            base = pl.multiple_of(step * ROWS, ROWS)
            if group == 0:
                for i in range(4):

                    @pl.when(step == i)
                    def _(i=i):
                        blocks[i].wait()

            @pl.when(step + 4 * group >= 2)
            def _():
                put(slot, group, step).wait()

            g_high = jnp.concatenate([high[pl.ds(base, ROWS), :], high[1024:1040, :]], axis=0)
            g_low = jnp.concatenate([low[pl.ds(base, ROWS), :], low[1024:1040, :]], axis=0)
            for u in range(4):
                product = dot3((g_high, g_low), (right_high[u], right_low[u]), NN)
                for h in range(2):
                    q = 2 * u + h
                    lanes = slice(128 * h, 128 * h + 128)
                    ready[slot, :, q, :] = block[pl.ds(base, ROWS), group, q, :] - product[0:ROWS, lanes]
                    at = 8 * group + q
                    kept = sums[at : at + 1, :] - product[ROWS : ROWS + 1, lanes]
                    if (group, u) == (0, 0):
                        kept = jnp.where(col_index < 2, 0.0, kept)
                    checksum[at : at + 1, :] = kept
            @pl.when((step == 0) & (row_index < 2))
            def _():
                ready[slot] = jnp.zeros((ROWS, 8, 128), F32)

            if group == 0:

                @pl.when(col_index < 2)
                def _():
                    ready[slot, :, 0:2, :] = jnp.zeros((ROWS, 2, 128), F32)

            put(slot, group, step).start()
            return carry

        lax.fori_loop(0, 4, body, 0)
    for slot in range(2):
        put(slot, 1, 2 + slot).wait()
    for copy in solves:
        copy.wait()


def final_call(place, flat, across, mine, theirs, w00, l10, w11, sums):
    hbm = pl.BlockSpec(memory_space=pl.ANY)
    return pl.pallas_call(
        final_kernel,
        out_shape=(
            jax.ShapeDtypeStruct((1024, 2, 8, 128), F32),
            jax.ShapeDtypeStruct((1024, 512), F32),
            jax.ShapeDtypeStruct((16, 128), F32),
        ),
        in_specs=[SMEM, hbm, hbm] + [VMEM] * 6,
        out_specs=(hbm, hbm, VMEM),
        scratch_shapes=[
            pltpu.VMEM((1024, 2, 8, 128), F32),
            pltpu.VMEM((16, NB, NB), F32),
            pltpu.VMEM((1024, 512), F32),
            pltpu.VMEM((1040, 512), BF16),
            pltpu.VMEM((1040, 512), BF16),
            pltpu.VMEM((4, 512, NB), BF16),
            pltpu.VMEM((4, 512, NB), BF16),
            pltpu.VMEM((2, ROWS, 8, 128), F32),
            pltpu.VMEM((2, 3, NB, NB), BF16),
            pltpu.SemaphoreType.DMA((4,)),
            pltpu.SemaphoreType.DMA((2,)),
            pltpu.SemaphoreType.DMA((2,)),
            pltpu.SemaphoreType.DMA((2,)),
        ],
        name="panels_and_trailing",
        compiler_params=pltpu.CompilerParams(vmem_limit_bytes=30 * 1024 * 1024),
        cost_estimate=SMALL,
    )(place, flat, across, mine, theirs, w00, l10, w11, sums)


def where_is(device):
    row, col = divmod(device, 8)
    return [row // 4, row % 4, col // 2, col % 2]


def device_at(z, y, x, core):
    return ((z % 4) * 4 + y % 4) * 8 + (x % 4) * 2 + core


def moved(device, dim, by):
    at = where_is(device)
    at[dim] += by
    return device_at(*at)


def spread(value, trees, here, beside):
    holders = [[device_at(z, y, 0, c)] for (z, y), c, _ in trees]
    stages = []
    for at in range(3):
        aways = [(here[dims[at]] - (z, y, 0)[dims[at]]) % 4 for (z, y), _, dims in trees]
        away = jnp.where(here[3] == trees[0][1], aways[0], aways[1])
        for half in range(2):
            pairs = []
            for held, (_, _, dims) in zip(holders, trees):
                dim = dims[at]
                if half == 0:
                    pairs += [(h, moved(h, dim, 1)) for h in held]
                else:
                    pairs += [(h, moved(h, dim, -1)) for h in held] + [(moved(h, dim, 1), moved(h, dim, 2)) for h in held]
            if stages:
                value = beside(len(stages), value)
            arrived = lax.ppermute(value, ("row", "col"), pairs)
            value = jnp.where((away == 1) if half == 0 else (away >= 2), arrived, value)
            stages.append(value)
        holders = [[moved(h, dims[at], k) for h in held for k in range(4)] for held, (_, _, dims) in zip(holders, trees)]
    return stages


def after(value, token):
    return lax.optimization_barrier((value, token))[0]


def shards(covariance, check_weights):
    row = lax.axis_index("row")
    col = lax.axis_index("col")
    core = col % 2
    x = col // 2
    here = [row // 4, row % 4, x, core]
    flat = pltpu.with_memory_space_constraint(covariance.reshape(1024, 16, 128), pltpu.HBM)
    tiles = jnp.arange(4, dtype=jnp.int32) * 16 + row
    weights = jnp.where((tiles >= 2)[:, None], check_weights.reshape(4, NB), 0.0).reshape(1024)
    place = jnp.stack([row, col]).astype(jnp.int32)
    swap_cores = [(c, c ^ 1) for c in range(8)]

    column, *pieces = corner_call(flat)
    fetched = lax.ppermute(pieces[0], ("row", "col"), [(8, 0), (9, 1)])
    corner = jnp.where(
        core == 0,
        jnp.concatenate([pieces[0], fetched[0:128]], axis=0),
        jnp.concatenate([fetched, pieces[9]], axis=0),
    )
    sums = sums_call(weights, after(flat, corner))
    partial = [sums]
    from_left = lax.ppermute(column, "col", [(0, 2), (1, 3)])
    from_right = lax.ppermute(column, "col", [(0, 6), (1, 7)])
    mine = jnp.where(x == 1, from_left, jnp.where(x == 3, from_right, column))
    upper = lax.ppermute(mine[0:512], "col", [(2, 4), (3, 5)])
    lower = lax.ppermute(mine[512:1024], "col", [(6, 4), (7, 5)])

    def beside(stage, value):
        before = partial[-1]
        if stage <= 4:
            d = (1, 3, 4, 12)[stage - 1]
            partial.append(before + lax.ppermute(after(before, value), "row", [(r, r ^ d) for r in range(16)]))
        more = {1: (from_left, from_right), 4: (upper, lower)}.get(stage, ())
        return after(value, (before, *more))

    tree = spread(corner, [((0, 0), 0, (2, 1, 0)), ((0, 0), 1, (1, 0, 2))], here, beside)
    sums = partial[-1]
    near_sums = jnp.broadcast_to(sums[0:2].reshape(1, NB), (16, NB))
    far_sums = [lax.ppermute(near_sums, "col", [(0, 2 * k), (1, 2 * k + 1)]) for k in (1, 2, 3)]
    own, far_sums = lax.optimization_barrier((tree[-1], far_sums))
    other = lax.ppermute(own, "col", swap_cores)

    piece = pieces[8]
    for j in range(1, 8):
        piece = jnp.where(row // 2 == j, lax.ppermute(pieces[j] if j < 4 else after(pieces[j], fetched), "row", [(0, 2 * j), (1, 2 * j + 1)]), piece)
    across = lax.all_gather(after(piece, (tree[0], partial[0], from_left, from_right)), "row", axis=0)
    across = pltpu.with_memory_space_constraint(across, pltpu.HBM)

    w00 = first_factor(place, own, other)
    panel_sums = near_sums
    for k in (1, 2, 3):
        panel_sums = jnp.where(x == k, far_sums[k - 1], panel_sums)

    l10, w11 = second_factor(place, w00, own, other)
    upper = jnp.where(x == 2, upper, mine[0:512])
    lower = jnp.where(x == 2, lower, mine[512:1024])
    mine = jnp.concatenate([upper, lower, panel_sums], axis=0)
    theirs = after(lax.ppermute(mine, "col", swap_cores), w11)

    grouped = pltpu.with_memory_space_constraint(covariance.reshape(1024, 2, 8, 128), pltpu.HBM)
    trailing, panels, checksum = final_call(place, grouped, across, mine, theirs, w00, l10, w11, sums)
    return (
        trailing.reshape(4, 1, NB, 8, 1, NB),
        panels.reshape(4, 1, NB, 512),
        checksum.reshape(8, 1, NB),
    )


def solution(mesh):
    in_specs = (P(None, "row", None, None, "col", None), P(None, "row", None))
    out_specs = (
        P(None, "row", None, None, "col", None),
        P(None, "row", None, None),
        P(None, "col", None),
    )
    return jax.shard_map(shards, mesh=mesh, in_specs=in_specs, out_specs=out_specs, check_vma=False)
```

```python
import functools

import jax
import jax.numpy as jnp
from jax import lax
from jax.experimental import pallas as pl
from jax.experimental.pallas import tpu as pltpu
from jax.sharding import PartitionSpec as P

HIGHEST = lax.Precision.HIGHEST
F32 = jnp.float32
BF16 = jnp.bfloat16
NB = 256
NT = (((1,), (1,)), ((), ()))
NN = (((1,), (0,)), ((), ()))


def dot6(a, b, dims):
    return lax.dot_general(a, b, dims, precision=HIGHEST, preferred_element_type=F32)


def halves(value):
    high = value.astype(BF16)
    return high, (value - high.astype(F32)).astype(BF16)


def dot3(a, b, dims):
    total = lax.dot_general(a[0], b[0], dims, preferred_element_type=F32)
    total += lax.dot_general(a[0], b[1], dims, preferred_element_type=F32)
    return total + lax.dot_general(a[1], b[0], dims, preferred_element_type=F32)


def splat_row(ref, row, lanes):
    return jnp.broadcast_to(ref[row : row + 1, lanes], (8, 128))


def splat_lane(value, lane):
    return jnp.broadcast_to(value[:, lane : lane + 1], (8, 128))


def invert_factor(m, put):
    left, right = slice(0, 128), slice(128, 256)
    for block in range(16):
        base = 8 * block
        rows = [[splat_row(m, base + a, side) for a in range(8)] for side in (left, right)]
        b = {(a, k): splat_lane(rows[0][a], base + k) for a in range(8) for k in range(a + 1)}
        n = {}
        inverse, root = [], []
        for i in range(8):
            inverse.append(1.0 / b[i, i])
            root.append(lax.rsqrt(b[i, i]))
            for k in range(i + 1, 8):
                ratio = b[k, i] * inverse[i]
                for j in range(i + 1, k + 1):
                    b[k, j] = b[k, j] - ratio * b[j, i]
                for j in range(i):
                    n[k, j] = n[k, j] - ratio * n[i, j]
                n[k, i] = -ratio
        solved = []
        for side in range(2):
            upper = []
            for i in range(8):
                value = rows[side][i]
                for j in range(i):
                    value = value + n[i, j] * rows[side][j]
                upper.append(value)
            if side == 1:
                for i in range(8):
                    put(base + i, root[i] * upper[i])
            scaled = [inverse[i] * upper[i] for i in range(8)]
            out = []
            for i in range(8):
                value = scaled[i]
                for k in range(i + 1, 8):
                    value = value + n[k, i] * scaled[k]
                out.append(value)
            solved.append(out)
        for other in range(block + 1, 16):
            span = slice(8 * other, 8 * other + 8)
            a_part, n_part = m[span, left], m[span, right]
            columns = [splat_lane(a_part, base + i) for i in range(8)]
            for i in range(8):
                a_part = a_part - columns[i] * solved[0][i]
                n_part = n_part - columns[i] * solved[1][i]
            m[span, left] = a_part
            m[span, right] = n_part


def factor_tile(source, out, m, part):
    eye = (lax.broadcasted_iota(jnp.int32, (128, 128), 0) == lax.broadcasted_iota(jnp.int32, (128, 128), 1)).astype(F32)
    m[:, 0:128] = source[0:128, 0:128]

    def body(i, carry):
        m[:, 128:256] = eye

        def put(row, value):
            part[i, row : row + 1, :] = value[0:1, :]

        invert_factor(m, put)

        @pl.when(i == 0)
        def _():
            low = dot6(source[128:256, 0:128], part[0], NT)
            m[:, 0:128] = source[128:256, 128:256] - dot6(low, low, NT)
            part[2] = low

        return carry

    lax.fori_loop(0, 2, body, 0)
    out[0:128, 0:128] = part[0]
    out[0:128, 128:256] = jnp.zeros((128, 128), F32)
    out[128:256, 128:256] = part[1]
    out[128:256, 0:128] = -dot6(part[1], dot6(part[2], part[0], NN), NN)


def first_kernel(place, own, other, w00, tile, m, part):
    tile[...] = jnp.where(place[1] % 2 == 0, own[0:NB], other[0:NB])
    factor_tile(tile, w00, m, part)


def second_kernel(place, w00, own, other, l10, w11, schur, m, part):
    even = place[1] % 2 == 0
    top, bottom = own[NB : NB + 128], other[NB : NB + 128]
    c10 = jnp.concatenate([jnp.where(even, top, bottom), jnp.where(even, bottom, top)], axis=0)
    low = dot6(c10, w00[...], NT)
    l10[...] = low
    schur[...] = jnp.where(even, other[0:NB], own[0:NB]) - dot6(low, low, NT)
    factor_tile(schur, w11, m, part)


TILE = jax.ShapeDtypeStruct((NB, NB), F32)
WORK = [pltpu.VMEM((128, 256), F32), pltpu.VMEM((3, 128, 128), F32)]
VMEM = pl.BlockSpec(memory_space=pltpu.VMEM)
SMEM = pl.BlockSpec(memory_space=pltpu.SMEM)


LIMIT = 24 * 1024 * 1024
SMALL = pl.CostEstimate(flops=100_000_000, bytes_accessed=100_000, transcendentals=0)
FACTOR = dict(compiler_params=pltpu.CompilerParams(vmem_limit_bytes=LIMIT), cost_estimate=SMALL)
TILE_WORK = [pltpu.VMEM((NB, NB), F32)] + WORK


def first_factor(place, own, other):
    return pl.pallas_call(
        first_kernel, out_shape=TILE, in_specs=[SMEM, VMEM, VMEM], out_specs=VMEM,
        scratch_shapes=TILE_WORK, name="first_factor", **FACTOR,
    )(place, own, other)


def second_factor(place, w00, own, other):
    return pl.pallas_call(
        second_kernel, out_shape=(TILE, TILE), in_specs=[SMEM, VMEM, VMEM, VMEM], out_specs=(VMEM, VMEM),
        scratch_shapes=TILE_WORK, name="second_factor", **FACTOR,
    )(place, w00, own, other)


def corner_kernel(a, *pieces):
    *pieces, flipped = pieces
    flipped[...] = a[:, 1, :].T
    for q in range(16):
        value = a[:, q, :]
        for ref in pieces[q // 2 :: 8]:
            ref[:, 128 * (q % 2) : 128 * (q % 2) + 128] = value


def corner_call(flat):
    return pl.pallas_call(
        corner_kernel, grid=(2,), out_shape=(TILE,) * 9 + (jax.ShapeDtypeStruct((128, NB), F32),),
        in_specs=[pl.BlockSpec((128, 16, 128), lambda i: (i, 0, 0))],
        out_specs=(pl.BlockSpec((128, NB), lambda i: (i, 0)),) * 9 + (pl.BlockSpec((128, 128), lambda i: (0, i)),),
        name="corner_tiles",
    )(flat)


def column_kernel(weights, a, column, sums):
    step = pl.program_id(0)
    for q in range(2):
        column[:, 128 * q : 128 * q + 128] = a[:, q, :]

    @pl.when(step == 0)
    def _():
        sums[...] = jnp.zeros_like(sums)

    def body(i, total):
        for j in range(8):
            row = 8 * i + j
            total = total + weights[step * 128 + row] * a[row]
        return total

    sums[...] += lax.fori_loop(0, 16, body, jnp.zeros((16, 128), F32))


def column_call(weights, flat):
    return pl.pallas_call(
        column_kernel, grid=(8,),
        out_shape=(jax.ShapeDtypeStruct((1024, NB), F32), jax.ShapeDtypeStruct((16, 128), F32)),
        in_specs=[SMEM, pl.BlockSpec((128, 16, 128), lambda i: (i, 0, 0))],
        out_specs=(
            pl.BlockSpec((128, NB), lambda i: (i, 0)),
            pl.BlockSpec((16, 128), lambda i: (0, 0)),
        ),
        name="first_column", **FACTOR,
    )(weights, flat)


ROWS = 256


def final_kernel(
    place, flat, across, mine, theirs, w00, l10, w11, sums, out, panels, checksum,
    block, right, solved, high, low, right_high, right_low, ready, factors, block_sem, right_sem, panel_sem, out_sem,
):
    row_index, col_index = place[0], place[1]
    even = col_index % 2 == 0
    blocks = [
        pltpu.make_async_copy(flat.at[pl.ds(ROWS * i, ROWS)], block.at[pl.ds(ROWS * i, ROWS)], block_sem.at[i]) for i in range(4)
    ]
    rights = [pltpu.make_async_copy(across.at[pl.ds(8 * i, 8)], right.at[pl.ds(8 * i, 8)], right_sem.at[i]) for i in range(2)]
    for copy in (rights[0], *blocks, rights[1]):
        copy.start()

    for k, ref in enumerate((w00, l10, w11)):
        factors[0, k], factors[1, k] = halves(ref[...])
    f00, f10, f11 = [(factors[0, k], factors[1, k]) for k in range(3)]
    solves = []
    for half in range(2):
        rows = slice(512 * half, 512 * half + 512 + 16 * half)
        first = jnp.where(even, mine[rows], theirs[rows])
        second = jnp.where(even, theirs[rows], mine[rows])
        left = dot3(halves(first), f00, NT)
        bottom = dot3(halves(second - dot3(halves(left), f10, NT)), f11, NT)
        solved[512 * half : 512 * half + 512, 0:256] = left[0:512]
        if half == 0:
            top = (row_index == 0) & (lax.broadcasted_iota(jnp.int32, (512, 1), 0) < NB)
            solved[0:512, 256:512] = jnp.where(top, 0.0, bottom)
        else:
            solved[512:1024, 256:512] = bottom[0:512]
        copy = pltpu.make_async_copy(
            solved.at[pl.ds(512 * half, 512)], panels.at[pl.ds(512 * half, 512)], panel_sem.at[half]
        )
        copy.start()
        solves.append(copy)
        last = halves(dot3(halves(bottom), f11, NN))
        high[rows, 256:512], low[rows, 256:512] = last
        high[rows, 0:256], low[rows, 0:256] = halves(dot3(halves(left - dot3(last, f10, NN)), f00, NN))

    def put(slot, group, step):
        return pltpu.make_async_copy(
            ready.at[slot], out.at[pl.ds(pl.multiple_of(step * ROWS, ROWS), ROWS), group], out_sem.at[slot]
        )

    for group in range(2):
        rights[group].wait()
        for u in range(4):
            for h in range(2):
                span = slice(NB * h, NB * h + NB)
                right_high[u, span], right_low[u, span] = halves(right[8 * group + 2 * u + h])

        def body(step, carry, group=group):
            slot = step % 2
            base = pl.multiple_of(step * ROWS, ROWS)
            if group == 0:
                for i in range(4):

                    @pl.when(step == i)
                    def _(i=i):
                        blocks[i].wait()

            @pl.when(step + 4 * group >= 2)
            def _():
                put(slot, group, step).wait()

            g_high = jnp.concatenate([high[pl.ds(base, ROWS), :], high[1024:1040, :]], axis=0)
            g_low = jnp.concatenate([low[pl.ds(base, ROWS), :], low[1024:1040, :]], axis=0)
            for u in range(4):
                product = dot3((g_high, g_low), (right_high[u], right_low[u]), NN)
                for h in range(2):
                    q = 2 * u + h
                    lanes = slice(128 * h, 128 * h + 128)
                    ready[slot, :, q, :] = block[pl.ds(base, ROWS), group, q, :] - product[0:ROWS, lanes]
                    at = 8 * group + q
                    kept = sums[at : at + 1, :] - product[ROWS : ROWS + 1, lanes]
                    if (group, u) == (0, 0):
                        kept = jnp.where(col_index < 2, 0.0, kept)
                    checksum[at : at + 1, :] = kept
            @pl.when((step == 0) & (row_index < 2))
            def _():
                ready[slot] = jnp.zeros((ROWS, 8, 128), F32)

            if group == 0:

                @pl.when(col_index < 2)
                def _():
                    ready[slot, :, 0:2, :] = jnp.zeros((ROWS, 2, 128), F32)

            put(slot, group, step).start()
            return carry

        lax.fori_loop(0, 4, body, 0)
    for slot in range(2):
        put(slot, 1, 2 + slot).wait()
    for copy in solves:
        copy.wait()


def final_call(place, flat, across, mine, theirs, w00, l10, w11, sums):
    hbm = pl.BlockSpec(memory_space=pl.ANY)
    return pl.pallas_call(
        final_kernel,
        out_shape=(
            jax.ShapeDtypeStruct((1024, 2, 8, 128), F32),
            jax.ShapeDtypeStruct((1024, 512), F32),
            jax.ShapeDtypeStruct((16, 128), F32),
        ),
        in_specs=[SMEM, hbm, hbm] + [VMEM] * 6,
        out_specs=(hbm, hbm, VMEM),
        scratch_shapes=[
            pltpu.VMEM((1024, 2, 8, 128), F32),
            pltpu.VMEM((16, NB, NB), F32),
            pltpu.VMEM((1024, 512), F32),
            pltpu.VMEM((1040, 512), BF16),
            pltpu.VMEM((1040, 512), BF16),
            pltpu.VMEM((4, 512, NB), BF16),
            pltpu.VMEM((4, 512, NB), BF16),
            pltpu.VMEM((2, ROWS, 8, 128), F32),
            pltpu.VMEM((2, 3, NB, NB), BF16),
            pltpu.SemaphoreType.DMA((4,)),
            pltpu.SemaphoreType.DMA((2,)),
            pltpu.SemaphoreType.DMA((2,)),
            pltpu.SemaphoreType.DMA((2,)),
        ],
        name="panels_and_trailing",
        compiler_params=pltpu.CompilerParams(vmem_limit_bytes=30 * 1024 * 1024),
        cost_estimate=SMALL,
    )(place, flat, across, mine, theirs, w00, l10, w11, sums)


def where_is(device):
    row, col = divmod(device, 8)
    return [row // 4, row % 4, col // 2, col % 2]


def device_at(z, y, x, core):
    return ((z % 4) * 4 + y % 4) * 8 + (x % 4) * 2 + core


def moved(device, dim, by):
    at = where_is(device)
    at[dim] += by
    return device_at(*at)


def spread(value, trees, here, beside):
    holders = [[device_at(z, y, 0, c)] for (z, y), c, _ in trees]
    stages = []
    for at in range(3):
        aways = [(here[dims[at]] - (z, y, 0)[dims[at]]) % 4 for (z, y), _, dims in trees]
        away = jnp.where(here[3] == trees[0][1], aways[0], aways[1])
        for half in range(2):
            pairs = []
            for held, (_, _, dims) in zip(holders, trees):
                dim = dims[at]
                if half == 0:
                    pairs += [(h, moved(h, dim, 1)) for h in held]
                else:
                    pairs += [(h, moved(h, dim, -1)) for h in held] + [(moved(h, dim, 1), moved(h, dim, 2)) for h in held]
            if stages:
                value = beside(len(stages), value)
            arrived = lax.ppermute(value, ("row", "col"), pairs)
            value = jnp.where((away == 1) if half == 0 else (away >= 2), arrived, value)
            stages.append(value)
        holders = [[moved(h, dims[at], k) for h in held for k in range(4)] for held, (_, _, dims) in zip(holders, trees)]
    return stages


def after(value, token):
    return lax.optimization_barrier((value, token))[0]


def shards(covariance, check_weights):
    row = lax.axis_index("row")
    col = lax.axis_index("col")
    core = col % 2
    x = col // 2
    here = [row // 4, row % 4, x, core]
    flat = pltpu.with_memory_space_constraint(covariance.reshape(1024, 16, 128), pltpu.HBM)
    tiles = jnp.arange(4, dtype=jnp.int32) * 16 + row
    weights = jnp.where((tiles >= 2)[:, None], check_weights.reshape(4, NB), 0.0).reshape(1024)
    place = jnp.stack([row, col]).astype(jnp.int32)
    swap_cores = [(c, c ^ 1) for c in range(8)]

    pieces = corner_call(flat)
    fetched = lax.ppermute(pieces[0], ("row", "col"), [(8, 0), (9, 1)])
    corner = jnp.where(
        core == 0,
        jnp.concatenate([pieces[0], fetched[0:128]], axis=0),
        jnp.concatenate([fetched, pieces[9]], axis=0),
    )
    column, sums = column_call(weights, after(flat, corner))
    partial = [sums]
    from_left = lax.ppermute(column, "col", [(0, 2), (1, 3)])
    from_right = lax.ppermute(column, "col", [(0, 6), (1, 7)])

    def beside(stage, value):
        before = partial[-1]
        if stage <= 4:
            d = (1, 3, 4, 12)[stage - 1]
            partial.append(before + lax.ppermute(after(before, value), "row", [(r, r ^ d) for r in range(16)]))
        return after(value, (before, from_left, from_right) if stage == 4 else before)

    tree = spread(corner, [((0, 0), 0, (0, 1, 2)), ((0, 0), 1, (0, 2, 1))], here, beside)
    sums = partial[-1]
    near_sums = jnp.broadcast_to(sums[0:2].reshape(1, NB), (16, NB))
    far_sums = [lax.ppermute(near_sums, "col", [(0, 2 * k), (1, 2 * k + 1)]) for k in (1, 2, 3)]
    own, far_sums = lax.optimization_barrier((tree[-1], far_sums))
    other = lax.ppermute(own, "col", swap_cores)

    piece = pieces[8]
    for j in range(1, 8):
        piece = jnp.where(row // 2 == j, lax.ppermute(pieces[j] if j < 4 else after(pieces[j], fetched), "row", [(0, 2 * j), (1, 2 * j + 1)]), piece)
    across = lax.all_gather(after(piece, (tree[0], column)), "row", axis=0)
    across = pltpu.with_memory_space_constraint(across, pltpu.HBM)

    w00 = first_factor(place, own, other)
    panel_sums = near_sums
    for k in (1, 2, 3):
        panel_sums = jnp.where(x == k, far_sums[k - 1], panel_sums)

    l10, w11 = second_factor(place, w00, own, other)
    mine = jnp.where(x == 1, from_left, jnp.where(x == 3, from_right, column))
    mine = after(mine, own)
    upper = lax.ppermute(mine[0:512], "col", [(2, 4), (3, 5)])
    lower = lax.ppermute(mine[512:1024], "col", [(6, 4), (7, 5)])
    upper, lower = after((upper, lower), w00)
    upper = jnp.where(x == 2, upper, mine[0:512])
    lower = jnp.where(x == 2, lower, mine[512:1024])
    mine = jnp.concatenate([upper, lower, panel_sums], axis=0)
    theirs = after(lax.ppermute(mine, "col", swap_cores), w11)

    grouped = pltpu.with_memory_space_constraint(covariance.reshape(1024, 2, 8, 128), pltpu.HBM)
    trailing, panels, checksum = final_call(place, grouped, across, mine, theirs, w00, l10, w11, sums)
    return (
        trailing.reshape(4, 1, NB, 8, 1, NB),
        panels.reshape(4, 1, NB, 512),
        checksum.reshape(8, 1, NB),
    )


def solution(mesh):
    in_specs = (P(None, "row", None, None, "col", None), P(None, "row", None))
    out_specs = (
        P(None, "row", None, None, "col", None),
        P(None, "row", None, None),
        P(None, "col", None),
    )
    return jax.shard_map(shards, mesh=mesh, in_specs=in_specs, out_specs=out_specs, check_vma=False)
```

```python
import functools

import jax
import jax.numpy as jnp
from jax import lax
from jax.experimental import pallas as pl
from jax.experimental.pallas import tpu as pltpu
from jax.sharding import PartitionSpec as P

HIGHEST = lax.Precision.HIGHEST
F32 = jnp.float32
BF16 = jnp.bfloat16
NB = 256
NT = (((1,), (1,)), ((), ()))
NN = (((1,), (0,)), ((), ()))


def dot6(a, b, dims):
    return lax.dot_general(a, b, dims, precision=HIGHEST, preferred_element_type=F32)


def halves(value):
    high = value.astype(BF16)
    return high, (value - high.astype(F32)).astype(BF16)


def dot3(a, b, dims):
    total = lax.dot_general(a[0], b[0], dims, preferred_element_type=F32)
    total += lax.dot_general(a[0], b[1], dims, preferred_element_type=F32)
    return total + lax.dot_general(a[1], b[0], dims, preferred_element_type=F32)


def splat_row(ref, row, lanes):
    return jnp.broadcast_to(ref[row : row + 1, lanes], (8, 128))


def splat_lane(value, lane):
    return jnp.broadcast_to(value[:, lane : lane + 1], (8, 128))


def invert_factor(m, put):
    left, right = slice(0, 128), slice(128, 256)
    for block in range(16):
        base = 8 * block
        rows = [[splat_row(m, base + a, side) for a in range(8)] for side in (left, right)]
        b = {(a, k): splat_lane(rows[0][a], base + k) for a in range(8) for k in range(a + 1)}
        n = {}
        inverse, root = [], []
        for i in range(8):
            inverse.append(1.0 / b[i, i])
            root.append(lax.rsqrt(b[i, i]))
            for k in range(i + 1, 8):
                ratio = b[k, i] * inverse[i]
                for j in range(i + 1, k + 1):
                    b[k, j] = b[k, j] - ratio * b[j, i]
                for j in range(i):
                    n[k, j] = n[k, j] - ratio * n[i, j]
                n[k, i] = -ratio
        solved = []
        for side in range(2):
            upper = []
            for i in range(8):
                value = rows[side][i]
                for j in range(i):
                    value = value + n[i, j] * rows[side][j]
                upper.append(value)
            if side == 1:
                for i in range(8):
                    put(base + i, root[i] * upper[i])
            scaled = [inverse[i] * upper[i] for i in range(8)]
            out = []
            for i in range(8):
                value = scaled[i]
                for k in range(i + 1, 8):
                    value = value + n[k, i] * scaled[k]
                out.append(value)
            solved.append(out)
        for other in range(block + 1, 16):
            span = slice(8 * other, 8 * other + 8)
            a_part, n_part = m[span, left], m[span, right]
            columns = [splat_lane(a_part, base + i) for i in range(8)]
            for i in range(8):
                a_part = a_part - columns[i] * solved[0][i]
                n_part = n_part - columns[i] * solved[1][i]
            m[span, left] = a_part
            m[span, right] = n_part


def factor_tile(source, out, m, part):
    eye = (lax.broadcasted_iota(jnp.int32, (128, 128), 0) == lax.broadcasted_iota(jnp.int32, (128, 128), 1)).astype(F32)
    m[:, 0:128] = source[0:128, 0:128]

    def body(i, carry):
        m[:, 128:256] = eye

        def put(row, value):
            part[i, row : row + 1, :] = value[0:1, :]

        invert_factor(m, put)

        @pl.when(i == 0)
        def _():
            low = dot6(source[128:256, 0:128], part[0], NT)
            m[:, 0:128] = source[128:256, 128:256] - dot6(low, low, NT)
            part[2] = low

        return carry

    lax.fori_loop(0, 2, body, 0)
    out[0:128, 0:128] = part[0]
    out[0:128, 128:256] = jnp.zeros((128, 128), F32)
    out[128:256, 128:256] = part[1]
    out[128:256, 0:128] = -dot6(part[1], dot6(part[2], part[0], NN), NN)


def first_kernel(place, own, other, w00, tile, m, part):
    tile[...] = jnp.where(place[1] % 2 == 0, own[0:NB], other[0:NB])
    factor_tile(tile, w00, m, part)


def second_kernel(place, w00, own, other, l10, w11, schur, m, part):
    even = place[1] % 2 == 0
    top, bottom = own[NB : NB + 128], other[NB : NB + 128]
    c10 = jnp.concatenate([jnp.where(even, top, bottom), jnp.where(even, bottom, top)], axis=0)
    low = dot6(c10, w00[...], NT)
    l10[...] = low
    schur[...] = jnp.where(even, other[0:NB], own[0:NB]) - dot6(low, low, NT)
    factor_tile(schur, w11, m, part)


TILE = jax.ShapeDtypeStruct((NB, NB), F32)
WORK = [pltpu.VMEM((128, 256), F32), pltpu.VMEM((3, 128, 128), F32)]
VMEM = pl.BlockSpec(memory_space=pltpu.VMEM)
SMEM = pl.BlockSpec(memory_space=pltpu.SMEM)


LIMIT = 24 * 1024 * 1024
SMALL = pl.CostEstimate(flops=100_000_000, bytes_accessed=100_000, transcendentals=0)
FACTOR = dict(compiler_params=pltpu.CompilerParams(vmem_limit_bytes=LIMIT), cost_estimate=SMALL)
TILE_WORK = [pltpu.VMEM((NB, NB), F32)] + WORK


def first_factor(place, own, other):
    return pl.pallas_call(
        first_kernel, out_shape=TILE, in_specs=[SMEM, VMEM, VMEM], out_specs=VMEM,
        scratch_shapes=TILE_WORK, name="first_factor", **FACTOR,
    )(place, own, other)


def second_factor(place, w00, own, other):
    return pl.pallas_call(
        second_kernel, out_shape=(TILE, TILE), in_specs=[SMEM, VMEM, VMEM, VMEM], out_specs=(VMEM, VMEM),
        scratch_shapes=TILE_WORK, name="second_factor", **FACTOR,
    )(place, w00, own, other)


def corner_kernel(a, *pieces):
    *pieces, flipped = pieces
    flipped[...] = a[:, 1, :].T
    for q in range(16):
        value = a[:, q, :]
        for ref in pieces[q // 2 :: 8]:
            ref[:, 128 * (q % 2) : 128 * (q % 2) + 128] = value


def corner_call(flat):
    return pl.pallas_call(
        corner_kernel, grid=(2,), out_shape=(TILE,) * 9 + (jax.ShapeDtypeStruct((128, NB), F32),),
        in_specs=[pl.BlockSpec((128, 16, 128), lambda i: (i, 0, 0))],
        out_specs=(pl.BlockSpec((128, NB), lambda i: (i, 0)),) * 9 + (pl.BlockSpec((128, 128), lambda i: (0, i)),),
        name="corner_tiles",
    )(flat)


def column_kernel(weights, a, column, sums):
    step = pl.program_id(0)
    for q in range(2):
        column[:, 128 * q : 128 * q + 128] = a[:, q, :]

    @pl.when(step == 0)
    def _():
        sums[...] = jnp.zeros_like(sums)

    def body(i, total):
        for j in range(8):
            row = 8 * i + j
            total = total + weights[step * 128 + row] * a[row]
        return total

    sums[...] += lax.fori_loop(0, 16, body, jnp.zeros((16, 128), F32))


def column_call(weights, flat):
    return pl.pallas_call(
        column_kernel, grid=(8,),
        out_shape=(jax.ShapeDtypeStruct((1024, NB), F32), jax.ShapeDtypeStruct((16, 128), F32)),
        in_specs=[SMEM, pl.BlockSpec((128, 16, 128), lambda i: (i, 0, 0))],
        out_specs=(
            pl.BlockSpec((128, NB), lambda i: (i, 0)),
            pl.BlockSpec((16, 128), lambda i: (0, 0)),
        ),
        name="first_column", **FACTOR,
    )(weights, flat)


ROWS = 256


def final_kernel(
    place, flat, across, mine, theirs, w00, l10, w11, sums, out, panels, checksum,
    block, right, solved, high, low, right_high, right_low, ready, factors, block_sem, right_sem, panel_sem, out_sem,
):
    row_index, col_index = place[0], place[1]
    even = col_index % 2 == 0
    blocks = [
        pltpu.make_async_copy(flat.at[pl.ds(ROWS * i, ROWS)], block.at[pl.ds(ROWS * i, ROWS)], block_sem.at[i]) for i in range(4)
    ]
    rights = [pltpu.make_async_copy(across.at[pl.ds(8 * i, 8)], right.at[pl.ds(8 * i, 8)], right_sem.at[i]) for i in range(2)]
    for copy in (rights[0], *blocks, rights[1]):
        copy.start()

    for k, ref in enumerate((w00, l10, w11)):
        factors[0, k], factors[1, k] = halves(ref[...])
    f00, f10, f11 = [(factors[0, k], factors[1, k]) for k in range(3)]
    solves = []
    for half in range(2):
        rows = slice(512 * half, 512 * half + 512 + 16 * half)
        first = jnp.where(even, mine[rows], theirs[rows])
        second = jnp.where(even, theirs[rows], mine[rows])
        left = dot3(halves(first), f00, NT)
        bottom = dot3(halves(second - dot3(halves(left), f10, NT)), f11, NT)
        solved[512 * half : 512 * half + 512, 0:256] = left[0:512]
        if half == 0:
            top = (row_index == 0) & (lax.broadcasted_iota(jnp.int32, (512, 1), 0) < NB)
            solved[0:512, 256:512] = jnp.where(top, 0.0, bottom)
        else:
            solved[512:1024, 256:512] = bottom[0:512]
        copy = pltpu.make_async_copy(
            solved.at[pl.ds(512 * half, 512)], panels.at[pl.ds(512 * half, 512)], panel_sem.at[half]
        )
        copy.start()
        solves.append(copy)
        last = halves(dot3(halves(bottom), f11, NN))
        high[rows, 256:512], low[rows, 256:512] = last
        high[rows, 0:256], low[rows, 0:256] = halves(dot3(halves(left - dot3(last, f10, NN)), f00, NN))

    def put(slot, group, step):
        return pltpu.make_async_copy(
            ready.at[slot], out.at[pl.ds(pl.multiple_of(step * ROWS, ROWS), ROWS), group], out_sem.at[slot]
        )

    for group in range(2):
        rights[group].wait()
        for u in range(4):
            for h in range(2):
                span = slice(NB * h, NB * h + NB)
                right_high[u, span], right_low[u, span] = halves(right[8 * group + 2 * u + h])

        def body(step, carry, group=group):
            slot = step % 2
            base = pl.multiple_of(step * ROWS, ROWS)
            if group == 0:
                for i in range(4):

                    @pl.when(step == i)
                    def _(i=i):
                        blocks[i].wait()

            @pl.when(step + 4 * group >= 2)
            def _():
                put(slot, group, step).wait()

            g_high = jnp.concatenate([high[pl.ds(base, ROWS), :], high[1024:1040, :]], axis=0)
            g_low = jnp.concatenate([low[pl.ds(base, ROWS), :], low[1024:1040, :]], axis=0)
            for u in range(4):
                product = dot3((g_high, g_low), (right_high[u], right_low[u]), NN)
                for h in range(2):
                    q = 2 * u + h
                    lanes = slice(128 * h, 128 * h + 128)
                    ready[slot, :, q, :] = block[pl.ds(base, ROWS), group, q, :] - product[0:ROWS, lanes]
                    at = 8 * group + q
                    kept = sums[at : at + 1, :] - product[ROWS : ROWS + 1, lanes]
                    if (group, u) == (0, 0):
                        kept = jnp.where(col_index < 2, 0.0, kept)
                    checksum[at : at + 1, :] = kept
            @pl.when((step == 0) & (row_index < 2))
            def _():
                ready[slot] = jnp.zeros((ROWS, 8, 128), F32)

            if group == 0:

                @pl.when(col_index < 2)
                def _():
                    ready[slot, :, 0:2, :] = jnp.zeros((ROWS, 2, 128), F32)

            put(slot, group, step).start()
            return carry

        lax.fori_loop(0, 4, body, 0)
    for slot in range(2):
        put(slot, 1, 2 + slot).wait()
    for copy in solves:
        copy.wait()


def final_call(place, flat, across, mine, theirs, w00, l10, w11, sums):
    hbm = pl.BlockSpec(memory_space=pl.ANY)
    return pl.pallas_call(
        final_kernel,
        out_shape=(
            jax.ShapeDtypeStruct((1024, 2, 8, 128), F32),
            jax.ShapeDtypeStruct((1024, 512), F32),
            jax.ShapeDtypeStruct((16, 128), F32),
        ),
        in_specs=[SMEM, hbm, hbm] + [VMEM] * 6,
        out_specs=(hbm, hbm, VMEM),
        scratch_shapes=[
            pltpu.VMEM((1024, 2, 8, 128), F32),
            pltpu.VMEM((16, NB, NB), F32),
            pltpu.VMEM((1024, 512), F32),
            pltpu.VMEM((1040, 512), BF16),
            pltpu.VMEM((1040, 512), BF16),
            pltpu.VMEM((4, 512, NB), BF16),
            pltpu.VMEM((4, 512, NB), BF16),
            pltpu.VMEM((2, ROWS, 8, 128), F32),
            pltpu.VMEM((2, 3, NB, NB), BF16),
            pltpu.SemaphoreType.DMA((4,)),
            pltpu.SemaphoreType.DMA((2,)),
            pltpu.SemaphoreType.DMA((2,)),
            pltpu.SemaphoreType.DMA((2,)),
        ],
        name="panels_and_trailing",
        compiler_params=pltpu.CompilerParams(vmem_limit_bytes=30 * 1024 * 1024),
        cost_estimate=SMALL,
    )(place, flat, across, mine, theirs, w00, l10, w11, sums)


def where_is(device):
    row, col = divmod(device, 8)
    return [row // 4, row % 4, col // 2, col % 2]


def device_at(z, y, x, core):
    return ((z % 4) * 4 + y % 4) * 8 + (x % 4) * 2 + core


def moved(device, dim, by):
    at = where_is(device)
    at[dim] += by
    return device_at(*at)


def spread(value, trees, here, beside):
    holders = [[device_at(z, y, 0, c)] for (z, y), c, _ in trees]
    stages = []
    for at in range(3):
        aways = [(here[dims[at]] - (z, y, 0)[dims[at]]) % 4 for (z, y), _, dims in trees]
        away = jnp.where(here[3] == trees[0][1], aways[0], aways[1])
        for half in range(2):
            pairs = []
            for held, (_, _, dims) in zip(holders, trees):
                dim = dims[at]
                if half == 0:
                    pairs += [(h, moved(h, dim, 1)) for h in held]
                else:
                    pairs += [(h, moved(h, dim, -1)) for h in held] + [(moved(h, dim, 1), moved(h, dim, 2)) for h in held]
            if stages:
                value = beside(len(stages), value)
            arrived = lax.ppermute(value, ("row", "col"), pairs)
            value = jnp.where((away == 1) if half == 0 else (away >= 2), arrived, value)
            stages.append(value)
        holders = [[moved(h, dims[at], k) for h in held for k in range(4)] for held, (_, _, dims) in zip(holders, trees)]
    return stages


def after(value, token):
    return lax.optimization_barrier((value, token))[0]


def shards(covariance, check_weights):
    row = lax.axis_index("row")
    col = lax.axis_index("col")
    core = col % 2
    x = col // 2
    here = [row // 4, row % 4, x, core]
    flat = pltpu.with_memory_space_constraint(covariance.reshape(1024, 16, 128), pltpu.HBM)
    tiles = jnp.arange(4, dtype=jnp.int32) * 16 + row
    weights = jnp.where((tiles >= 2)[:, None], check_weights.reshape(4, NB), 0.0).reshape(1024)
    place = jnp.stack([row, col]).astype(jnp.int32)
    swap_cores = [(c, c ^ 1) for c in range(8)]

    pieces = corner_call(flat)
    fetched = lax.ppermute(pieces[0], ("row", "col"), [(8, 0), (9, 1)])
    corner = jnp.where(
        core == 0,
        jnp.concatenate([pieces[0], fetched[0:128]], axis=0),
        jnp.concatenate([fetched, pieces[9]], axis=0),
    )
    column, sums = column_call(weights, after(flat, corner))
    partial = [sums]
    from_left = lax.ppermute(column, "col", [(0, 2), (1, 3)])
    from_right = lax.ppermute(column, "col", [(0, 6), (1, 7)])

    def beside(stage, value):
        before = partial[-1]
        if stage <= 4:
            d = (1, 3, 4, 12)[stage - 1]
            partial.append(before + lax.ppermute(after(before, value), "row", [(r, r ^ d) for r in range(16)]))
        return after(value, (before, from_left, from_right) if stage == 5 else before)

    tree = spread(corner, [((0, 0), 0, (0, 1, 2)), ((0, 0), 1, (0, 2, 1))], here, beside)
    sums = partial[-1]
    near_sums = jnp.broadcast_to(sums[0:2].reshape(1, NB), (16, NB))
    far_sums = [lax.ppermute(near_sums, "col", [(0, 2 * k), (1, 2 * k + 1)]) for k in (1, 2, 3)]
    own, far_sums = lax.optimization_barrier((tree[-1], far_sums))
    other = lax.ppermute(own, "col", swap_cores)

    piece = pieces[8]
    for j in range(1, 8):
        piece = jnp.where(row // 2 == j, lax.ppermute(pieces[j] if j < 4 else after(pieces[j], fetched), "row", [(0, 2 * j), (1, 2 * j + 1)]), piece)
    across = lax.all_gather(after(piece, (tree[0], column)), "row", axis=0)
    across = pltpu.with_memory_space_constraint(across, pltpu.HBM)

    w00 = first_factor(place, own, other)
    panel_sums = near_sums
    for k in (1, 2, 3):
        panel_sums = jnp.where(x == k, far_sums[k - 1], panel_sums)

    l10, w11 = second_factor(place, w00, own, other)
    mine = jnp.where(x == 1, from_left, jnp.where(x == 3, from_right, column))
    mine = after(mine, own)
    upper = lax.ppermute(mine[0:512], "col", [(2, 4), (3, 5)])
    lower = lax.ppermute(mine[512:1024], "col", [(6, 4), (7, 5)])
    upper, lower = after((upper, lower), w00)
    upper = jnp.where(x == 2, upper, mine[0:512])
    lower = jnp.where(x == 2, lower, mine[512:1024])
    mine = jnp.concatenate([upper, lower, panel_sums], axis=0)
    theirs = after(lax.ppermute(mine, "col", swap_cores), w11)

    grouped = pltpu.with_memory_space_constraint(covariance.reshape(1024, 2, 8, 128), pltpu.HBM)
    trailing, panels, checksum = final_call(place, grouped, across, mine, theirs, w00, l10, w11, sums)
    return (
        trailing.reshape(4, 1, NB, 8, 1, NB),
        panels.reshape(4, 1, NB, 512),
        checksum.reshape(8, 1, NB),
    )


def solution(mesh):
    in_specs = (P(None, "row", None, None, "col", None), P(None, "row", None))
    out_specs = (
        P(None, "row", None, None, "col", None),
        P(None, "row", None, None),
        P(None, "col", None),
    )
    return jax.shard_map(shards, mesh=mesh, in_specs=in_specs, out_specs=out_specs, check_vma=False)
```

```python
import functools

import jax
import jax.numpy as jnp
from jax import lax
from jax.experimental import pallas as pl
from jax.experimental.pallas import tpu as pltpu
from jax.sharding import PartitionSpec as P

HIGHEST = lax.Precision.HIGHEST
F32 = jnp.float32
BF16 = jnp.bfloat16
NB = 256
NT = (((1,), (1,)), ((), ()))
NN = (((1,), (0,)), ((), ()))


def dot6(a, b, dims):
    return lax.dot_general(a, b, dims, precision=HIGHEST, preferred_element_type=F32)


def halves(value):
    high = value.astype(BF16)
    return high, (value - high.astype(F32)).astype(BF16)


def dot3(a, b, dims):
    total = lax.dot_general(a[0], b[0], dims, preferred_element_type=F32)
    total += lax.dot_general(a[0], b[1], dims, preferred_element_type=F32)
    return total + lax.dot_general(a[1], b[0], dims, preferred_element_type=F32)


def splat_row(ref, row, lanes):
    return jnp.broadcast_to(ref[row : row + 1, lanes], (8, 128))


def splat_lane(value, lane):
    return jnp.broadcast_to(value[:, lane : lane + 1], (8, 128))


def invert_factor(m, put):
    left, right = slice(0, 128), slice(128, 256)
    for block in range(16):
        base = 8 * block
        rows = [[splat_row(m, base + a, side) for a in range(8)] for side in (left, right)]
        b = {(a, k): splat_lane(rows[0][a], base + k) for a in range(8) for k in range(a + 1)}
        n = {}
        inverse, root = [], []
        for i in range(8):
            inverse.append(1.0 / b[i, i])
            root.append(lax.rsqrt(b[i, i]))
            for k in range(i + 1, 8):
                ratio = b[k, i] * inverse[i]
                for j in range(i + 1, k + 1):
                    b[k, j] = b[k, j] - ratio * b[j, i]
                for j in range(i):
                    n[k, j] = n[k, j] - ratio * n[i, j]
                n[k, i] = -ratio
        solved = []
        for side in range(2):
            upper = []
            for i in range(8):
                value = rows[side][i]
                for j in range(i):
                    value = value + n[i, j] * rows[side][j]
                upper.append(value)
            if side == 1:
                for i in range(8):
                    put(base + i, root[i] * upper[i])
            scaled = [inverse[i] * upper[i] for i in range(8)]
            out = []
            for i in range(8):
                value = scaled[i]
                for k in range(i + 1, 8):
                    value = value + n[k, i] * scaled[k]
                out.append(value)
            solved.append(out)
        for other in range(block + 1, 16):
            span = slice(8 * other, 8 * other + 8)
            a_part, n_part = m[span, left], m[span, right]
            columns = [splat_lane(a_part, base + i) for i in range(8)]
            for i in range(8):
                a_part = a_part - columns[i] * solved[0][i]
                n_part = n_part - columns[i] * solved[1][i]
            m[span, left] = a_part
            m[span, right] = n_part


def factor_tile(source, out, m, part):
    eye = (lax.broadcasted_iota(jnp.int32, (128, 128), 0) == lax.broadcasted_iota(jnp.int32, (128, 128), 1)).astype(F32)
    m[:, 0:128] = source[0:128, 0:128]

    def body(i, carry):
        m[:, 128:256] = eye

        def put(row, value):
            part[i, row : row + 1, :] = value[0:1, :]

        invert_factor(m, put)

        @pl.when(i == 0)
        def _():
            low = dot6(source[128:256, 0:128], part[0], NT)
            m[:, 0:128] = source[128:256, 128:256] - dot6(low, low, NT)
            part[2] = low

        return carry

    lax.fori_loop(0, 2, body, 0)
    out[0:128, 0:128] = part[0]
    out[0:128, 128:256] = jnp.zeros((128, 128), F32)
    out[128:256, 128:256] = part[1]
    out[128:256, 0:128] = -dot6(part[1], dot6(part[2], part[0], NN), NN)


def first_kernel(place, own, other, w00, tile, m, part):
    tile[...] = jnp.where(place[1] % 2 == 0, own[0:NB], other[0:NB])
    factor_tile(tile, w00, m, part)


def second_kernel(place, w00, own, other, l10, w11, schur, m, part):
    even = place[1] % 2 == 0
    top, bottom = own[NB : NB + 128], other[NB : NB + 128]
    c10 = jnp.concatenate([jnp.where(even, top, bottom), jnp.where(even, bottom, top)], axis=0)
    low = dot6(c10, w00[...], NT)
    l10[...] = low
    schur[...] = jnp.where(even, other[0:NB], own[0:NB]) - dot6(low, low, NT)
    factor_tile(schur, w11, m, part)


TILE = jax.ShapeDtypeStruct((NB, NB), F32)
WORK = [pltpu.VMEM((128, 256), F32), pltpu.VMEM((3, 128, 128), F32)]
VMEM = pl.BlockSpec(memory_space=pltpu.VMEM)
SMEM = pl.BlockSpec(memory_space=pltpu.SMEM)


LIMIT = 24 * 1024 * 1024
SMALL = pl.CostEstimate(flops=100_000_000, bytes_accessed=100_000, transcendentals=0)
FACTOR = dict(compiler_params=pltpu.CompilerParams(vmem_limit_bytes=LIMIT), cost_estimate=SMALL)
TILE_WORK = [pltpu.VMEM((NB, NB), F32)] + WORK


def first_factor(place, own, other):
    return pl.pallas_call(
        first_kernel, out_shape=TILE, in_specs=[SMEM, VMEM, VMEM], out_specs=VMEM,
        scratch_shapes=TILE_WORK, name="first_factor", **FACTOR,
    )(place, own, other)


def second_factor(place, w00, own, other):
    return pl.pallas_call(
        second_kernel, out_shape=(TILE, TILE), in_specs=[SMEM, VMEM, VMEM, VMEM], out_specs=(VMEM, VMEM),
        scratch_shapes=TILE_WORK, name="second_factor", **FACTOR,
    )(place, w00, own, other)


def corner_kernel(a, *pieces):
    *pieces, flipped = pieces
    flipped[...] = a[:, 1, :].T
    for q in range(16):
        value = a[:, q, :]
        for ref in pieces[q // 2 :: 8]:
            ref[:, 128 * (q % 2) : 128 * (q % 2) + 128] = value


def corner_call(flat):
    return pl.pallas_call(
        corner_kernel, grid=(2,), out_shape=(TILE,) * 9 + (jax.ShapeDtypeStruct((128, NB), F32),),
        in_specs=[pl.BlockSpec((128, 16, 128), lambda i: (i, 0, 0))],
        out_specs=(pl.BlockSpec((128, NB), lambda i: (i, 0)),) * 9 + (pl.BlockSpec((128, 128), lambda i: (0, i)),),
        name="corner_tiles",
    )(flat)


def column_kernel(weights, a, column, sums):
    step = pl.program_id(0)
    for q in range(2):
        column[:, 128 * q : 128 * q + 128] = a[:, q, :]

    @pl.when(step == 0)
    def _():
        sums[...] = jnp.zeros_like(sums)

    def body(i, total):
        for j in range(8):
            row = 8 * i + j
            total = total + weights[step * 128 + row] * a[row]
        return total

    sums[...] += lax.fori_loop(0, 16, body, jnp.zeros((16, 128), F32))


def column_call(weights, flat):
    return pl.pallas_call(
        column_kernel, grid=(8,),
        out_shape=(jax.ShapeDtypeStruct((1024, NB), F32), jax.ShapeDtypeStruct((16, 128), F32)),
        in_specs=[SMEM, pl.BlockSpec((128, 16, 128), lambda i: (i, 0, 0))],
        out_specs=(
            pl.BlockSpec((128, NB), lambda i: (i, 0)),
            pl.BlockSpec((16, 128), lambda i: (0, 0)),
        ),
        name="first_column", **FACTOR,
    )(weights, flat)


ROWS = 256


def final_kernel(
    place, flat, across, mine, theirs, w00, l10, w11, sums, out, panels, checksum,
    block, right, solved, high, low, right_high, right_low, ready, factors, block_sem, right_sem, panel_sem, out_sem,
):
    row_index, col_index = place[0], place[1]
    even = col_index % 2 == 0
    blocks = [
        pltpu.make_async_copy(flat.at[pl.ds(ROWS * i, ROWS)], block.at[pl.ds(ROWS * i, ROWS)], block_sem.at[i]) for i in range(4)
    ]
    rights = [pltpu.make_async_copy(across.at[pl.ds(8 * i, 8)], right.at[pl.ds(8 * i, 8)], right_sem.at[i]) for i in range(2)]
    for copy in (rights[0], *blocks, rights[1]):
        copy.start()

    for k, ref in enumerate((w00, l10, w11)):
        factors[0, k], factors[1, k] = halves(ref[...])
    f00, f10, f11 = [(factors[0, k], factors[1, k]) for k in range(3)]
    solves = []
    for half in range(2):
        rows = slice(512 * half, 512 * half + 512 + 16 * half)
        first = jnp.where(even, mine[rows], theirs[rows])
        second = jnp.where(even, theirs[rows], mine[rows])
        left = dot3(halves(first), f00, NT)
        bottom = dot3(halves(second - dot3(halves(left), f10, NT)), f11, NT)
        solved[512 * half : 512 * half + 512, 0:256] = left[0:512]
        if half == 0:
            top = (row_index == 0) & (lax.broadcasted_iota(jnp.int32, (512, 1), 0) < NB)
            solved[0:512, 256:512] = jnp.where(top, 0.0, bottom)
        else:
            solved[512:1024, 256:512] = bottom[0:512]
        copy = pltpu.make_async_copy(
            solved.at[pl.ds(512 * half, 512)], panels.at[pl.ds(512 * half, 512)], panel_sem.at[half]
        )
        copy.start()
        solves.append(copy)
        last = halves(dot3(halves(bottom), f11, NN))
        high[rows, 256:512], low[rows, 256:512] = last
        high[rows, 0:256], low[rows, 0:256] = halves(dot3(halves(left - dot3(last, f10, NN)), f00, NN))

    def put(slot, group, step):
        return pltpu.make_async_copy(
            ready.at[slot], out.at[pl.ds(pl.multiple_of(step * ROWS, ROWS), ROWS), group], out_sem.at[slot]
        )

    for group in range(2):
        rights[group].wait()
        for u in range(4):
            for h in range(2):
                span = slice(NB * h, NB * h + NB)
                right_high[u, span], right_low[u, span] = halves(right[8 * group + 2 * u + h])

        def body(step, carry, group=group):
            slot = step % 2
            base = pl.multiple_of(step * ROWS, ROWS)
            if group == 0:
                for i in range(4):

                    @pl.when(step == i)
                    def _(i=i):
                        blocks[i].wait()

            @pl.when(step + 4 * group >= 2)
            def _():
                put(slot, group, step).wait()

            g_high = jnp.concatenate([high[pl.ds(base, ROWS), :], high[1024:1040, :]], axis=0)
            g_low = jnp.concatenate([low[pl.ds(base, ROWS), :], low[1024:1040, :]], axis=0)
            for u in range(4):
                product = dot3((g_high, g_low), (right_high[u], right_low[u]), NN)
                for h in range(2):
                    q = 2 * u + h
                    lanes = slice(128 * h, 128 * h + 128)
                    ready[slot, :, q, :] = block[pl.ds(base, ROWS), group, q, :] - product[0:ROWS, lanes]
                    at = 8 * group + q
                    kept = sums[at : at + 1, :] - product[ROWS : ROWS + 1, lanes]
                    if (group, u) == (0, 0):
                        kept = jnp.where(col_index < 2, 0.0, kept)
                    checksum[at : at + 1, :] = kept
            @pl.when((step == 0) & (row_index < 2))
            def _():
                ready[slot] = jnp.zeros((ROWS, 8, 128), F32)

            if group == 0:

                @pl.when(col_index < 2)
                def _():
                    ready[slot, :, 0:2, :] = jnp.zeros((ROWS, 2, 128), F32)

            put(slot, group, step).start()
            return carry

        lax.fori_loop(0, 4, body, 0)
    for slot in range(2):
        put(slot, 1, 2 + slot).wait()
    for copy in solves:
        copy.wait()


def final_call(place, flat, across, mine, theirs, w00, l10, w11, sums):
    hbm = pl.BlockSpec(memory_space=pl.ANY)
    return pl.pallas_call(
        final_kernel,
        out_shape=(
            jax.ShapeDtypeStruct((1024, 2, 8, 128), F32),
            jax.ShapeDtypeStruct((1024, 512), F32),
            jax.ShapeDtypeStruct((16, 128), F32),
        ),
        in_specs=[SMEM, hbm, hbm] + [VMEM] * 6,
        out_specs=(hbm, hbm, VMEM),
        scratch_shapes=[
            pltpu.VMEM((1024, 2, 8, 128), F32),
            pltpu.VMEM((16, NB, NB), F32),
            pltpu.VMEM((1024, 512), F32),
            pltpu.VMEM((1040, 512), BF16),
            pltpu.VMEM((1040, 512), BF16),
            pltpu.VMEM((4, 512, NB), BF16),
            pltpu.VMEM((4, 512, NB), BF16),
            pltpu.VMEM((2, ROWS, 8, 128), F32),
            pltpu.VMEM((2, 3, NB, NB), BF16),
            pltpu.SemaphoreType.DMA((4,)),
            pltpu.SemaphoreType.DMA((2,)),
            pltpu.SemaphoreType.DMA((2,)),
            pltpu.SemaphoreType.DMA((2,)),
        ],
        name="panels_and_trailing",
        compiler_params=pltpu.CompilerParams(vmem_limit_bytes=30 * 1024 * 1024),
        cost_estimate=SMALL,
    )(place, flat, across, mine, theirs, w00, l10, w11, sums)


def where_is(device):
    row, col = divmod(device, 8)
    return [row // 4, row % 4, col // 2, col % 2]


def device_at(z, y, x, core):
    return ((z % 4) * 4 + y % 4) * 8 + (x % 4) * 2 + core


def moved(device, dim, by):
    at = where_is(device)
    at[dim] += by
    return device_at(*at)


def spread(value, trees, here, beside):
    holders = [[device_at(z, y, 0, c)] for (z, y), c, _ in trees]
    stages = []
    for at in range(3):
        aways = [(here[dims[at]] - (z, y, 0)[dims[at]]) % 4 for (z, y), _, dims in trees]
        away = jnp.where(here[3] == trees[0][1], aways[0], aways[1])
        for half in range(2):
            pairs = []
            for held, (_, _, dims) in zip(holders, trees):
                dim = dims[at]
                if half == 0:
                    pairs += [(h, moved(h, dim, 1)) for h in held]
                else:
                    pairs += [(h, moved(h, dim, -1)) for h in held] + [(moved(h, dim, 1), moved(h, dim, 2)) for h in held]
            if stages:
                value = beside(len(stages), value)
            arrived = lax.ppermute(value, ("row", "col"), pairs)
            value = jnp.where((away == 1) if half == 0 else (away >= 2), arrived, value)
            stages.append(value)
        holders = [[moved(h, dims[at], k) for h in held for k in range(4)] for held, (_, _, dims) in zip(holders, trees)]
    return stages


def after(value, token):
    return lax.optimization_barrier((value, token))[0]


def shards(covariance, check_weights):
    row = lax.axis_index("row")
    col = lax.axis_index("col")
    core = col % 2
    x = col // 2
    here = [row // 4, row % 4, x, core]
    flat = pltpu.with_memory_space_constraint(covariance.reshape(1024, 16, 128), pltpu.HBM)
    tiles = jnp.arange(4, dtype=jnp.int32) * 16 + row
    weights = jnp.where((tiles >= 2)[:, None], check_weights.reshape(4, NB), 0.0).reshape(1024)
    place = jnp.stack([row, col]).astype(jnp.int32)
    swap_cores = [(c, c ^ 1) for c in range(8)]

    pieces = corner_call(flat)
    fetched = lax.ppermute(pieces[0], ("row", "col"), [(8, 0), (9, 1)])
    corner = jnp.where(
        core == 0,
        jnp.concatenate([pieces[0], fetched[0:128]], axis=0),
        jnp.concatenate([fetched, pieces[9]], axis=0),
    )
    column, sums = column_call(weights, after(flat, corner))
    partial = [sums]
    from_left = lax.ppermute(column, "col", [(0, 2), (1, 3)])
    from_right = lax.ppermute(column, "col", [(0, 6), (1, 7)])

    def beside(stage, value):
        before = partial[-1]
        if stage <= 4:
            d = (1, 3, 4, 12)[stage - 1]
            partial.append(before + lax.ppermute(after(before, value), "row", [(r, r ^ d) for r in range(16)]))
        return after(value, (before, from_left, from_right) if stage == 5 else before)

    tree = spread(corner, [((0, 0), 0, (2, 0, 1)), ((0, 0), 1, (0, 2, 1))], here, beside)
    sums = partial[-1]
    near_sums = jnp.broadcast_to(sums[0:2].reshape(1, NB), (16, NB))
    far_sums = [lax.ppermute(near_sums, "col", [(0, 2 * k), (1, 2 * k + 1)]) for k in (1, 2, 3)]
    own, far_sums = lax.optimization_barrier((tree[-1], far_sums))
    other = lax.ppermute(own, "col", swap_cores)

    piece = pieces[8]
    for j in range(1, 8):
        piece = jnp.where(row // 2 == j, lax.ppermute(pieces[j] if j < 4 else after(pieces[j], fetched), "row", [(0, 2 * j), (1, 2 * j + 1)]), piece)
    across = lax.all_gather(after(piece, (tree[0], column)), "row", axis=0)
    across = pltpu.with_memory_space_constraint(across, pltpu.HBM)

    w00 = first_factor(place, own, other)
    panel_sums = near_sums
    for k in (1, 2, 3):
        panel_sums = jnp.where(x == k, far_sums[k - 1], panel_sums)

    l10, w11 = second_factor(place, w00, own, other)
    mine = jnp.where(x == 1, from_left, jnp.where(x == 3, from_right, column))
    mine = after(mine, own)
    upper = lax.ppermute(mine[0:512], "col", [(2, 4), (3, 5)])
    lower = lax.ppermute(mine[512:1024], "col", [(6, 4), (7, 5)])
    upper, lower = after((upper, lower), w00)
    upper = jnp.where(x == 2, upper, mine[0:512])
    lower = jnp.where(x == 2, lower, mine[512:1024])
    mine = jnp.concatenate([upper, lower, panel_sums], axis=0)
    theirs = after(lax.ppermute(mine, "col", swap_cores), w11)

    grouped = pltpu.with_memory_space_constraint(covariance.reshape(1024, 2, 8, 128), pltpu.HBM)
    trailing, panels, checksum = final_call(place, grouped, across, mine, theirs, w00, l10, w11, sums)
    return (
        trailing.reshape(4, 1, NB, 8, 1, NB),
        panels.reshape(4, 1, NB, 512),
        checksum.reshape(8, 1, NB),
    )


def solution(mesh):
    in_specs = (P(None, "row", None, None, "col", None), P(None, "row", None))
    out_specs = (
        P(None, "row", None, None, "col", None),
        P(None, "row", None, None),
        P(None, "col", None),
    )
    return jax.shard_map(shards, mesh=mesh, in_specs=in_specs, out_specs=out_specs, check_vma=False)
```

```python
import functools

import jax
import jax.numpy as jnp
from jax import lax
from jax.experimental import pallas as pl
from jax.experimental.pallas import tpu as pltpu
from jax.sharding import PartitionSpec as P

HIGHEST = lax.Precision.HIGHEST
F32 = jnp.float32
BF16 = jnp.bfloat16
NB = 256
NT = (((1,), (1,)), ((), ()))
NN = (((1,), (0,)), ((), ()))


def dot6(a, b, dims):
    return lax.dot_general(a, b, dims, precision=HIGHEST, preferred_element_type=F32)


def halves(value):
    high = value.astype(BF16)
    return high, (value - high.astype(F32)).astype(BF16)


def dot3(a, b, dims):
    total = lax.dot_general(a[0], b[0], dims, preferred_element_type=F32)
    total += lax.dot_general(a[0], b[1], dims, preferred_element_type=F32)
    return total + lax.dot_general(a[1], b[0], dims, preferred_element_type=F32)


def splat_row(ref, row, lanes):
    return jnp.broadcast_to(ref[row : row + 1, lanes], (8, 128))


def splat_lane(value, lane):
    return jnp.broadcast_to(value[:, lane : lane + 1], (8, 128))


def invert_factor(m, put):
    left, right = slice(0, 128), slice(128, 256)
    for block in range(16):
        base = 8 * block
        rows = [[splat_row(m, base + a, side) for a in range(8)] for side in (left, right)]
        b = {(a, k): splat_lane(rows[0][a], base + k) for a in range(8) for k in range(a + 1)}
        n = {}
        inverse, root = [], []
        for i in range(8):
            inverse.append(1.0 / b[i, i])
            root.append(lax.rsqrt(b[i, i]))
            for k in range(i + 1, 8):
                ratio = b[k, i] * inverse[i]
                for j in range(i + 1, k + 1):
                    b[k, j] = b[k, j] - ratio * b[j, i]
                for j in range(i):
                    n[k, j] = n[k, j] - ratio * n[i, j]
                n[k, i] = -ratio
        solved = []
        for side in range(2):
            upper = []
            for i in range(8):
                value = rows[side][i]
                for j in range(i):
                    value = value + n[i, j] * rows[side][j]
                upper.append(value)
            if side == 1:
                for i in range(8):
                    put(base + i, root[i] * upper[i])
            scaled = [inverse[i] * upper[i] for i in range(8)]
            out = []
            for i in range(8):
                value = scaled[i]
                for k in range(i + 1, 8):
                    value = value + n[k, i] * scaled[k]
                out.append(value)
            solved.append(out)
        for other in range(block + 1, 16):
            span = slice(8 * other, 8 * other + 8)
            a_part, n_part = m[span, left], m[span, right]
            columns = [splat_lane(a_part, base + i) for i in range(8)]
            for i in range(8):
                a_part = a_part - columns[i] * solved[0][i]
                n_part = n_part - columns[i] * solved[1][i]
            m[span, left] = a_part
            m[span, right] = n_part


def factor_tile(source, out, m, part):
    eye = (lax.broadcasted_iota(jnp.int32, (128, 128), 0) == lax.broadcasted_iota(jnp.int32, (128, 128), 1)).astype(F32)
    m[:, 0:128] = source[0:128, 0:128]

    def body(i, carry):
        m[:, 128:256] = eye

        def put(row, value):
            part[i, row : row + 1, :] = value[0:1, :]

        invert_factor(m, put)

        @pl.when(i == 0)
        def _():
            low = dot6(source[128:256, 0:128], part[0], NT)
            m[:, 0:128] = source[128:256, 128:256] - dot6(low, low, NT)
            part[2] = low

        return carry

    lax.fori_loop(0, 2, body, 0)
    out[0:128, 0:128] = part[0]
    out[0:128, 128:256] = jnp.zeros((128, 128), F32)
    out[128:256, 128:256] = part[1]
    out[128:256, 0:128] = -dot6(part[1], dot6(part[2], part[0], NN), NN)


def first_kernel(place, own, other, w00, tile, m, part):
    tile[...] = jnp.where(place[1] % 2 == 0, own[0:NB], other[0:NB])
    factor_tile(tile, w00, m, part)


def second_kernel(place, w00, own, other, l10, w11, schur, m, part):
    even = place[1] % 2 == 0
    top, bottom = own[NB : NB + 128], other[NB : NB + 128]
    c10 = jnp.concatenate([jnp.where(even, top, bottom), jnp.where(even, bottom, top)], axis=0)
    low = dot6(c10, w00[...], NT)
    l10[...] = low
    schur[...] = jnp.where(even, other[0:NB], own[0:NB]) - dot6(low, low, NT)
    factor_tile(schur, w11, m, part)


TILE = jax.ShapeDtypeStruct((NB, NB), F32)
WORK = [pltpu.VMEM((128, 256), F32), pltpu.VMEM((3, 128, 128), F32)]
VMEM = pl.BlockSpec(memory_space=pltpu.VMEM)
SMEM = pl.BlockSpec(memory_space=pltpu.SMEM)


LIMIT = 24 * 1024 * 1024
SMALL = pl.CostEstimate(flops=100_000_000, bytes_accessed=100_000, transcendentals=0)
FACTOR = dict(compiler_params=pltpu.CompilerParams(vmem_limit_bytes=LIMIT), cost_estimate=SMALL)
TILE_WORK = [pltpu.VMEM((NB, NB), F32)] + WORK


def first_factor(place, own, other):
    return pl.pallas_call(
        first_kernel, out_shape=TILE, in_specs=[SMEM, VMEM, VMEM], out_specs=VMEM,
        scratch_shapes=TILE_WORK, name="first_factor", **FACTOR,
    )(place, own, other)


def second_factor(place, w00, own, other):
    return pl.pallas_call(
        second_kernel, out_shape=(TILE, TILE), in_specs=[SMEM, VMEM, VMEM, VMEM], out_specs=(VMEM, VMEM),
        scratch_shapes=TILE_WORK, name="second_factor", **FACTOR,
    )(place, w00, own, other)


def corner_kernel(a, *pieces):
    *pieces, flipped = pieces
    flipped[...] = a[:, 1, :].T
    for q in range(16):
        value = a[:, q, :]
        for ref in pieces[q // 2 :: 8]:
            ref[:, 128 * (q % 2) : 128 * (q % 2) + 128] = value


def corner_call(flat):
    return pl.pallas_call(
        corner_kernel, grid=(2,), out_shape=(TILE,) * 9 + (jax.ShapeDtypeStruct((128, NB), F32),),
        in_specs=[pl.BlockSpec((128, 16, 128), lambda i: (i, 0, 0))],
        out_specs=(pl.BlockSpec((128, NB), lambda i: (i, 0)),) * 9 + (pl.BlockSpec((128, 128), lambda i: (0, i)),),
        name="corner_tiles",
    )(flat)


def column_kernel(weights, a, column, sums):
    step = pl.program_id(0)
    for q in range(2):
        column[:, 128 * q : 128 * q + 128] = a[:, q, :]

    @pl.when(step == 0)
    def _():
        sums[...] = jnp.zeros_like(sums)

    def body(i, total):
        for j in range(8):
            row = 8 * i + j
            total = total + weights[step * 128 + row] * a[row]
        return total

    sums[...] += lax.fori_loop(0, 16, body, jnp.zeros((16, 128), F32))


def column_call(weights, flat):
    return pl.pallas_call(
        column_kernel, grid=(8,),
        out_shape=(jax.ShapeDtypeStruct((1024, NB), F32), jax.ShapeDtypeStruct((16, 128), F32)),
        in_specs=[SMEM, pl.BlockSpec((128, 16, 128), lambda i: (i, 0, 0))],
        out_specs=(
            pl.BlockSpec((128, NB), lambda i: (i, 0)),
            pl.BlockSpec((16, 128), lambda i: (0, 0)),
        ),
        name="first_column", **FACTOR,
    )(weights, flat)


ROWS = 256


def final_kernel(
    place, flat, across, mine, theirs, w00, l10, w11, sums, out, panels, checksum,
    block, right, solved, high, low, right_high, right_low, ready, factors, block_sem, right_sem, panel_sem, out_sem,
):
    row_index, col_index = place[0], place[1]
    even = col_index % 2 == 0
    blocks = [
        pltpu.make_async_copy(flat.at[pl.ds(ROWS * i, ROWS)], block.at[pl.ds(ROWS * i, ROWS)], block_sem.at[i]) for i in range(4)
    ]
    rights = [pltpu.make_async_copy(across.at[pl.ds(8 * i, 8)], right.at[pl.ds(8 * i, 8)], right_sem.at[i]) for i in range(2)]
    for copy in (rights[0], *blocks, rights[1]):
        copy.start()

    for k, ref in enumerate((w00, l10, w11)):
        factors[0, k], factors[1, k] = halves(ref[...])
    f00, f10, f11 = [(factors[0, k], factors[1, k]) for k in range(3)]
    solves = []
    for half in range(2):
        rows = slice(512 * half, 512 * half + 512 + 16 * half)
        first = jnp.where(even, mine[rows], theirs[rows])
        second = jnp.where(even, theirs[rows], mine[rows])
        left = dot3(halves(first), f00, NT)
        bottom = dot3(halves(second - dot3(halves(left), f10, NT)), f11, NT)
        solved[512 * half : 512 * half + 512, 0:256] = left[0:512]
        if half == 0:
            top = (row_index == 0) & (lax.broadcasted_iota(jnp.int32, (512, 1), 0) < NB)
            solved[0:512, 256:512] = jnp.where(top, 0.0, bottom)
        else:
            solved[512:1024, 256:512] = bottom[0:512]
        copy = pltpu.make_async_copy(
            solved.at[pl.ds(512 * half, 512)], panels.at[pl.ds(512 * half, 512)], panel_sem.at[half]
        )
        copy.start()
        solves.append(copy)
        last = halves(dot3(halves(bottom), f11, NN))
        high[rows, 256:512], low[rows, 256:512] = last
        high[rows, 0:256], low[rows, 0:256] = halves(dot3(halves(left - dot3(last, f10, NN)), f00, NN))

    def put(slot, group, step):
        return pltpu.make_async_copy(
            ready.at[slot], out.at[pl.ds(pl.multiple_of(step * ROWS, ROWS), ROWS), group], out_sem.at[slot]
        )

    for group in range(2):
        rights[group].wait()
        for u in range(4):
            for h in range(2):
                span = slice(NB * h, NB * h + NB)
                right_high[u, span], right_low[u, span] = halves(right[8 * group + 2 * u + h])

        def body(step, carry, group=group):
            slot = step % 2
            base = pl.multiple_of(step * ROWS, ROWS)
            if group == 0:
                for i in range(4):

                    @pl.when(step == i)
                    def _(i=i):
                        blocks[i].wait()

            @pl.when(step + 4 * group >= 2)
            def _():
                put(slot, group, step).wait()

            g_high = jnp.concatenate([high[pl.ds(base, ROWS), :], high[1024:1040, :]], axis=0)
            g_low = jnp.concatenate([low[pl.ds(base, ROWS), :], low[1024:1040, :]], axis=0)
            for u in range(4):
                product = dot3((g_high, g_low), (right_high[u], right_low[u]), NN)
                for h in range(2):
                    q = 2 * u + h
                    lanes = slice(128 * h, 128 * h + 128)
                    ready[slot, :, q, :] = block[pl.ds(base, ROWS), group, q, :] - product[0:ROWS, lanes]
                    at = 8 * group + q
                    kept = sums[at : at + 1, :] - product[ROWS : ROWS + 1, lanes]
                    if (group, u) == (0, 0):
                        kept = jnp.where(col_index < 2, 0.0, kept)
                    checksum[at : at + 1, :] = kept
            @pl.when((step == 0) & (row_index < 2))
            def _():
                ready[slot] = jnp.zeros((ROWS, 8, 128), F32)

            if group == 0:

                @pl.when(col_index < 2)
                def _():
                    ready[slot, :, 0:2, :] = jnp.zeros((ROWS, 2, 128), F32)

            put(slot, group, step).start()
            return carry

        lax.fori_loop(0, 4, body, 0)
    for slot in range(2):
        put(slot, 1, 2 + slot).wait()
    for copy in solves:
        copy.wait()


def final_call(place, flat, across, mine, theirs, w00, l10, w11, sums):
    hbm = pl.BlockSpec(memory_space=pl.ANY)
    return pl.pallas_call(
        final_kernel,
        out_shape=(
            jax.ShapeDtypeStruct((1024, 2, 8, 128), F32),
            jax.ShapeDtypeStruct((1024, 512), F32),
            jax.ShapeDtypeStruct((16, 128), F32),
        ),
        in_specs=[SMEM, hbm, hbm] + [VMEM] * 6,
        out_specs=(hbm, hbm, VMEM),
        scratch_shapes=[
            pltpu.VMEM((1024, 2, 8, 128), F32),
            pltpu.VMEM((16, NB, NB), F32),
            pltpu.VMEM((1024, 512), F32),
            pltpu.VMEM((1040, 512), BF16),
            pltpu.VMEM((1040, 512), BF16),
            pltpu.VMEM((4, 512, NB), BF16),
            pltpu.VMEM((4, 512, NB), BF16),
            pltpu.VMEM((2, ROWS, 8, 128), F32),
            pltpu.VMEM((2, 3, NB, NB), BF16),
            pltpu.SemaphoreType.DMA((4,)),
            pltpu.SemaphoreType.DMA((2,)),
            pltpu.SemaphoreType.DMA((2,)),
            pltpu.SemaphoreType.DMA((2,)),
        ],
        name="panels_and_trailing",
        compiler_params=pltpu.CompilerParams(vmem_limit_bytes=30 * 1024 * 1024),
        cost_estimate=SMALL,
    )(place, flat, across, mine, theirs, w00, l10, w11, sums)


def where_is(device):
    row, col = divmod(device, 8)
    return [row // 4, row % 4, col // 2, col % 2]


def device_at(z, y, x, core):
    return ((z % 4) * 4 + y % 4) * 8 + (x % 4) * 2 + core


def moved(device, dim, by):
    at = where_is(device)
    at[dim] += by
    return device_at(*at)


def spread(value, trees, here, beside):
    holders = [[device_at(z, y, 0, c)] for (z, y), c, _ in trees]
    stages = []
    for at in range(3):
        aways = [(here[dims[at]] - (z, y, 0)[dims[at]]) % 4 for (z, y), _, dims in trees]
        away = jnp.where(here[3] == trees[0][1], aways[0], aways[1])
        for half in range(2):
            pairs = []
            for held, (_, _, dims) in zip(holders, trees):
                dim = dims[at]
                if half == 0:
                    pairs += [(h, moved(h, dim, 1)) for h in held]
                else:
                    pairs += [(h, moved(h, dim, -1)) for h in held] + [(moved(h, dim, 1), moved(h, dim, 2)) for h in held]
            if stages:
                value = beside(len(stages), value)
            arrived = lax.ppermute(value, ("row", "col"), pairs)
            value = jnp.where((away == 1) if half == 0 else (away >= 2), arrived, value)
            stages.append(value)
        holders = [[moved(h, dims[at], k) for h in held for k in range(4)] for held, (_, _, dims) in zip(holders, trees)]
    return stages


def after(value, token):
    return lax.optimization_barrier((value, token))[0]


def shards(covariance, check_weights):
    row = lax.axis_index("row")
    col = lax.axis_index("col")
    core = col % 2
    x = col // 2
    here = [row // 4, row % 4, x, core]
    flat = pltpu.with_memory_space_constraint(covariance.reshape(1024, 16, 128), pltpu.HBM)
    tiles = jnp.arange(4, dtype=jnp.int32) * 16 + row
    weights = jnp.where((tiles >= 2)[:, None], check_weights.reshape(4, NB), 0.0).reshape(1024)
    place = jnp.stack([row, col]).astype(jnp.int32)
    swap_cores = [(c, c ^ 1) for c in range(8)]

    pieces = corner_call(flat)
    fetched = lax.ppermute(pieces[0], ("row", "col"), [(8, 0), (9, 1)])
    corner = jnp.where(
        core == 0,
        jnp.concatenate([pieces[0], fetched[0:128]], axis=0),
        jnp.concatenate([fetched, pieces[9]], axis=0),
    )
    column, sums = column_call(weights, after(flat, corner))
    partial = [sums]
    from_left = lax.ppermute(column, "col", [(0, 2), (1, 3)])
    from_right = lax.ppermute(column, "col", [(0, 6), (1, 7)])

    def beside(stage, value):
        before = partial[-1]
        if stage <= 4:
            d = (1, 3, 4, 12)[stage - 1]
            partial.append(before + lax.ppermute(after(before, value), "row", [(r, r ^ d) for r in range(16)]))
        return after(value, (before, from_left, from_right) if stage == 5 else before)

    tree = spread(corner, [((0, 0), 0, (2, 0, 1)), ((0, 0), 1, (0, 2, 1))], here, beside)
    sums = partial[-1]
    near_sums = jnp.broadcast_to(sums[0:2].reshape(1, NB), (16, NB))
    far_sums = [lax.ppermute(near_sums, "col", [(0, 2 * k), (1, 2 * k + 1)]) for k in (1, 2, 3)]
    own, far_sums = lax.optimization_barrier((tree[-1], far_sums))
    other = lax.ppermute(own, "col", swap_cores)

    piece = pieces[8]
    for j in range(1, 8):
        piece = jnp.where(row // 2 == j, lax.ppermute(pieces[j] if j < 4 else after(pieces[j], fetched), "row", [(0, 2 * j), (1, 2 * j + 1)]), piece)
    across = lax.all_gather(after(piece, (tree[0], column)), "row", axis=0)
    across = pltpu.with_memory_space_constraint(across, pltpu.HBM)

    w00 = first_factor(place, own, other)
    panel_sums = near_sums
    for k in (1, 2, 3):
        panel_sums = jnp.where(x == k, far_sums[k - 1], panel_sums)

    l10, w11 = second_factor(place, w00, own, other)
    mine = jnp.where(x == 1, from_left, jnp.where(x == 3, from_right, column))
    mine = after(mine, tree[4])
    upper = lax.ppermute(mine[0:512], "col", [(2, 4), (3, 5)])
    lower = lax.ppermute(mine[512:1024], "col", [(6, 4), (7, 5)])
    upper, lower = after((upper, lower), w00)
    upper = jnp.where(x == 2, upper, mine[0:512])
    lower = jnp.where(x == 2, lower, mine[512:1024])
    mine = jnp.concatenate([upper, lower, panel_sums], axis=0)
    theirs = after(lax.ppermute(mine, "col", swap_cores), w11)

    grouped = pltpu.with_memory_space_constraint(covariance.reshape(1024, 2, 8, 128), pltpu.HBM)
    trailing, panels, checksum = final_call(place, grouped, across, mine, theirs, w00, l10, w11, sums)
    return (
        trailing.reshape(4, 1, NB, 8, 1, NB),
        panels.reshape(4, 1, NB, 512),
        checksum.reshape(8, 1, NB),
    )


def solution(mesh):
    in_specs = (P(None, "row", None, None, "col", None), P(None, "row", None))
    out_specs = (
        P(None, "row", None, None, "col", None),
        P(None, "row", None, None),
        P(None, "col", None),
    )
    return jax.shard_map(shards, mesh=mesh, in_specs=in_specs, out_specs=out_specs, check_vma=False)
```
